32 devices in a mesh: dp: 8 (over z, x), tensor: 4 (over y, core).
Axes of the slice: x: 2, y: 2, z: 4, core: 2. Of those that a mesh axis runs over, the one named last changes fastest.
Arguments:
- tokens: bfloat16 [16384, 768], P(('dp', 'tensor')), may hold values from -6 to 6
- segment_ids: int32 [16, 1024], P('dp'), may hold values from 0 to 63, never falling along the last dimension, each value on 1 to 512 neighbouring positions
- pad_mask: int32 [16, 1024], P('dp'), may hold values from 0 to 1, as said below
- buckets: int32 [2047], replicated, may hold values from 0 to 255
- projections: bfloat16 [768, 3, 768], P(None, None, 'tensor'), may hold values from -0.21875 to 0.21875
- projected_bias: float32 [2, 768], P(None, 'tensor'), may hold values from -3 to 3
- relative_table: float32 [256, 12], P(None, 'tensor'), may hold values from -6 to 6
- mixing_weight: bfloat16 [768, 768], P('tensor'), may hold values from -0.875 to 0.875
- residual_biases: float32 [2, 768], replicated, may hold values from -3 to 3
- norm_gains: float32 [2, 768], replicated, may hold values from 0.5 to 1.5
- norm_shifts: float32 [2, 768], replicated, may hold values from -3 to 3
- expand_weight: bfloat16 [768, 3072], P(None, 'tensor'), may hold values from -0.21875 to 0.21875
- expand_bias: float32 [3072], P('tensor'), may hold values from -3 to 3
- contract_weight: bfloat16 [3072, 768], P('tensor'), may hold values from -0.109375 to 0.109375
- cotangent: bfloat16 [16384, 768], P(('dp', 'tensor')), may hold values from -6 to 6
Outputs:
- layer_out: bfloat16 [16384, 768], P(('dp', 'tensor'))
- tokens_grad: float32 [16384, 768], P(('dp', 'tensor'))
- projections_grad: float32 [768, 3, 768], P(None, None, 'tensor')
- projected_grad: float32 [2, 768], P(None, 'tensor')
- relative_grad: float32 [256, 12], P(None, 'tensor')
- mixing_grad: float32 [768, 768], P('tensor')
- residual_grad: float32 [2, 768], replicated
- gains_grad: float32 [2, 768], replicated
- shifts_grad: float32 [2, 768], replicated
- expand_grad: float32 [768, 3072], P(None, 'tensor')
- bias_grad: float32 [3072], P('tensor')
- contract_grad: float32 [3072, 768], P('tensor')
The draws below stay inside these ranges and needn't reach their ends.
Inputs may be any that keep to these rules, and one draw needn't show every extreme that they name: `segment_ids`: along each sequence the segment numbers never fall, and a document has at most 512 tokens. `pad_mask`: in each sequence the entries equal to 1 come first.
All inputs are finite; a program needn't handle non-finite values.
Results may differ from the reference program's by a relative error of at most 0.013.
Values may be sent and summed in bfloat16 or wider, within the bound.
No kernel may reach another device: no remote copies, remote signals or barrier semaphores. Data moves between devices by JAX's collectives and lax.ppermute only.
A program may use at most 192 MiB of HBM per device.

```python
import math
import jax
import jax.numpy as jnp
import numpy as np
from jax import lax

D = 768
H = 12
HEAD = 64
FF = 3072
NB = 256
LEN = 1024
QB = 512
SEQS = 16
TOKENS = 16384


def draw_pad_mask(key, part):
    counts = jax.random.randint(key, (SEQS, 1), 0, LEN // 4 + 1)
    places = jnp.arange(LEN, dtype=jnp.int32)[None, :]
    return (places < LEN - counts).astype(jnp.int32)


def touch_ends(entries, own_key, low, high):
    longest = entries.shape.index(max(entries.shape))
    spots = []
    for shift in (0, 1):
        where = [jax.random.randint(jax.random.fold_in(own_key, axis), (), 0, length) for axis, length in enumerate(entries.shape)]
        where[longest] = (where[longest] + shift) % entries.shape[longest]
        spots.append(tuple(where))
    return entries.at[spots[0]].set(low).at[spots[1]].set(high)


def levels(key, extent, shards, low, top_value):
    level, own = 1.0, jax.random.fold_in(key, 6)
    for dim, shards_of in shards:
        steps = jnp.exp(jax.random.uniform(jax.random.fold_in(own, dim), (shards_of,), jnp.float32, low / len(shards), top_value / len(shards)))
        level = level * jnp.repeat(steps, extent[dim] // shards_of).reshape([-1 if axis == dim else 1 for axis in range(len(extent))])
    return level


def length_profile(number_of, total, bound, lean):
    weights = [(1 << 20) // math.isqrt(rank ** lean) + 1 for rank in range(2, number_of + 1)]
    spare, given = total - bound - (number_of - 1), [1] * (number_of - 1)
    while spare > 0:
        movable = [i for i in range(number_of - 1) if given[i] < bound]
        pool, remaining = sum([weights[i] for i in movable]), spare
        for i in movable:
            extra = min(bound - given[i], max(1, remaining * weights[i] // pool), spare)
            given[i] = given[i] + extra
            spare = spare - extra
    return np.array([bound] + given)


def uneven(rng, amount, total, limit, lean):
    if amount == 2:
        one = jax.random.randint(rng, (), max(1, total - limit), min(limit, total - 1) + 1)
        return jnp.stack([one, total - one])
    tallies = jnp.asarray(length_profile(amount, total, limit, lean), jnp.int32)
    twos = (amount - 1) // 2
    source_of, receiver = tallies[1:1 + 2 * twos:2], tallies[2:2 + 2 * twos:2]
    slack = jnp.minimum(source_of - 1, limit - receiver)
    moved = jax.random.randint(jax.random.fold_in(rng, 1), (twos,), 0, 1 << 20) % (slack + 1)
    tallies = tallies.at[1:1 + 2 * twos:2].set(source_of - moved).at[2:2 + 2 * twos:2].set(receiver + moved)
    return tallies[jax.random.permutation(jax.random.fold_in(rng, 2), amount)]


def centred(key, shape, deviation, bound, cuts=(), kind=jnp.bfloat16):
    drawn = jax.random.normal(key, shape, jnp.float32) * deviation
    if len(cuts) > 0:
        drawn = levels(key, shape, cuts, -0.22, 0.18) * drawn
    return jnp.clip(drawn, min=-bound, max=bound).astype(kind)


def setup_inputs(seed: int = 0) -> dict:
    arg_keys = jax.random.split(jax.random.key(seed), 16)
    tokens = centred(arg_keys[0], (TOKENS, D), 1.0, 6.0, ((0, 32),))
    segment_ids = jax.vmap(lambda own: jnp.searchsorted(jnp.cumsum(uneven(own, max(4, LEN // 16), LEN, LEN // 2, 2)), jnp.arange(LEN), side="right"))(jax.random.split(arg_keys[1], SEQS)).reshape((SEQS, LEN)).astype(jnp.int32)
    pad_mask = draw_pad_mask(jax.random.fold_in(arg_keys[15], 71), 0)
    buckets = touch_ends(jax.random.randint(arg_keys[3], (2 * LEN - 1,), 0, NB), jax.random.fold_in(arg_keys[3], 1), 0, NB - 1).astype(jnp.int32)
    projections = centred(arg_keys[4], (D, 3, H * HEAD), D ** -0.5, 0.21875, ((2, 4),))
    projected_bias = centred(arg_keys[5], (2, H * HEAD), 0.5, 3.0, ((1, 4),), jnp.float32)
    relative_table = centred(arg_keys[6], (NB, H), 1.0, 6.0, ((1, 4),), jnp.float32)
    mixing_weight = centred(arg_keys[7], (H * HEAD, D), (D // 16) ** -0.5, 0.875, ((0, 4),))
    residual_biases = centred(arg_keys[8], (2, D), 0.5, 3.0, (), jnp.float32)
    norm_gains = jnp.clip(1.0 + 0.1 * jax.random.normal(arg_keys[9], (2, D), jnp.float32), 0.5, 1.5)
    norm_shifts = centred(arg_keys[10], (2, D), 0.5, 3.0, (), jnp.float32)
    expand_weight = centred(arg_keys[11], (D, FF), D ** -0.5, 0.21875, ((1, 4),))
    expand_bias = centred(arg_keys[12], (FF,), 0.5, 3.0, ((0, 4),), jnp.float32)
    contract_weight = centred(arg_keys[13], (FF, D), FF ** -0.5, 0.109375, ((0, 4),))
    cotangent = centred(arg_keys[14], (TOKENS, D), 1.0, 6.0, ((0, 32),))
    return {"tokens": tokens, "segment_ids": segment_ids, "pad_mask": pad_mask, "buckets": buckets, "projections": projections, "projected_bias": projected_bias, "relative_table": relative_table, "mixing_weight": mixing_weight, "residual_biases": residual_biases, "norm_gains": norm_gains, "norm_shifts": norm_shifts, "expand_weight": expand_weight, "expand_bias": expand_bias, "contract_weight": contract_weight, "cotangent": cotangent}


norm_eps = 1e-05
big_negative = -1e+30

@jax.custom_vjp
def low(v):
    return lax.optimization_barrier(v.astype(jnp.bfloat16)).astype(jnp.float32)

@jax.custom_vjp
def low_back(v):
    return v

def low_keep(v):
    return (low(v), None)

def low_pass(kept, grad):
    return (grad,)

def back_keep(v):
    return (v, None)

def back_low(kept, grad):
    return (low(grad),)
low.defvjp(low_keep, low_pass)
low_back.defvjp(back_keep, back_low)

def matmul(left_side, right_side):
    return jnp.dot(left_side, right_side, precision=lax.Precision.HIGHEST, preferred_element_type=jnp.float32)

def layer_norm(inputs, gain_row, shift_row):
    average = lax.optimization_barrier(jnp.mean(inputs, axis=-1, keepdims=True))
    centered = inputs - average
    variance = lax.optimization_barrier(jnp.mean(centered * centered, axis=-1, keepdims=True))
    return centered * lax.rsqrt(variance + norm_eps) * gain_row + shift_row

def group_forward(params, bucket_hot, inputs, segments, padding):
    projections, projected_bias, relative_table, mixing_weight, residual_biases, norm_gains, norm_shifts, expand_weight, expand_bias, contract_weight = params
    seq_group = segments.shape[0]
    width_all = H * HEAD
    scale_factor = HEAD ** (-0.5)
    queries = low(low_back(matmul(inputs, projections[:, 0, :]) + projected_bias[0]))
    key_rows = low(low_back(matmul(inputs, projections[:, 1, :])))
    values_all = low(low_back(matmul(inputs, projections[:, 2, :]) + projected_bias[1]))
    offset_bias = matmul(bucket_hot, relative_table)
    blocks = LEN // QB

    def one_block(block_index):
        sequence = block_index // blocks
        begin_row = block_index % blocks * QB
        block_q = lax.dynamic_slice_in_dim(queries, sequence * LEN + begin_row, QB, 0).reshape(QB, H, HEAD)
        block_k = lax.dynamic_slice_in_dim(key_rows, sequence * LEN, LEN, 0).reshape(LEN, H, HEAD)
        block_v = lax.dynamic_slice_in_dim(values_all, sequence * LEN, LEN, 0).reshape(LEN, H, HEAD)
        raw_scores = jnp.einsum('qhd,khd->hqk', block_q, block_k, precision=lax.Precision.HIGHEST) * scale_factor
        query_place = begin_row + jnp.arange(QB, dtype=jnp.int32)
        key_place = jnp.arange(LEN, dtype=jnp.int32)
        relative = offset_bias[key_place[None, :] - query_place[:, None] + (LEN - 1)]
        scores = low_back(raw_scores) + jnp.transpose(relative, (2, 0, 1))
        segment_row = lax.dynamic_index_in_dim(segments, sequence, 0, keepdims=False)
        padding_row = lax.dynamic_index_in_dim(padding, sequence, 0, keepdims=False)
        segment_query = lax.dynamic_slice_in_dim(segment_row, begin_row, QB, 0)
        allowed = (segment_query[:, None] == segment_row[None, :]) & ((padding_row[None, :] == 1) | (query_place[:, None] == key_place[None, :]))
        scores = jnp.where(allowed[None], scores, big_negative)
        largest = lax.optimization_barrier(jnp.max(scores, axis=-1, keepdims=True))
        exponent = jnp.exp(scores - largest)
        probability = exponent / lax.optimization_barrier(jnp.sum(exponent, axis=-1, keepdims=True))
        mixed_rows = jnp.einsum('hqk,khd->qhd', low(probability), block_v, precision=lax.Precision.HIGHEST)
        return mixed_rows.reshape(QB, width_all)
    attended = lax.map(jax.checkpoint(one_block), jnp.arange(seq_group * blocks, dtype=jnp.int32))
    attended = low(low_back(attended.reshape(seq_group * LEN, width_all)))
    branch = low_back(matmul(attended, mixing_weight))
    normed = layer_norm(inputs + branch + residual_biases[0], norm_gains[0], norm_shifts[0])
    expanded = low_back(matmul(low(normed), expand_weight) + expand_bias)
    hidden = low(jax.nn.gelu(expanded, approximate=False))
    contracted = low_back(matmul(hidden, contract_weight))
    return layer_norm(normed + contracted + residual_biases[1], norm_gains[1], norm_shifts[1])

def reference(tokens, segment_ids, pad_mask, buckets, projections, projected_bias, relative_table, mixing_weight, residual_biases, norm_gains, norm_shifts, expand_weight, expand_bias, contract_weight, cotangent):
    groups = math.gcd(SEQS, max(1, 4096 // LEN))
    group_steps = SEQS // groups
    bucket_hot = (buckets[:, None] == jnp.arange(NB, dtype=jnp.int32)[None, :]).astype(jnp.float32)
    params = tuple((member.astype(jnp.float32) for member in (projections, projected_bias, relative_table, mixing_weight, residual_biases, norm_gains, norm_shifts, expand_weight, expand_bias, contract_weight)))
    inputs = tokens.astype(jnp.float32).reshape(group_steps, groups * LEN, D)
    segment_groups = segment_ids.reshape(group_steps, groups, LEN)
    padding_groups = pad_mask.reshape(group_steps, groups, LEN)

    def forward(weights, inputs_all):

        def one_group(carried, pieces):
            return (carried, group_forward(weights, bucket_hot, pieces[0], pieces[1], pieces[2]))
        _, outputs_all = lax.scan(jax.checkpoint(one_group), jnp.zeros((), jnp.float32), (inputs_all, segment_groups, padding_groups))
        return outputs_all
    outputs, pullback = jax.vjp(forward, params, inputs)
    gradients = pullback(cotangent.astype(jnp.float32).reshape(outputs.shape))
    weight_grads = gradients[0]
    return (outputs.reshape(TOKENS, D).astype(jnp.bfloat16), gradients[1].reshape(TOKENS, D), weight_grads[0], weight_grads[1], weight_grads[2], weight_grads[3], weight_grads[4], weight_grads[5], weight_grads[6], weight_grads[7], weight_grads[8], weight_grads[9])
```

```python
import functools
import jax
import jax.numpy as jnp
from jax import lax
from jax.experimental import pallas as pl
from jax.experimental.pallas import tpu as pltpu
from jax.sharding import PartitionSpec as P

norm_eps = 1e-05
big_negative = -1e30
KB = 128
QT = 256
HALF = 512
SEQ = 1024
HW = 64
NH = 3
TILES = 11
SPAN = 1536
f32 = jnp.float32
bf16 = jnp.bfloat16
dot32 = functools.partial(lax.dot_general, preferred_element_type=f32)
NN = (((1,), (0,)), ((), ()))
NT = (((1,), (1,)), ((), ()))


def three_parts(value):
    high = value.astype(bf16)
    rest = value - high.astype(f32)
    middle = rest.astype(bf16)
    low = (rest - middle.astype(f32)).astype(bf16)
    return high, middle, low


def bucket_grid(bucket_ref, count):
    rows = lax.broadcasted_iota(jnp.int32, (count, SPAN), 0)
    return (rows == bucket_ref[...]).astype(bf16)


def tile_mask(key_code, seg_row, difference, shift):
    codes = jnp.concatenate([key_code, key_code], axis=1)
    return (codes == seg_row) | (difference == shift)


def forward_kernel(limits, x_own, x_other, weight, bias_row, table, buckets, key_code, seg_row,
                   own_out, other_out, out_full, totals, heads_out, turned_out, tiles,
                   best, total, gathered):
    flip = limits[8]
    for half, x_ref in enumerate((x_own, x_other)):
        full = dot32(x_ref[...], weight[...], NN) + bias_row[...]
        low = full.astype(bf16)
        scaled = low[:, : NH * HW] * 0.125
        rows = pl.ds(half * HALF, HALF)
        for g in range(3 * NH):
            piece = scaled[:, g * HW : (g + 1) * HW] if g < NH else low[:, g * HW : (g + 1) * HW]
            heads_out[g, rows, :] = piece
        whole = low.astype(f32)
        for g in range(3 * NH):
            piece = whole[:, g * HW : (g + 1) * HW]
            if g < NH:
                piece = piece * 0.125
            turned = piece.T.astype(bf16)
            for c in range(HALF // KB):
                turned_out[half * (HALF // KB) + c, g * HW : (g + 1) * HW, :] = turned[
                    :, c * KB : (c + 1) * KB
                ]
    hot = bucket_grid(buckets, table.shape[1])
    line = sum(dot32(part, hot, NN) for part in three_parts(table[...]))
    for h in range(NH):
        for u in range(TILES):
            start = 640 - 128 * (u - 5)
            spread = jnp.broadcast_to(line[h : h + 1, start : start + 256], (KB, 256))
            tiles[h, u] = pltpu.roll(spread, 129, 1, stride=1, stride_axis=0)[:, :KB]
    difference = lax.broadcasted_iota(jnp.int32, (KB, QT), 1) - lax.broadcasted_iota(
        jnp.int32, (KB, QT), 0
    )

    def query_step(block, carry):
        place = block ^ (flip * 2)
        best[...] = jnp.full(best.shape, big_negative, f32)
        total[...] = jnp.zeros(total.shape, f32)
        gathered[...] = jnp.zeros(gathered.shape, f32)
        segs = seg_row[place]

        def key_step(key_place, carry):
            key_block = key_place ^ (flip * 4)
            gap = key_place - 2 * place
            allowed = tile_mask(key_code[key_place], segs, difference, gap * KB)
            for h in range(NH):
                keys = heads_out[NH + h, pl.ds(key_block * KB, KB), :]
                turned_q = jnp.concatenate(
                    [turned_out[2 * block, h * HW : (h + 1) * HW, :],
                     turned_out[2 * block + 1, h * HW : (h + 1) * HW, :]], axis=1)
                scores = dot32(keys, turned_q, NN)
                scores = scores + jnp.concatenate(
                    [tiles[h, gap + 5], tiles[h, gap + 4]], axis=1
                )
                scores = jnp.where(allowed, scores, big_negative)
                old = best[h]
                new = jnp.maximum(old, jnp.max(scores, axis=0, keepdims=True))
                weightings = jnp.exp(scores - new)
                shrink = jnp.exp(old - new)
                best[h] = new
                total[h] = shrink * total[h] + jnp.sum(weightings, axis=0, keepdims=True)
                turned_v = turned_out[key_block, (2 * NH + h) * HW : (2 * NH + h + 1) * HW, :]
                gathered[h] = gathered[h] * shrink + dot32(turned_v, weightings.astype(bf16), NN)
            return carry

        lax.fori_loop(limits[place], limits[4 + place], key_step, 0)
        for h in range(NH):
            result = gathered[h] / total[h]
            out_full[block, h * HW : (h + 1) * HW, :] = result
            totals[block, h : h + 1, :] = best[h] + jnp.log(total[h])
        return carry

    lax.fori_loop(0, SEQ // QT, query_step, 0)
    for c in range(2):
        own_out[:, c * QT : (c + 1) * QT] = out_full[c].astype(bf16)
        other_out[:, c * QT : (c + 1) * QT] = out_full[2 + c].astype(bf16)


def attend(limits, x_own, x_other, weight, bias_row, table, buckets, key_code, seg_row):
    vm = pl.BlockSpec(memory_space=pltpu.VMEM)
    return pl.pallas_call(
        forward_kernel,
        out_shape=(
            jax.ShapeDtypeStruct((NH * HW, HALF), bf16),
            jax.ShapeDtypeStruct((NH * HW, HALF), bf16),
            jax.ShapeDtypeStruct((SEQ // QT, NH * HW, QT), f32),
            jax.ShapeDtypeStruct((SEQ // QT, 8, QT), f32),
            jax.ShapeDtypeStruct((3 * NH, SEQ, HW), bf16),
            jax.ShapeDtypeStruct((SEQ // KB, 3 * NH * HW, KB), bf16),
            jax.ShapeDtypeStruct((NH, TILES, KB, KB), f32),
        ),
        in_specs=[pl.BlockSpec(memory_space=pltpu.SMEM)] + [vm] * 8,
        out_specs=tuple([vm] * 7),
        scratch_shapes=[
            pltpu.VMEM((NH, 1, QT), f32),
            pltpu.VMEM((NH, 1, QT), f32),
            pltpu.VMEM((NH, HW, QT), f32),
        ],
        compiler_params=pltpu.CompilerParams(vmem_limit_bytes=48 << 20),
        name="attend",
    )(limits, x_own, x_other, weight, bias_row, table, buckets, key_code, seg_row)


def backward_kernel(limits, grad_own, grad_other, out_full, totals, heads, turned, tiles, buckets,
                    key_code, seg_row,
                    grads_out, sums_out, table_out,
                    turned_grad, plain_grad, row_dots, query_acc, query_all, key_acc, value_acc, tile_acc):
    flip = limits[8]
    for half, ref in enumerate((grad_own, grad_other)):
        for c in range(2):
            block = 2 * half + c
            piece = ref[:, c * QT : (c + 1) * QT]
            turned_grad[block] = piece
            wide = piece.astype(f32)
            product = wide * out_full[block]
            for h in range(NH):
                rows = slice(h * HW, (h + 1) * HW)
                row_dots[block, h : h + 1, :] = jnp.sum(product[rows], axis=0, keepdims=True)
                plain_grad[h, block * QT : (block + 1) * QT, :] = wide[rows].T.astype(bf16)
    key_acc[...] = jnp.zeros(key_acc.shape, f32)
    value_acc[...] = jnp.zeros(value_acc.shape, f32)
    tile_acc[...] = jnp.zeros(tile_acc.shape, f32)
    difference = lax.broadcasted_iota(jnp.int32, (KB, QT), 1) - lax.broadcasted_iota(
        jnp.int32, (KB, QT), 0
    )

    def query_step(block, carry):
        place = block ^ (flip * 2)
        query_acc[...] = jnp.zeros(query_acc.shape, f32)
        segs = seg_row[place]
        q_rows = pl.ds(block * QT, QT)

        def key_step(key_place, carry):
            key_block = key_place ^ (flip * 4)
            gap = key_place - 2 * place
            k_rows = pl.ds(key_block * KB, KB)
            allowed = tile_mask(key_code[key_place], segs, difference, gap * KB)
            for h in range(NH):
                keys = heads[NH + h, k_rows, :]
                turned_q = jnp.concatenate(
                    [turned[2 * block, h * HW : (h + 1) * HW, :],
                     turned[2 * block + 1, h * HW : (h + 1) * HW, :]], axis=1)
                scores = dot32(keys, turned_q, NN)
                scores = scores + jnp.concatenate(
                    [tiles[h, gap + 5], tiles[h, gap + 4]], axis=1
                )
                scores = jnp.where(allowed, scores, big_negative)
                chances = jnp.exp(scores - totals[block, h : h + 1, :])
                values = heads[2 * NH + h, k_rows, :]
                chance_grad = dot32(values, turned_grad[block, h * HW : (h + 1) * HW, :], NN)
                score_grad = chances * (chance_grad - row_dots[block, h : h + 1, :])
                tile_acc[h, gap + 5] += score_grad[:, :KB]
                tile_acc[h, gap + 4] += score_grad[:, KB:]
                score_low = score_grad.astype(bf16)
                value_acc[h, k_rows, :] += dot32(chances.astype(bf16), plain_grad[h, q_rows, :], NN)
                key_acc[h, k_rows, :] += dot32(score_low, heads[h, q_rows, :], NN)
                turned_k = turned[key_block, (NH + h) * HW : (NH + h + 1) * HW, :]
                query_acc[h] += dot32(turned_k, score_low, NN)
            return carry

        lax.fori_loop(limits[place], limits[4 + place], key_step, 0)
        for h in range(NH):
            query_all[h, q_rows, :] = (query_acc[h] * 0.125).T
        return carry

    lax.fori_loop(0, SEQ // QT, query_step, 0)
    sums = []
    for g, acc in ((0, query_all), (1, key_acc), (2, value_acc)):
        for h in range(NH):
            low = acc[h].astype(bf16)
            at = (g * NH + h) * HW
            grads_out[:, at : at + HW] = low
            sums_out[0:1, at : at + HW] = jnp.sum(low.astype(f32), axis=0, keepdims=True)
    hot = bucket_grid(buckets, table_out.shape[1])
    lines = []
    for h in range(NH):
        spans = [jnp.zeros((1, KB), f32) for _ in range(SPAN // KB)]
        for u in range(TILES):
            wide = jnp.concatenate([tile_acc[h, u], jnp.zeros((KB, KB), f32)], axis=1)
            count = KB // 2
            while count:
                wide = wide[count:] + pltpu.roll(wide[:count], count, 1)
                count //= 2
            sums = wide
            at = (640 - 128 * (u - 5)) // KB
            spans[at] = spans[at] + sums[:, :KB]
            spans[at + 1] = spans[at + 1] + sums[:, KB:]
        lines.append(jnp.concatenate(spans, axis=1))
    lines.append(jnp.zeros((8 - NH, SPAN), f32))
    line = jnp.concatenate(lines, axis=0)
    table_out[...] = sum(dot32(part, hot, NT) for part in three_parts(line))


def attend_back(limits, grad_own, grad_other, out_full, totals, heads, turned, tiles, buckets,
                key_code, seg_row, bucket_count):
    vm = pl.BlockSpec(memory_space=pltpu.VMEM)
    return pl.pallas_call(
        backward_kernel,
        out_shape=(
            jax.ShapeDtypeStruct((SEQ, 3 * NH * HW), bf16),
            jax.ShapeDtypeStruct((8, 3 * NH * HW), f32),
            jax.ShapeDtypeStruct((8, bucket_count), f32),
        ),
        in_specs=[pl.BlockSpec(memory_space=pltpu.SMEM)] + [vm] * 10,
        out_specs=tuple([vm] * 3),
        scratch_shapes=[
            pltpu.VMEM((SEQ // QT, NH * HW, QT), bf16),
            pltpu.VMEM((NH, SEQ, HW), bf16),
            pltpu.VMEM((SEQ // QT, 8, QT), f32),
            pltpu.VMEM((NH, HW, QT), f32),
            pltpu.VMEM((NH, SEQ, HW), f32),
            pltpu.VMEM((NH, SEQ, HW), f32),
            pltpu.VMEM((NH, SEQ, HW), f32),
            pltpu.VMEM((NH, TILES, KB, KB), f32),
        ],
        compiler_params=pltpu.CompilerParams(vmem_limit_bytes=56 << 20),
        name="attend_back",
    )(limits, grad_own, grad_other, out_full, totals, heads, turned, tiles, buckets, key_code, seg_row)


def sequence_tables(segments, padding, flip):
    seq = segments.shape[0]
    firsts = segments[0::QT]
    lasts = segments[QT - 1 :: QT]
    low = jnp.sum((segments[None, :] < firsts[:, None]).astype(jnp.int32), axis=1) // KB
    high = (jnp.sum((segments[None, :] <= lasts[:, None]).astype(jnp.int32), axis=1) + KB - 1) // KB
    limits = jnp.concatenate([low, high, flip[None]]).astype(jnp.int32)
    code = jnp.where(padding == 1, segments, -1)
    key_code = jnp.broadcast_to(code.reshape(seq // KB, KB, 1), (seq // KB, KB, KB))
    seg_row = segments.reshape(seq // QT, 1, QT)
    return limits, key_code, seg_row


def layer_norm(inputs, gain_row, shift_row):
    average = jnp.mean(inputs, axis=-1, keepdims=True)
    centered = inputs - average
    inverse = lax.rsqrt(jnp.mean(centered * centered, axis=-1, keepdims=True) + norm_eps)
    normed = centered * inverse
    return (normed * gain_row + shift_row, normed, inverse)


def norm_back(incoming, normed, inverse, gain_row):
    scaled = incoming * gain_row
    first_mean = jnp.mean(scaled, axis=-1, keepdims=True)
    second_mean = jnp.mean(scaled * normed, axis=-1, keepdims=True)
    return inverse * (scaled - first_mean - normed * second_mean)


def assemble_kernel(place, mine, theirs, out):
    low = place[0] & 1
    high = place[0] >> 1
    for r in range(mine.shape[0]):
        at = (r ^ high) * 2
        out[at + low] = mine[r].astype(f32)
        out[at + 1 - low] = theirs[r].astype(f32)


def assemble(place, mine, theirs):
    half, rows, cols = mine.shape
    vm = pl.BlockSpec(memory_space=pltpu.VMEM)
    return pl.pallas_call(
        assemble_kernel,
        out_shape=jax.ShapeDtypeStruct((2 * half, rows, cols), f32),
        in_specs=[pl.BlockSpec(memory_space=pltpu.SMEM), vm, vm],
        out_specs=vm,
        compiler_params=pltpu.CompilerParams(vmem_limit_bytes=32 << 20),
        name="assemble",
    )(place, mine, theirs)


def digits_of(count):
    radices = [2]
    count //= 2
    while count > 1:
        radices.append(4 if count % 4 == 0 else count)
        count //= radices[-1]
    return radices


def make_body(dp_count):
    radices = digits_of(dp_count)

    def swap(value, axis, count, bits):
        return lax.ppermute(value, axis, [(i, i ^ bits) for i in range(count)])

    swap_core = lambda value: swap(value, "tensor", 4, 1)
    swap_y = lambda value: swap(value, "tensor", 4, 2)
    swap_dp = lambda value, bits: swap(value, "dp", dp_count, bits)

    def sum_doubling(value):
        bits = 1
        while bits < dp_count:
            value = value + swap_dp(value, bits)
            bits *= 2
        return value

    def sum_over_dp(grad):
        place = lax.axis_index("dp")
        rows, cols = grad.shape
        piece = rows // dp_count
        current = grad.reshape(dp_count, piece, cols)
        left = dp_count
        step = 1
        for radix in radices:
            left //= radix
            current = current.reshape(left, radix, piece, cols)
            digit = place // step % radix

            def part(r):
                return lax.dynamic_index_in_dim(current, digit ^ r, 1, keepdims=False)

            sent = [swap_dp(part(r).astype(bf16), r * step) for r in range(1, radix)]
            total = part(0).astype(f32)
            for piece_in in sent:
                total = total + piece_in.astype(f32)
            current = total.astype(bf16)
            step *= radix
        mine = current.reshape(piece, cols)[None]
        for radix in radices[:0:-1]:
            step //= radix
            others = [mine] + [swap_dp(mine, r * step) for r in range(1, radix)]
            mine = jnp.stack(others, axis=1).reshape(mine.shape[0] * radix, piece, cols)
        theirs = swap_dp(mine, 1)
        return assemble(place.astype(jnp.int32)[None], mine, theirs).reshape(rows, cols)

    def body(
        tokens,
        segment_ids,
        pad_mask,
        buckets,
        projections,
        projected_bias,
        relative_table,
        mixing_weight,
        residual_biases,
        norm_gains,
        norm_shifts,
        expand_weight,
        expand_bias,
        contract_weight,
        cotangent,
    ):
        rows_here, model_width = tokens.shape
        bucket_count = relative_table.shape[0]
        width = projections.shape[2]
        units = expand_weight.shape[1]
        spot = lax.axis_index("tensor")
        flip = spot % 2

        weight_own = projections.reshape(model_width, 3 * width)
        weight_y = swap_y(weight_own)
        x_other = swap_core(tokens)
        small_own = jnp.concatenate(
            [relative_table.T.reshape(-1), projected_bias.reshape(-1), expand_bias]
        )
        small_y = swap_y(small_own)
        bias_slots = [expand_bias, None, small_y[-units:], None]
        pair = swap_core(jnp.concatenate([expand_bias, small_y[-units:]]))
        bias_slots[1], bias_slots[3] = pair[:units], pair[units:]

        def unpack(small):
            table = small[: NH * bucket_count].reshape(NH, bucket_count)
            rows = small[NH * bucket_count : NH * bucket_count + 2 * width]
            bias_row = jnp.concatenate([rows[:width], jnp.zeros((width,), f32), rows[width:]])
            return jnp.pad(table, ((0, 8 - NH), (0, 0))), bias_row[None]

        def four(weight, after):
            weight, _ = lax.optimization_barrier((weight, after))
            across = swap_y(weight)
            return [weight, swap_core(weight), across, swap_core(across)]

        mixing = four(mixing_weight, tokens)
        expand = four(expand_weight, weight_y)
        contract = four(contract_weight, expand[2])

        chip = spot // 2
        segments = lax.dynamic_index_in_dim(segment_ids, chip, 0, keepdims=False)
        padding = lax.dynamic_index_in_dim(pad_mask, chip, 0, keepdims=False)
        limits, key_code, seg_row = sequence_tables(segments, padding, flip)
        bucket_row = buckets[255:1791][::-1][None]
        table_own, row_own = unpack(small_own)
        table_y, row_y = unpack(small_y)

        def forward(weight, row, table):
            return attend(
                limits, tokens, x_other, weight, row, table, bucket_row, key_code, seg_row
            )

        own_a, other_a, *saved_a = forward(weight_own, row_own, table_own)
        own_b, other_b, *saved_b = forward(weight_y, row_y, table_y)
        attended = jnp.concatenate([own_a, swap_core(other_a), own_b, swap_core(other_b)], axis=0)
        mixing_all = jnp.concatenate(mixing, axis=0)
        branch = lax.dot_general(
            attended, mixing_all, (((0,), (0,)), ((), ())), preferred_element_type=f32
        )
        first_sum = tokens.astype(f32) + branch + residual_biases[0]
        normed_out, normed_one, inverse_one = layer_norm(first_sum, norm_gains[0], norm_shifts[0])
        expand_input = normed_out.astype(bf16)
        expanded = [dot32(expand_input, expand[s], NN) + bias_slots[s] for s in range(4)]
        hidden = [jax.nn.gelu(value, approximate=False).astype(bf16) for value in expanded]
        contracted = sum(dot32(hidden[s], contract[s], NN) for s in range(4))
        second_sum = normed_out + contracted + residual_biases[1]
        final_norm, normed_two, inverse_two = layer_norm(second_sum, norm_gains[1], norm_shifts[1])
        layer_out = final_norm.astype(bf16)

        outer_grad = cotangent.astype(f32)
        grad_two = norm_back(outer_grad, normed_two, inverse_two, norm_gains[1])
        upstream = grad_two.astype(bf16)

        def gelu_slope(value):
            cumulative = 0.5 * (1.0 + lax.erf(value * 0.7071067811865476))
            density = jnp.exp(-0.5 * value * value) * 0.3989422804014327
            return cumulative + value * density

        unit_grad = [
            (dot32(upstream, contract[s], NT) * gelu_slope(expanded[s])).astype(bf16)
            for s in range(4)
        ]
        TN = (((0,), (0,)), ((), ()))

        def over_tensor(make):
            from_one, from_three = make(1).astype(bf16), make(3).astype(bf16)
            in_three = swap_core(from_three)
            in_one = swap_core(from_one)
            across = swap_y((make(2) + in_three.astype(f32)).astype(bf16))
            return make(0) + in_one.astype(f32) + across.astype(f32)

        contract_grad = over_tensor(lambda s: dot32(hidden[s], upstream, TN))
        expand_grad = over_tensor(lambda s: dot32(expand_input, unit_grad[s], TN))
        normed_grad = grad_two + sum(dot32(unit_grad[s], expand[s], NT) for s in range(4))
        grad_one = norm_back(normed_grad, normed_one, inverse_one, norm_gains[0])
        outgoing = grad_one.astype(bf16)
        attended_grad = dot32(mixing_all, outgoing, NT).astype(bf16)
        slots = [attended_grad[s * width : (s + 1) * width] for s in range(4)]
        mixing_grad = over_tensor(
            lambda s: dot32(attended[s * width : (s + 1) * width], outgoing, NN)
        )

        column = lambda value: jnp.sum(value, axis=0)[None]
        wide_sums = jnp.concatenate(
            [
                column(grad_one),
                column(grad_two),
                column(normed_grad * normed_one),
                column(outer_grad * normed_two),
                column(normed_grad),
                column(outer_grad),
            ]
        )
        bias_sums = [column(unit_grad[s].astype(f32)) for s in range(4)]
        arrived = swap_core(jnp.concatenate([wide_sums, bias_sums[1], bias_sums[3]]))
        wide_sums = wide_sums + arrived[:6]
        first_bias, second_bias = bias_sums[0] + arrived[6:7], bias_sums[2] + arrived[7:8]
        arrived = swap_y(jnp.concatenate([wide_sums, second_bias]))
        sums = sum_doubling(jnp.concatenate([wide_sums, first_bias]) + arrived)

        contract_total = sum_over_dp(contract_grad)
        expand_total = sum_over_dp(expand_grad)
        mixing_total = sum_over_dp(mixing_grad)

        x_both = jnp.concatenate([tokens, x_other], axis=0)

        def backward(saved, grad_own, grad_other, weight):
            grads, column_sums, table_sums = attend_back(
                limits, grad_own, grad_other, *saved, bucket_row, key_code, seg_row, bucket_count
            )
            weight_grad = dot32(x_both, grads, TN)
            tail = jnp.concatenate(
                [
                    table_sums[:NH].reshape(-1),
                    column_sums[0, :width],
                    column_sums[0, 2 * width :],
                ]
            )
            return weight_grad, dot32(grads, weight, NT), tail

        weight_grad_b, input_b, tail_b = backward(saved_b, slots[2], swap_core(slots[3]), weight_y)
        sent_grad = swap_y(weight_grad_b.astype(bf16))
        sent_tail = swap_y(tail_b)
        weight_grad_a, input_a, tail_a = backward(
            saved_a, slots[0], swap_core(slots[1]), weight_own
        )
        projection_total = sum_over_dp(weight_grad_a + sent_grad.astype(f32))
        tail = sum_doubling(tail_a + sent_tail)
        inputs = input_a + input_b
        input_there = swap_core(inputs[rows_here:].astype(bf16))
        tokens_grad = inputs[:rows_here] + input_there.astype(f32) + grad_one

        edge = NH * bucket_count
        return (
            layer_out,
            tokens_grad,
            projection_total.reshape(model_width, 3, width),
            tail[edge:].reshape(2, width),
            tail[:edge].reshape(NH, bucket_count).T,
            mixing_total,
            sums[0:2],
            sums[2:4],
            sums[4:6],
            expand_total,
            sums[6],
            contract_total,
        )

    return body


def solution(mesh):
    return jax.shard_map(
        make_body(mesh.shape["dp"]),
        mesh=mesh,
        in_specs=(
            P(("dp", "tensor"), None),
            P("dp", None),
            P("dp", None),
            P(),
            P(None, None, "tensor"),
            P(None, "tensor"),
            P(None, "tensor"),
            P("tensor", None),
            P(),
            P(),
            P(),
            P(None, "tensor"),
            P("tensor"),
            P("tensor", None),
            P(("dp", "tensor"), None),
        ),
        out_specs=(
            P(("dp", "tensor"), None),
            P(("dp", "tensor"), None),
            P(None, None, "tensor"),
            P(None, "tensor"),
            P(None, "tensor"),
            P("tensor", None),
            P(),
            P(),
            P(),
            P(None, "tensor"),
            P("tensor"),
            P("tensor", None),
        ),
        check_vma=False,
    )
```

```python
import functools
import jax
import jax.numpy as jnp
from jax import lax
from jax.experimental import pallas as pl
from jax.experimental.pallas import tpu as pltpu
from jax.sharding import PartitionSpec as P

big_negative = -1e30
KB = 128
QT = 256
HALF = 512
SEQ = 1024
HW = 64
NH = 3
TILES = 11
SPAN = 1536
f32 = jnp.float32
bf16 = jnp.bfloat16
dot32 = functools.partial(lax.dot_general, preferred_element_type=f32)
NN = (((1,), (0,)), ((), ()))
NT = (((1,), (1,)), ((), ()))


def took(micros):
    return pl.CostEstimate(flops=int(micros * 8e5), transcendentals=0, bytes_accessed=int(micros * 3e3))


def in_hbm(value):
    return pltpu.with_memory_space_constraint(value, pltpu.HBM)


def three_parts(value):
    high = value.astype(bf16)
    rest = value - high.astype(f32)
    middle = rest.astype(bf16)
    low = (rest - middle.astype(f32)).astype(bf16)
    return high, middle, low


def bucket_grid(bucket_ref, count):
    rows = lax.broadcasted_iota(jnp.int32, (count, SPAN), 0)
    return (rows == bucket_ref[...]).astype(bf16)


def tile_mask(key_code, seg_row, difference, shift):
    codes = jnp.concatenate([key_code, key_code], axis=1)
    return (codes == seg_row) | (difference == shift)


def prepare_kernel(place, seg_scalar, segments, padding, table, pair_bias, unit_bias,
                   limits, key_code, seg_row, small):
    flip = place[0]
    chip = place[1]
    segs = segments[pl.ds(chip, 1), :]
    code = jnp.where(padding[pl.ds(chip, 1), :] == 1, segs, -1).astype(f32)
    wide = segs.astype(f32)
    for b in range(SEQ // QT):
        seg_row[b] = wide[:, b * QT : (b + 1) * QT]
        first = seg_scalar[chip, b * QT]
        last = seg_scalar[chip, b * QT + QT - 1]
        limits[b] = jnp.sum((segs < first).astype(f32)).astype(jnp.int32) // KB
        limits[4 + b] = (jnp.sum((segs <= last).astype(f32)).astype(jnp.int32) + KB - 1) // KB
    limits[8] = flip
    for b in range(SEQ // KB):
        key_code[b] = jnp.broadcast_to(code[:, b * KB : (b + 1) * KB], (KB, KB)).T
    small[...] = jnp.zeros(small.shape, f32)
    small[0:NH, : table.shape[1]] = table[...]
    small[NH : NH + 2, : pair_bias.shape[1]] = pair_bias[...]
    small[NH + 2 : NH + 3, : unit_bias.shape[1]] = unit_bias[...]


def prepare(place, segment_ids, pad_mask, table, pair_bias, unit_bias):
    vm = pl.BlockSpec(memory_space=pltpu.VMEM)
    sm = pl.BlockSpec(memory_space=pltpu.SMEM)
    return pl.pallas_call(
        prepare_kernel,
        out_shape=(
            jax.ShapeDtypeStruct((9,), jnp.int32),
            jax.ShapeDtypeStruct((SEQ // KB, KB, KB), f32),
            jax.ShapeDtypeStruct((SEQ // QT, 1, QT), f32),
            jax.ShapeDtypeStruct((8, unit_bias.shape[1]), f32),
        ),
        in_specs=[sm, sm, vm, vm, vm, vm, vm],
        out_specs=(sm, vm, vm, vm),
        cost_estimate=took(2),
        name="prepare",
    )(place, segment_ids, segment_ids, pad_mask, table, pair_bias, unit_bias)


def forward_kernel(limits, x_own, x_other, weight, small, buckets, key_code, seg_row,
                   own_out, other_out, full_far, totals_far, heads_far, turned_far, tiles_far,
                   out_full, totals, heads_out, turned_out, tiles, best, total, gathered, done):
    flip = limits[8]

    def send(count, *pairs):
        copies = [
            pltpu.make_async_copy(near, far, done.at[count + i]) for i, (near, far) in enumerate(pairs)
        ]
        for copy in copies:
            copy.start()
        return copies

    width = NH * HW
    columns = small[:, :256].T
    for half, x_ref in enumerate((x_own, x_other)):
        plain = dot32(x_ref[...], weight[...], NT)
        across = dot32(weight[...], x_ref[...], NT)
        rows = pl.ds(half * HALF, HALF)
        for c in range(3):
            part, turned = plain[:, c * width : (c + 1) * width], across[c * width : (c + 1) * width]
            if c != 1:
                r = NH + c // 2
                part = part + small[r : r + 1, :width]
                turned = turned + columns[:width, r : r + 1]
            part, turned = part.astype(bf16), turned.astype(bf16)
            if c == 0:
                part, turned = part * 0.125, turned * 0.125
            for h in range(NH):
                heads_out[c * NH + h, rows, :] = part[:, h * HW : (h + 1) * HW]
            for k in range(HALF // KB):
                turned_out[half * (HALF // KB) + k, c * width : (c + 1) * width, :] = turned[
                    :, k * KB : (k + 1) * KB
                ]
    hot = bucket_grid(buckets, 256)
    line = sum(dot32(part, hot, NN) for part in three_parts(small[:, :256]))
    for h in range(NH):
        for u in range(TILES):
            start = 640 - 128 * (u - 5)
            spread = jnp.broadcast_to(line[h : h + 1, start : start + 256], (KB, 256))
            tiles[h, u] = pltpu.roll(spread, 129, 1, stride=1, stride_axis=0)[:, :KB]
    copies = send(0, (heads_out, heads_far), (turned_out, turned_far), (tiles, tiles_far))
    difference = lax.broadcasted_iota(jnp.int32, (KB, QT), 1) - lax.broadcasted_iota(
        jnp.int32, (KB, QT), 0
    )

    def query_step(block, carry):
        place = block ^ (flip * 2)
        best[...] = jnp.full(best.shape, big_negative, f32)
        total[...] = jnp.zeros(total.shape, f32)
        gathered[...] = jnp.zeros(gathered.shape, f32)
        segs = seg_row[place]

        def key_step(key_place, carry):
            key_block = key_place ^ (flip * 4)
            gap = key_place - 2 * place
            allowed = tile_mask(key_code[key_place], segs, difference, gap * KB)
            for h in range(NH):
                keys = heads_out[NH + h, pl.ds(key_block * KB, KB), :]
                turned_q = jnp.concatenate(
                    [turned_out[2 * block, h * HW : (h + 1) * HW, :],
                     turned_out[2 * block + 1, h * HW : (h + 1) * HW, :]], axis=1)
                scores = dot32(keys, turned_q, NN)
                scores = scores + jnp.concatenate(
                    [tiles[h, gap + 5], tiles[h, gap + 4]], axis=1
                )
                scores = jnp.where(allowed, scores, big_negative)
                old = best[h]
                new = jnp.maximum(old, jnp.max(scores, axis=0, keepdims=True))
                weightings = jnp.exp(scores - new)
                shrink = jnp.exp(old - new)
                best[h] = new
                total[h] = shrink * total[h] + jnp.sum(weightings, axis=0, keepdims=True)
                turned_v = turned_out[key_block, (2 * NH + h) * HW : (2 * NH + h + 1) * HW, :]
                gathered[h] = gathered[h] * shrink + dot32(turned_v, weightings.astype(bf16), NN)
            return carry

        lax.fori_loop(limits[place], limits[4 + place], key_step, 0)
        for h in range(NH):
            result = gathered[h] / total[h]
            out_full[block, h * HW : (h + 1) * HW, :] = result
            totals[block, h : h + 1, :] = best[h] + jnp.log(total[h])
        return carry

    lax.fori_loop(0, SEQ // QT, query_step, 0)
    copies = copies + send(3, (out_full, full_far), (totals, totals_far))
    for c in range(2):
        own_out[:, c * QT : (c + 1) * QT] = out_full[c].astype(bf16)
        other_out[:, c * QT : (c + 1) * QT] = out_full[2 + c].astype(bf16)
    for copy in copies:
        copy.wait()


def saved_shapes():
    return (
        ((SEQ // QT, NH * HW, QT), f32),
        ((SEQ // QT, 8, QT), f32),
        ((3 * NH, SEQ, HW), bf16),
        ((SEQ // KB, 3 * NH * HW, KB), bf16),
        ((NH, TILES, KB, KB), f32),
    )


def attend(limits, x_own, x_other, weight, small, buckets, key_code, seg_row):
    vm = pl.BlockSpec(memory_space=pltpu.VMEM)
    return pl.pallas_call(
        forward_kernel,
        out_shape=(
            jax.ShapeDtypeStruct((NH * HW, HALF), bf16),
            jax.ShapeDtypeStruct((NH * HW, HALF), bf16),
        )
        + tuple(pltpu.HBM(shape, kind) for shape, kind in saved_shapes()),
        in_specs=[pl.BlockSpec(memory_space=pltpu.SMEM)] + [vm] * 7,
        out_specs=(vm, vm) + (pl.BlockSpec(memory_space=pltpu.HBM),) * 5,
        scratch_shapes=[pltpu.VMEM(shape, kind) for shape, kind in saved_shapes()]
        + [
            pltpu.VMEM((NH, 1, QT), f32),
            pltpu.VMEM((NH, 1, QT), f32),
            pltpu.VMEM((NH, HW, QT), f32),
            pltpu.SemaphoreType.DMA((5,)),
        ],
        compiler_params=pltpu.CompilerParams(vmem_limit_bytes=20 << 20),
        cost_estimate=took(20),
        name="attend",
    )(limits, x_own, x_other, weight, small, buckets, key_code, seg_row)


def backward_kernel(limits, mixing, outgoing_own, outgoing_other, full_far, totals_far, heads_far,
                    turned_far, tiles_far, buckets, key_code, seg_row, x_own_far, x_other_far, weight_far, attended_own,
                    attended_other, early, early_there, *rest, last):
    if last:
        before_own_far, before_other_far, *rest = rest
    (pieces_out, own_out, other_out, tail_out,
     out_full, totals, heads, turned, tiles,
     turned_grad, plain_grad, row_dots, query_acc, query_all, key_acc, value_acc, tile_acc,
     grads, done, *rest) = rest
    flip = limits[8]
    fetched = [
        pltpu.make_async_copy(far, near, done.at[i])
        for i, (far, near) in enumerate(
            ((full_far, out_full), (totals_far, totals), (heads_far, heads), (turned_far, turned),
             (tiles_far, tiles))
        )
    ]
    x_own, x_other, weight, *rest = rest
    pairs = [(x_own_far, x_own), (x_other_far, x_other), (weight_far, weight)]
    if last:
        before_own, before_other = rest
        pairs += [(before_own_far, before_own), (before_other_far, before_other)]
    late = [pltpu.make_async_copy(far, near, done.at[5 + i]) for i, (far, near) in enumerate(pairs)]
    for copy in fetched:
        copy.start()
    key_acc[...] = jnp.zeros(key_acc.shape, f32)
    value_acc[...] = jnp.zeros(value_acc.shape, f32)
    tile_acc[...] = jnp.zeros(tile_acc.shape, f32)
    fetched[0].wait()
    for half, ref in enumerate((outgoing_own, outgoing_other)):
        across = dot32(mixing[...], ref[...], NT).astype(bf16)
        for c in range(2):
            block = 2 * half + c
            piece = across[:, c * QT : (c + 1) * QT]
            turned_grad[block] = piece
            wide = piece.astype(f32)
            product = wide * out_full[block]
            for h in range(NH):
                rows = slice(h * HW, (h + 1) * HW)
                row_dots[block, h : h + 1, :] = jnp.sum(product[rows], axis=0, keepdims=True)
                plain_grad[h, block * QT : (block + 1) * QT, :] = wide[rows].T.astype(bf16)
    for copy in fetched[1:]:
        copy.wait()
    for copy in late:
        copy.start()
    difference = lax.broadcasted_iota(jnp.int32, (KB, QT), 1) - lax.broadcasted_iota(
        jnp.int32, (KB, QT), 0
    )

    def query_step(block, carry):
        place = block ^ (flip * 2)
        query_acc[...] = jnp.zeros(query_acc.shape, f32)
        segs = seg_row[place]
        q_rows = pl.ds(block * QT, QT)

        def key_step(key_place, carry):
            key_block = key_place ^ (flip * 4)
            gap = key_place - 2 * place
            k_rows = pl.ds(key_block * KB, KB)
            allowed = tile_mask(key_code[key_place], segs, difference, gap * KB)
            for h in range(NH):
                keys = heads[NH + h, k_rows, :]
                turned_q = jnp.concatenate(
                    [turned[2 * block, h * HW : (h + 1) * HW, :],
                     turned[2 * block + 1, h * HW : (h + 1) * HW, :]], axis=1)
                scores = dot32(keys, turned_q, NN)
                scores = scores + jnp.concatenate(
                    [tiles[h, gap + 5], tiles[h, gap + 4]], axis=1
                )
                scores = jnp.where(allowed, scores, big_negative)
                chances = jnp.exp(scores - totals[block, h : h + 1, :])
                values = heads[2 * NH + h, k_rows, :]
                chance_grad = dot32(values, turned_grad[block, h * HW : (h + 1) * HW, :], NN)
                score_grad = chances * (chance_grad - row_dots[block, h : h + 1, :])
                tile_acc[h, gap + 5] += score_grad[:, :KB]
                tile_acc[h, gap + 4] += score_grad[:, KB:]
                score_low = score_grad.astype(bf16)
                value_acc[h, k_rows, :] += dot32(chances.astype(bf16), plain_grad[h, q_rows, :], NN)
                key_acc[h, k_rows, :] += dot32(score_low, heads[h, q_rows, :], NN)
                turned_k = turned[key_block, (NH + h) * HW : (NH + h + 1) * HW, :]
                query_acc[h] += dot32(turned_k, score_low, NN)
            return carry

        lax.fori_loop(limits[place], limits[4 + place], key_step, 0)
        for h in range(NH):
            query_all[h, q_rows, :] = (query_acc[h] * 0.125).T
        return carry

    lax.fori_loop(0, SEQ // QT, query_step, 0)
    width = NH * HW
    for g, acc in ((0, query_all), (1, key_acc), (2, value_acc)):
        for h in range(NH):
            at = (g * NH + h) * HW
            grads[:, at : at + HW] = acc[h].astype(bf16)
    tail_out[...] = jnp.zeros(tail_out.shape, f32)
    tail_out[5:11, :] = early[5:11, :] + early_there[5:11, :]
    r = 11 if last else 12
    tail_out[11:12, :] = early[r : r + 1, :] + early_there[r + 2 : r + 3, :]
    for r in range(2):
        sums = jnp.sum(grads[:, 2 * r * width : (2 * r + 1) * width].astype(f32), axis=0, keepdims=True)
        tail_out[NH + r : NH + r + 1, :width] = sums
    for copy in late:
        copy.wait()
    total = dot32(grads[:HALF, :], x_own[...], TN) + dot32(grads[HALF:, :], x_other[...], TN)
    mixed = dot32(attended_own[...], outgoing_own[...], NN) + dot32(
        attended_other[...], outgoing_other[...], NN
    )
    pieces = pieces_out.shape[0]
    first, second = total.shape[0] // pieces, mixed.shape[0] // pieces
    for p in range(pieces):
        pieces_out[p, :first] = total[p * first : (p + 1) * first].astype(bf16)
        pieces_out[p, first:] = mixed[p * second : (p + 1) * second].astype(bf16)
    own = dot32(grads[:HALF, :], weight[...], NN)
    other = dot32(grads[HALF:, :], weight[...], NN)
    if last:
        own = own + before_own[...]
        other = other + before_other[...]
    own_out[...] = own
    other_out[...] = other.astype(other_out.dtype)
    hot = bucket_grid(buckets, 256)
    lines = []
    for h in range(NH):
        spans = [jnp.zeros((1, KB), f32) for _ in range(SPAN // KB)]
        for u in range(TILES):
            wide = jnp.concatenate([tile_acc[h, u], jnp.zeros((KB, KB), f32)], axis=1)
            count = KB // 2
            while count:
                wide = wide[count:] + pltpu.roll(wide[:count], count, 1)
                count //= 2
            at = (640 - 128 * (u - 5)) // KB
            spans[at] = spans[at] + wide[:, :KB]
            spans[at + 1] = spans[at + 1] + wide[:, KB:]
        lines.append(jnp.concatenate(spans, axis=1))
    lines.append(jnp.zeros((8 - NH, SPAN), f32))
    line = jnp.concatenate(lines, axis=0)
    tail_out[:NH, :256] = sum(dot32(part, hot, NT) for part in three_parts(line))[:NH]


def attend_back(limits, *args, pieces, last):
    vm = pl.BlockSpec(memory_space=pltpu.VMEM)
    wide, model = args[13].shape
    rows = args[1].shape[0]
    piece = (wide + wide // 3) // pieces
    return pl.pallas_call(
        functools.partial(backward_kernel, last=last),
        out_shape=(
            jax.ShapeDtypeStruct((pieces, piece, model), bf16),
            jax.ShapeDtypeStruct((rows, model), f32),
            jax.ShapeDtypeStruct((rows, model), bf16 if last else f32),
            jax.ShapeDtypeStruct((16, model), f32),
        ),
        in_specs=[pl.BlockSpec(memory_space=pltpu.SMEM)] + [vm] * 3
        + [pl.BlockSpec(memory_space=pltpu.HBM)] * 5 + [vm] * 3
        + [pl.BlockSpec(memory_space=pltpu.HBM)] * 3 + [vm] * 4
        + [pl.BlockSpec(memory_space=pltpu.HBM)] * (2 if last else 0),
        out_specs=tuple([vm] * 4),
        scratch_shapes=[pltpu.VMEM(shape, kind) for shape, kind in saved_shapes()]
        + [
            pltpu.VMEM((SEQ // QT, NH * HW, QT), bf16),
            pltpu.VMEM((NH, SEQ, HW), bf16),
            pltpu.VMEM((SEQ // QT, 8, QT), f32),
            pltpu.VMEM((NH, HW, QT), f32),
            pltpu.VMEM((NH, SEQ, HW), f32),
            pltpu.VMEM((NH, SEQ, HW), f32),
            pltpu.VMEM((NH, SEQ, HW), f32),
            pltpu.VMEM((NH, TILES, KB, KB), f32),
            pltpu.VMEM((SEQ, 3 * NH * HW), bf16),
            pltpu.SemaphoreType.DMA((10,)),
            pltpu.VMEM((rows, model), bf16),
            pltpu.VMEM((rows, model), bf16),
            pltpu.VMEM((wide, model), bf16),
        ]
        + [pltpu.VMEM((rows, model), f32)] * (2 if last else 0),
        compiler_params=pltpu.CompilerParams(vmem_limit_bytes=36 << 20),
        cost_estimate=took(25),
        name="attend_back",
    )(limits, *args[:3], *[in_hbm(arg) for arg in args[3:8]], *args[8:11],
      *[in_hbm(arg) for arg in args[11:14]], *args[14:18], *[in_hbm(arg) for arg in args[18:]])


ROWS = 128
TN = (((0,), (0,)), ((), ()))
norm_eps = 1e-05


def whole(count):
    return [pl.BlockSpec(memory_space=pltpu.VMEM)] * count


def normalise(value):
    centered = value - jnp.mean(value, axis=-1, keepdims=True)
    inverse = lax.rsqrt(jnp.mean(centered * centered, axis=-1, keepdims=True) + norm_eps)
    return centered * inverse, inverse


def normalise_back(scaled, normed, inverse):
    first_mean = jnp.mean(scaled, axis=-1, keepdims=True)
    second_mean = jnp.mean(scaled * normed, axis=-1, keepdims=True)
    return inverse * (scaled - first_mean - normed * second_mean)


def gelu_parts(value):
    cumulative = 0.5 * (1.0 + lax.erf(value * 0.7071067811865476))
    density = jnp.exp(-0.5 * value * value) * 0.3989422804014327
    return (value * cumulative).astype(bf16), cumulative + value * density


def add_column(ref, at, value):
    ref[at] += jnp.sum(value.reshape(-1, 8, value.shape[1]), axis=0)


def first_half_kernel(tokens, own_a, recv_a, own_b, recv_b, mix0, mix1, mix2, mix3, biases, gains,
                      shifts, expand0, contract0, expand1, contract1, small0, small1,
                      normed_out, inverse_out, pair_out, hidden0_out, slope0_out, slope1_out, partial_out):
    def step(r, carry):
        at = pl.multiple_of(r * ROWS, ROWS)
        rows = pl.ds(at, ROWS)
        branch = tokens[rows, :].astype(f32) + biases[0:1, :]
        for attended, mixing in ((own_a, mix0), (recv_a, mix1), (own_b, mix2), (recv_b, mix3)):
            branch = branch + dot32(attended[:, rows], mixing[...], TN)
        normed, inverse = normalise(branch)
        normed_out[rows, :] = normed
        inverse_out[rows, :] = inverse
        low = (normed * gains[0:1, :] + shifts[0:1, :]).astype(bf16)
        pair_out[0, rows, :] = low
        partial = biases[1:2, :]
        for s, expand, contract, small in ((0, expand0, contract0, small0), (1, expand1, contract1, small1)):
            hidden, slope = gelu_parts(dot32(low, expand[...], NN) + small[5:6, :])
            if s == 0:
                hidden0_out[rows, :] = hidden
                slope0_out[rows, :] = slope
            else:
                pair_out[1, rows, :] = hidden
                slope1_out[rows, :] = slope
            partial = partial + dot32(hidden, contract[...], NN)
        partial_out[rows, :] = partial
        return carry

    lax.fori_loop(0, tokens.shape[0] // ROWS, step, 0)


def first_half(*args):
    rows, cols = args[0].shape
    wide = jax.ShapeDtypeStruct((rows, cols), f32)
    return pl.pallas_call(
        first_half_kernel,
        out_shape=(wide, jax.ShapeDtypeStruct((rows, 1), f32),
                   jax.ShapeDtypeStruct((2, rows, cols), bf16),
                   jax.ShapeDtypeStruct((rows, cols), bf16), wide, wide, wide),
        in_specs=whole(len(args)),
        out_specs=tuple(whole(7)),
        compiler_params=pltpu.CompilerParams(vmem_limit_bytes=16 << 20),
        cost_estimate=took(12),
        name="first_half",
    )(*args)


def third_slot_kernel(pair, expand, contract, small, partial_in, hidden_out, slope_out, partial_out):
    def step(r, carry):
        rows = pl.ds(pl.multiple_of(r * ROWS, ROWS), ROWS)
        hidden, slope = gelu_parts(dot32(pair[0, rows, :], expand[...], NN) + small[5:6, :])
        hidden_out[rows, :] = hidden
        slope_out[rows, :] = slope
        partial_out[rows, :] = partial_in[rows, :] + dot32(hidden, contract[...], NN)
        return carry

    lax.fori_loop(0, partial_in.shape[0] // ROWS, step, 0)


def third_slot(*args):
    rows, cols = args[4].shape
    wide = jax.ShapeDtypeStruct((rows, cols), f32)
    return pl.pallas_call(
        third_slot_kernel,
        out_shape=(jax.ShapeDtypeStruct((rows, cols), bf16), wide, wide),
        in_specs=whole(5),
        out_specs=tuple(whole(3)),
        compiler_params=pltpu.CompilerParams(vmem_limit_bytes=16 << 20),
        cost_estimate=took(5),
        name="third_slot",
    )(*args)


def second_half_kernel(normed_in, pair, partial_in, gains, shifts, expand3, contract3, contract1,
                       small, slope1, cotangent,
                       layer_out, grad_two_out, send_out, sums_out):
    sums_out[...] = jnp.zeros(sums_out.shape, f32)

    def step(r, carry):
        rows = pl.ds(pl.multiple_of(r * ROWS, ROWS), ROWS)
        low = pair[0, rows, :]
        total = normed_in[rows, :] * gains[0:1, :] + shifts[0:1, :] + partial_in[rows, :]
        hidden3, slope3 = gelu_parts(dot32(low, expand3[...], NN) + small[5:6, :])
        send_out[3, rows, :] = hidden3
        total = total + dot32(hidden3, contract3[...], NN)
        normed, inverse = normalise(total)
        layer_out[rows, :] = (normed * gains[1:2, :] + shifts[1:2, :]).astype(bf16)
        outer = cotangent[rows, :].astype(f32)
        grad_two = normalise_back(outer * gains[1:2, :], normed, inverse)
        grad_two_out[rows, :] = grad_two
        upstream = grad_two.astype(bf16)
        send_out[0, rows, :] = upstream
        add_column(sums_out, 0, grad_two)
        add_column(sums_out, 1, outer * normed)
        add_column(sums_out, 2, outer)
        for at, contract, slope in ((1, contract1, slope1[rows, :]), (2, contract3, slope3)):
            unit_grad = (dot32(upstream, contract[...], NT) * slope).astype(bf16)
            send_out[at, rows, :] = unit_grad
            add_column(sums_out, 2 + at, unit_grad.astype(f32))
        return carry

    lax.fori_loop(0, normed_in.shape[0] // ROWS, step, 0)


def second_half(*args):
    rows, cols = args[0].shape
    wide = jax.ShapeDtypeStruct((rows, cols), f32)
    low = jax.ShapeDtypeStruct((rows, cols), bf16)
    return pl.pallas_call(
        second_half_kernel,
        out_shape=(low, wide, jax.ShapeDtypeStruct((4, rows, cols), bf16),
                   jax.ShapeDtypeStruct((5, 8, cols), f32)),
        in_specs=whole(len(args)),
        out_specs=tuple(whole(4)),
        compiler_params=pltpu.CompilerParams(vmem_limit_bytes=16 << 20),
        cost_estimate=took(15),
        name="second_half",
    )(*args)


def unit_back_kernel(send, contract0, contract2, slope0, slope2, expand0, expand1, expand2, expand3,
                     grad_two, normed_in, inverse_in, gains, later,
                     grad0_out, grad2_out, grad_one_out, outgoing_out, rows_out, sums_out):
    sums_out[...] = jnp.zeros(sums_out.shape, f32)

    def step(r, carry):
        rows = pl.ds(pl.multiple_of(r * ROWS, ROWS), ROWS)
        upstream = send[0, rows, :]
        total = grad_two[rows, :]
        total = total + dot32(send[1, rows, :], expand1[...], NT)
        total = total + dot32(send[2, rows, :], expand3[...], NT)
        for at, contract, slope, expand, out in ((3, contract0, slope0, expand0, grad0_out),
                                                 (4, contract2, slope2, expand2, grad2_out)):
            unit_grad = (dot32(upstream, contract[...], NT) * slope[rows, :]).astype(bf16)
            out[rows, :] = unit_grad
            add_column(sums_out, at, unit_grad.astype(f32))
            total = total + dot32(unit_grad, expand[...], NT)
        normed = normed_in[rows, :]
        grad_one = normalise_back(total * gains[0:1, :], normed, inverse_in[rows, :])
        grad_one_out[rows, :] = grad_one
        outgoing_out[rows, :] = grad_one.astype(bf16)
        add_column(sums_out, 0, grad_one)
        add_column(sums_out, 1, total * normed)
        add_column(sums_out, 2, total)
        return carry

    lax.fori_loop(0, grad_two.shape[0] // ROWS, step, 0)
    rows_out[...] = jnp.zeros(rows_out.shape, f32)
    order = (sums_out[0], later[0], sums_out[1], later[1], sums_out[2], later[2],
             sums_out[3], sums_out[4], later[3], later[4])
    for r, value in enumerate(order):
        rows_out[5 + r : 6 + r, :] = jnp.sum(value, axis=0, keepdims=True)


def unit_back(*args):
    rows, cols = args[9].shape
    low = jax.ShapeDtypeStruct((rows, cols), bf16)
    return pl.pallas_call(
        unit_back_kernel,
        out_shape=(low, low, jax.ShapeDtypeStruct((rows, cols), f32), low,
                   jax.ShapeDtypeStruct((16, cols), f32)),
        in_specs=whole(len(args)),
        out_specs=tuple(whole(5)),
        scratch_shapes=[pltpu.VMEM((5, 8, cols), f32)],
        compiler_params=pltpu.CompilerParams(vmem_limit_bytes=16 << 20),
        cost_estimate=took(17),
        name="unit_back",
    )(*args)


def pair_grad_kernel(left, left_there, right, right_there, out):
    total = dot32(left[...], right[...], TN) + dot32(left_there[...], right_there[...], TN)
    rows = out.shape[1]
    for p in range(out.shape[0]):
        out[p] = total[p * rows : (p + 1) * rows].astype(bf16)


def pair_halves_kernel(place, left, left_there, right, right_there, keep_out, give_out):
    total = dot32(left[...], right[...], TN) + dot32(left_there[...], right_there[...], TN)
    rows = keep_out.shape[1]
    for q in range(keep_out.shape[0]):
        first = total[2 * q * rows : (2 * q + 1) * rows]
        second = total[(2 * q + 1) * rows : (2 * q + 2) * rows]
        keep_out[q] = jnp.where(place[0] & 1 == 0, first, second)
        give_out[q] = jnp.where(place[0] & 1 == 0, second, first).astype(bf16)


def pair_grad(pieces, *operands, place=None):
    arrays, specs = [], []
    for operand in operands:
        array, index = operand if isinstance(operand, tuple) else (operand[None], 0)
        arrays.append(array)
        specs.append(pl.BlockSpec((None,) + array.shape[1:], lambda i, index=index: (index, 0, 0)))
    rows, cols = arrays[0].shape[2] // pieces, arrays[2].shape[2]
    if place is None:
        kernel, count, kinds = pair_grad_kernel, pieces, (bf16,)
    else:
        kernel, count, kinds = pair_halves_kernel, pieces // 2, (f32, bf16)
        arrays.insert(0, place)
        specs.insert(0, pl.BlockSpec(memory_space=pltpu.SMEM))
    result = pl.pallas_call(
        kernel,
        out_shape=tuple(jax.ShapeDtypeStruct((count, rows, cols), kind) for kind in kinds),
        grid=(1,),
        in_specs=specs,
        out_specs=tuple(pl.BlockSpec((count, rows, cols), lambda i: (0, 0, 0)) for _ in kinds),
        compiler_params=pltpu.CompilerParams(vmem_limit_bytes=16 << 20),
        cost_estimate=took(4),
        name="pair_grad",
    )(*arrays)
    return result if place is not None else result[0]


def assemble_kernel(place, mine, theirs, *outs):
    low = place[0] & 1
    high = place[0] >> 1
    for r in range(mine.shape[0]):
        at = (r ^ high) * 2
        start = 0
        for out in outs:
            rows = out.shape[1]
            out[at + low] = mine[r, start : start + rows].astype(f32)
            out[at + 1 - low] = theirs[r, start : start + rows].astype(f32)
            start += rows


def assemble(place, mine, theirs, splits):
    half, rows, cols = mine.shape
    vm = pl.BlockSpec(memory_space=pltpu.VMEM)
    return pl.pallas_call(
        assemble_kernel,
        out_shape=tuple(jax.ShapeDtypeStruct((2 * half, part, cols), f32) for part in splits),
        in_specs=[pl.BlockSpec(memory_space=pltpu.SMEM), vm, vm],
        out_specs=tuple(vm for _ in splits),
        compiler_params=pltpu.CompilerParams(vmem_limit_bytes=32 << 20),
        cost_estimate=took(2),
        name="assemble",
    )(place, mine, theirs)


def small_call(kernel, name, outs, *args):
    vm = pl.BlockSpec(memory_space=pltpu.VMEM)
    return pl.pallas_call(
        kernel,
        out_shape=tuple(jax.ShapeDtypeStruct(shape, kind) for shape, kind in outs),
        in_specs=[pl.BlockSpec(memory_space=pltpu.SMEM)] + [vm] * (len(args) - 1),
        out_specs=tuple(vm for _ in outs),
        compiler_params=pltpu.CompilerParams(vmem_limit_bytes=16 << 20),
        cost_estimate=took(1),
        name=name,
    )(*args)


def split_kernel(digit, first, second, keep_out, give_out):
    for q in range(keep_out.shape[0]):
        keep, give = 2 * q + digit[0], 2 * q + 1 - digit[0]
        keep_out[q] = first[keep].astype(f32) + second[keep].astype(f32)
        give_out[q] = (first[give].astype(f32) + second[give].astype(f32)).astype(bf16)


def split(digit, first, second):
    shape = (first.shape[0] // 2,) + first.shape[1:]
    return small_call(split_kernel, "split", ((shape, f32), (shape, bf16)), digit, first, second)


def total_kernel(digit, first, second, out):
    out[...] = (first[...].astype(f32) + second[...].astype(f32)).astype(out.dtype)


def total_of(digit, first, second, kind):
    return small_call(total_kernel, "total", ((first.shape, kind),), digit, first, second)[0]


def join_kernel(digit, first, second, out):
    for q in range(first.shape[0]):
        out[2 * q] = first[q]
        out[2 * q + 1] = second[q]


def join(digit, first, second):
    shape = (2 * first.shape[0],) + first.shape[1:]
    return small_call(join_kernel, "join", ((shape, first.dtype),), digit, first, second)[0]


def make_body(dp_count):
    stages = dp_count.bit_length() - 1

    def swap(value, axis, count, bits):
        return lax.ppermute(value, axis, [(i, i ^ bits) for i in range(count)])

    swap_core = lambda value: swap(value, "tensor", 4, 1)
    swap_y = lambda value: swap(value, "tensor", 4, 2)
    swap_dp = lambda value, bits: swap(value, "dp", dp_count, bits)

    def sum_doubling(value):
        for bit in range(stages):
            value = value + (yield value, bit)
        return value

    def digit_of(bit):
        return (lax.axis_index("dp").astype(jnp.int32) >> bit & 1)[None]

    def sum_over_dp(keep, came, splits=None):
        for bit in range(1, stages):
            keep, give = split(digit_of(bit), keep, came)
            came = yield give, bit
        mine = total_of(digit_of(0), keep, came, bf16)
        for bit in range(stages - 1, 0, -1):
            came = yield mine, bit
            mine = join(digit_of(0), mine, came)
        theirs = yield mine, 0
        place = lax.axis_index("dp").astype(jnp.int32)[None]
        parts = assemble(place, mine, theirs, splits or (keep.shape[1],))
        return [part.reshape(-1, part.shape[2]) for part in parts]

    def sum_pieces(grad, across, splits):
        keep, give = split(digit_of(0), grad, across)
        came = yield give, 0
        return (yield from sum_over_dp(keep, came, splits))

    def interleave(order, steps):
        came = {name: None for name in steps}
        results = {}
        token = None
        names = list(order) + list(steps) * (4 * stages)
        for name in names:
            if name in results:
                continue
            try:
                value, bit = steps[name].send(came[name])
            except StopIteration as stop:
                results[name] = stop.value
                continue
            if token is not None:
                value = lax.optimization_barrier((value, token))[0]
            token = value
            came[name] = swap_dp(value, 1 << bit)
        return results

    def body(
        tokens,
        segment_ids,
        pad_mask,
        buckets,
        projections,
        projected_bias,
        relative_table,
        mixing_weight,
        residual_biases,
        norm_gains,
        norm_shifts,
        expand_weight,
        expand_bias,
        contract_weight,
        cotangent,
    ):
        rows_here, model_width = tokens.shape
        bucket_count = relative_table.shape[0]
        width = projections.shape[2]
        spot = lax.axis_index("tensor")
        flip = spot % 2

        def after(value, ready):
            return lax.optimization_barrier((value, ready))[0]

        dp_place = lax.axis_index("dp").astype(jnp.int32)
        odd = dp_place & 1
        weight_own = projections.transpose(1, 2, 0).reshape(3 * width, model_width)
        x_other = swap_core(tokens)
        weight_y = swap_y(weight_own)
        place = jnp.stack([flip, spot // 2]).astype(jnp.int32)
        limits, key_code, seg_row, small_own = prepare(
            place, segment_ids, pad_mask, relative_table.T, projected_bias, expand_bias[None]
        )
        mixing_y = swap_y(mixing_weight)
        half_rows = contract_weight.shape[0] // 2
        half_y = swap_y(lax.dynamic_slice_in_dim(contract_weight, odd * half_rows, half_rows, 0))
        small_y = swap_y(small_own)
        bucket_row = buckets[255:1791][::-1][None]

        def forward(weight, small, x_in):
            return attend(limits, x_in, x_other, weight, small, bucket_row, key_code, seg_row)

        own_a, other_a, *saved_a = forward(weight_own, small_own, tokens)
        expand_y = swap_y(after(expand_weight, own_a))
        half_x = swap_dp(after(half_y, own_a), 1)
        recv_a = swap_core(other_a)
        own_b, other_b, *saved_b = forward(weight_y, small_y, after(tokens, (own_a, half_y)))
        mixing_core, expand_core, contract_core, small_core = [
            swap_core(value)
            for value in after((mixing_weight, expand_weight, contract_weight, small_own), own_a)
        ]
        mixing_diag, small_diag = swap_core(after(mixing_y, own_a)), swap_core(after(small_y, own_a))
        recv_b = swap_core(other_b)
        contract_y = jnp.where(
            odd == 0, jnp.concatenate([half_y, half_x]), jnp.concatenate([half_x, half_y])
        )
        contract_diag = swap_core(contract_y)
        normed_one, inverse_one, pair, hidden0, slope0, slope1, partial = first_half(
            tokens, own_a, recv_a, own_b, recv_b, mixing_weight, mixing_core, mixing_y, mixing_diag,
            residual_biases, norm_gains, norm_shifts,
            expand_weight, contract_weight, expand_core, contract_core, small_own, small_core,
        )
        pair_there = swap_core(pair)
        expand_y = after(expand_y, partial)
        expand_diag = swap_core(expand_y)
        hidden2, slope2, partial = third_slot(pair, expand_y, contract_y, small_y, partial)
        layer_out, grad_two, send, later_sums = second_half(
            normed_one, pair, partial, norm_gains, norm_shifts,
            expand_diag, contract_diag, contract_core, small_diag, slope1, cotangent,
        )
        arrived = swap_core(send)
        unit_grad0, unit_grad2, grad_one, outgoing, early = unit_back(
            send, contract_weight, contract_y, slope0, slope2,
            expand_weight, expand_core, expand_y, expand_diag,
            grad_two, normed_one, inverse_one, norm_gains, later_sums,
        )
        outgoing_there = swap_core(outgoing)
        early_there = swap_core(early)

        contract_two = pair_grad(dp_count, hidden2, (arrived, 3), (send, 0), (arrived, 0))
        contract_across = swap_y(contract_two)
        keep_two, give_two = pair_grad(
            dp_count, (after(pair, contract_two), 0), (pair_there, 0), unit_grad2, (arrived, 2),
            place=dp_place[None],
        )
        keep_own, give_own = pair_grad(
            dp_count, (after(pair, give_two), 0), (pair_there, 0), unit_grad0, (arrived, 1),
            place=dp_place[None],
        )
        came_two, came_own = swap_dp(give_two, 1), swap_dp(give_own, 1)
        contract_own = pair_grad(
            dp_count, after(hidden0, give_own), (pair_there, 1), (send, 0), (arrived, 0)
        )

        def backward(saved, weight, mixing_here, attended, ready, before=()):
            return attend_back(
                limits, mixing_here, after(outgoing, ready), outgoing_there, *saved, bucket_row,
                key_code, seg_row, tokens, x_other, weight, *attended, early, early_there, *before,
                pieces=dp_count, last=bool(before),
            )

        pieces_b, inputs_own, inputs_other, tail_b = backward(
            saved_b, weight_y, mixing_y, (own_b, other_b), contract_own
        )
        pieces_y = swap_y(pieces_b)
        came_two, came_own = after((came_two, came_own), pieces_b)
        expand_two = total_of(digit_of(0), keep_two, came_two, bf16)
        expand_across = swap_y(expand_two)
        contract_keep, contract_give = split(
            digit_of(0), contract_own, after(contract_across, pieces_b)
        )
        contract_came = swap_dp(contract_give, 1)
        tail_y = swap_y(tail_b)
        pieces_a, inputs_own, inputs_other, tail_a = backward(
            saved_a, weight_own, mixing_weight, (own_a, other_a), (expand_two, contract_give),
            (inputs_own, inputs_other),
        )
        inputs_there = swap_core(inputs_other)
        contract_came = after(contract_came, pieces_a)
        expand_across, pieces_y, tail_y = after((expand_across, pieces_y, tail_y), pieces_a)
        results = interleave(
            "cpecescpecpsecpsepp",
            {
                "c": sum_over_dp(contract_keep, contract_came),
                "p": sum_pieces(pieces_a, pieces_y, (3 * width // dp_count, width // dp_count)),
                "e": sum_over_dp(total_of(digit_of(0), keep_own, came_own, f32), expand_across),
                "s": sum_doubling(tail_a + tail_y),
            },
        )
        (contract_total,), (expand_total,) = results["c"], results["e"]
        projection_total, mixing_total = results["p"]
        sums = results["s"]
        tokens_grad = inputs_own + inputs_there.astype(f32) + grad_one

        return (
            layer_out,
            tokens_grad,
            projection_total.reshape(3, width, model_width).transpose(2, 0, 1),
            sums[NH : NH + 2, :width],
            sums[:NH, :bucket_count].T,
            mixing_total,
            sums[5:7],
            sums[7:9],
            sums[9:11],
            expand_total,
            sums[11],
            contract_total,
        )

    return body


def solution(mesh):
    return jax.shard_map(
        make_body(mesh.shape["dp"]),
        mesh=mesh,
        in_specs=(
            P(("dp", "tensor"), None),
            P("dp", None),
            P("dp", None),
            P(),
            P(None, None, "tensor"),
            P(None, "tensor"),
            P(None, "tensor"),
            P("tensor", None),
            P(),
            P(),
            P(),
            P(None, "tensor"),
            P("tensor"),
            P("tensor", None),
            P(("dp", "tensor"), None),
        ),
        out_specs=(
            P(("dp", "tensor"), None),
            P(("dp", "tensor"), None),
            P(None, None, "tensor"),
            P(None, "tensor"),
            P(None, "tensor"),
            P("tensor", None),
            P(),
            P(),
            P(),
            P(None, "tensor"),
            P("tensor"),
            P("tensor", None),
        ),
        check_vma=False,
    )
```

```python
import functools
import jax
import jax.numpy as jnp
from jax import lax
from jax.experimental import pallas as pl
from jax.experimental.pallas import tpu as pltpu
from jax.sharding import PartitionSpec as P

big_negative = -1e30
KB = 128
QT = 256
HALF = 512
SEQ = 1024
HW = 64
NH = 3
TILES = 11
SPAN = 1536
f32 = jnp.float32
bf16 = jnp.bfloat16
dot32 = functools.partial(lax.dot_general, preferred_element_type=f32)
NN = (((1,), (0,)), ((), ()))
NT = (((1,), (1,)), ((), ()))


def took(micros):
    return pl.CostEstimate(flops=int(micros * 8e5), transcendentals=0, bytes_accessed=int(micros * 3e3))


def in_hbm(value):
    return pltpu.with_memory_space_constraint(value, pltpu.HBM)


def three_parts(value):
    high = value.astype(bf16)
    rest = value - high.astype(f32)
    middle = rest.astype(bf16)
    low = (rest - middle.astype(f32)).astype(bf16)
    return high, middle, low


def bucket_grid(bucket_ref, count):
    rows = lax.broadcasted_iota(jnp.int32, (count, SPAN), 0)
    return (rows == bucket_ref[...]).astype(bf16)


def tile_mask(key_code, seg_row, difference, shift):
    codes = jnp.concatenate([key_code, key_code], axis=1)
    return (codes == seg_row) | (difference == shift)


def prepare_kernel(place, seg_scalar, segments, padding, table, pair_bias, unit_bias,
                   limits, key_code, seg_row, small):
    flip = place[0]
    chip = place[1]
    segs = segments[pl.ds(chip, 1), :]
    code = jnp.where(padding[pl.ds(chip, 1), :] == 1, segs, -1).astype(f32)
    wide = segs.astype(f32)
    for b in range(SEQ // QT):
        seg_row[b] = wide[:, b * QT : (b + 1) * QT]
        first = seg_scalar[chip, b * QT]
        last = seg_scalar[chip, b * QT + QT - 1]
        limits[b] = jnp.sum((segs < first).astype(f32)).astype(jnp.int32) // KB
        limits[4 + b] = (jnp.sum((segs <= last).astype(f32)).astype(jnp.int32) + KB - 1) // KB
    limits[8] = flip
    for b in range(SEQ // KB):
        key_code[b] = jnp.broadcast_to(code[:, b * KB : (b + 1) * KB], (KB, KB)).T
    small[...] = jnp.zeros(small.shape, f32)
    small[0:NH, : table.shape[1]] = table[...]
    small[NH : NH + 2, : pair_bias.shape[1]] = pair_bias[...]
    small[NH + 2 : NH + 3, : unit_bias.shape[1]] = unit_bias[...]


def prepare(place, segment_ids, pad_mask, table, pair_bias, unit_bias):
    vm = pl.BlockSpec(memory_space=pltpu.VMEM)
    sm = pl.BlockSpec(memory_space=pltpu.SMEM)
    return pl.pallas_call(
        prepare_kernel,
        out_shape=(
            jax.ShapeDtypeStruct((9,), jnp.int32),
            jax.ShapeDtypeStruct((SEQ // KB, KB, KB), f32),
            jax.ShapeDtypeStruct((SEQ // QT, 1, QT), f32),
            jax.ShapeDtypeStruct((8, unit_bias.shape[1]), f32),
        ),
        in_specs=[sm, sm, vm, vm, vm, vm, vm],
        out_specs=(sm, vm, vm, vm),
        cost_estimate=took(2),
        name="prepare",
    )(place, segment_ids, segment_ids, pad_mask, table, pair_bias, unit_bias)


def forward_kernel(limits, x_own, x_other, weight, small, buckets, key_code, seg_row,
                   own_out, other_out, full_far, totals_far, heads_far, turned_far, tiles_far,
                   out_full, totals, heads_out, turned_out, tiles, best, total, gathered, done):
    flip = limits[8]

    def send(count, *pairs):
        copies = [
            pltpu.make_async_copy(near, far, done.at[count + i]) for i, (near, far) in enumerate(pairs)
        ]
        for copy in copies:
            copy.start()
        return copies

    width = NH * HW
    columns = small[:, :256].T
    for half, x_ref in enumerate((x_own, x_other)):
        plain = dot32(x_ref[...], weight[...], NT)
        across = dot32(weight[...], x_ref[...], NT)
        rows = pl.ds(half * HALF, HALF)
        for c in range(3):
            part, turned = plain[:, c * width : (c + 1) * width], across[c * width : (c + 1) * width]
            if c != 1:
                r = NH + c // 2
                part = part + small[r : r + 1, :width]
                turned = turned + columns[:width, r : r + 1]
            part, turned = part.astype(bf16), turned.astype(bf16)
            if c == 0:
                part, turned = part * 0.125, turned * 0.125
            for h in range(NH):
                heads_out[c * NH + h, rows, :] = part[:, h * HW : (h + 1) * HW]
            for k in range(HALF // KB):
                turned_out[half * (HALF // KB) + k, c * width : (c + 1) * width, :] = turned[
                    :, k * KB : (k + 1) * KB
                ]
    hot = bucket_grid(buckets, 256)
    line = sum(dot32(part, hot, NN) for part in three_parts(small[:, :256]))
    for h in range(NH):
        for u in range(TILES):
            start = 640 - 128 * (u - 5)
            spread = jnp.broadcast_to(line[h : h + 1, start : start + 256], (KB, 256))
            tiles[h, u] = pltpu.roll(spread, 129, 1, stride=1, stride_axis=0)[:, :KB]
    copies = send(0, (heads_out, heads_far), (turned_out, turned_far), (tiles, tiles_far))
    difference = lax.broadcasted_iota(jnp.int32, (KB, QT), 1) - lax.broadcasted_iota(
        jnp.int32, (KB, QT), 0
    )

    def query_step(block, carry):
        place = block ^ (flip * 2)
        best[...] = jnp.full(best.shape, big_negative, f32)
        total[...] = jnp.zeros(total.shape, f32)
        gathered[...] = jnp.zeros(gathered.shape, f32)
        segs = seg_row[place]

        def key_step(key_place, carry):
            key_block = key_place ^ (flip * 4)
            gap = key_place - 2 * place
            allowed = tile_mask(key_code[key_place], segs, difference, gap * KB)
            queries = [
                jnp.concatenate([turned_out[2 * block + i, h * HW : (h + 1) * HW, :] for i in range(2)], axis=1)
                for h in range(NH)
            ]
            k_rows = pl.ds(key_block * KB, KB)
            scores = [dot32(heads_out[NH + h, k_rows, :], queries[h], NN) for h in range(NH)]
            lows, shrinks = [], []
            for h in range(NH):
                bias = jnp.concatenate([tiles[h, gap + 5], tiles[h, gap + 4]], axis=1)
                value = jnp.where(allowed, scores[h] + bias, big_negative)
                old = best[h]
                new = jnp.maximum(old, jnp.max(value, axis=0, keepdims=True))
                value = jnp.exp(value - new)
                shrink = jnp.exp(old - new)
                best[h] = new
                total[h] = shrink * total[h] + jnp.sum(value, axis=0, keepdims=True)
                lows.append(value.astype(bf16))
                shrinks.append(shrink)
            for h in range(NH):
                turned_v = turned_out[key_block, (2 * NH + h) * HW : (2 * NH + h + 1) * HW, :]
                gathered[h] = gathered[h] * shrinks[h] + dot32(turned_v, lows[h], NN)
            return carry

        lax.fori_loop(limits[place], limits[4 + place], key_step, 0)
        for h in range(NH):
            result = gathered[h] / total[h]
            out_full[block, h * HW : (h + 1) * HW, :] = result
            totals[block, h : h + 1, :] = best[h] + jnp.log(total[h])
        return carry

    lax.fori_loop(0, SEQ // QT, query_step, 0)
    copies = copies + send(3, (out_full, full_far), (totals, totals_far))
    for c in range(2):
        own_out[:, c * QT : (c + 1) * QT] = out_full[c].astype(bf16)
        other_out[:, c * QT : (c + 1) * QT] = out_full[2 + c].astype(bf16)
    for copy in copies:
        copy.wait()


def saved_shapes():
    return (
        ((SEQ // QT, NH * HW, QT), f32),
        ((SEQ // QT, 8, QT), f32),
        ((3 * NH, SEQ, HW), bf16),
        ((SEQ // KB, 3 * NH * HW, KB), bf16),
        ((NH, TILES, KB, KB), f32),
    )


def attend(limits, x_own, x_other, weight, small, buckets, key_code, seg_row):
    vm = pl.BlockSpec(memory_space=pltpu.VMEM)
    return pl.pallas_call(
        forward_kernel,
        out_shape=(
            jax.ShapeDtypeStruct((NH * HW, HALF), bf16),
            jax.ShapeDtypeStruct((NH * HW, HALF), bf16),
        )
        + tuple(pltpu.HBM(shape, kind) for shape, kind in saved_shapes()),
        in_specs=[pl.BlockSpec(memory_space=pltpu.SMEM)] + [vm] * 7,
        out_specs=(vm, vm) + (pl.BlockSpec(memory_space=pltpu.HBM),) * 5,
        scratch_shapes=[pltpu.VMEM(shape, kind) for shape, kind in saved_shapes()]
        + [
            pltpu.VMEM((NH, 1, QT), f32),
            pltpu.VMEM((NH, 1, QT), f32),
            pltpu.VMEM((NH, HW, QT), f32),
            pltpu.SemaphoreType.DMA((5,)),
        ],
        compiler_params=pltpu.CompilerParams(vmem_limit_bytes=20 << 20),
        cost_estimate=took(20),
        name="attend",
    )(limits, x_own, x_other, weight, small, buckets, key_code, seg_row)


def backward_kernel(limits, mixing, outgoing_own, outgoing_other, full_far, totals_far, heads_far,
                    turned_far, tiles_far, buckets, key_code, seg_row, x_own_far, x_other_far, weight_far, attended_own,
                    attended_other, early, early_there, *rest, last):
    if last:
        before_own_far, before_other_far, *rest = rest
    (pieces_out, own_out, other_out, tail_out,
     out_full, totals, heads, turned, tiles,
     turned_grad, plain_grad, row_dots, query_acc, query_all, key_acc, value_acc, tile_acc,
     grads, done, *rest) = rest
    flip = limits[8]
    fetched = [
        pltpu.make_async_copy(far, near, done.at[i])
        for i, (far, near) in enumerate(
            ((full_far, out_full), (totals_far, totals), (heads_far, heads), (turned_far, turned),
             (tiles_far, tiles))
        )
    ]
    x_own, x_other, weight, *rest = rest
    pairs = [(x_own_far, x_own), (x_other_far, x_other), (weight_far, weight)]
    if last:
        before_own, before_other = rest
        pairs += [(before_own_far, before_own), (before_other_far, before_other)]
    late = [pltpu.make_async_copy(far, near, done.at[5 + i]) for i, (far, near) in enumerate(pairs)]
    for copy in fetched:
        copy.start()
    key_acc[...] = jnp.zeros(key_acc.shape, f32)
    value_acc[...] = jnp.zeros(value_acc.shape, f32)
    tile_acc[...] = jnp.zeros(tile_acc.shape, f32)
    fetched[0].wait()
    for half, ref in enumerate((outgoing_own, outgoing_other)):
        across = dot32(mixing[...], ref[...], NT).astype(bf16)
        for c in range(2):
            block = 2 * half + c
            piece = across[:, c * QT : (c + 1) * QT]
            turned_grad[block] = piece
            wide = piece.astype(f32)
            product = wide * out_full[block]
            for h in range(NH):
                rows = slice(h * HW, (h + 1) * HW)
                row_dots[block, h : h + 1, :] = jnp.sum(product[rows], axis=0, keepdims=True)
                plain_grad[h, block * QT : (block + 1) * QT, :] = wide[rows].T.astype(bf16)
    for copy in fetched[1:]:
        copy.wait()
    for copy in late:
        copy.start()
    difference = lax.broadcasted_iota(jnp.int32, (KB, QT), 1) - lax.broadcasted_iota(
        jnp.int32, (KB, QT), 0
    )

    def query_step(block, carry):
        place = block ^ (flip * 2)
        query_acc[...] = jnp.zeros(query_acc.shape, f32)
        segs = seg_row[place]
        q_rows = pl.ds(block * QT, QT)

        def key_step(key_place, carry):
            key_block = key_place ^ (flip * 4)
            gap = key_place - 2 * place
            k_rows = pl.ds(key_block * KB, KB)
            allowed = tile_mask(key_code[key_place], segs, difference, gap * KB)
            queries = [
                jnp.concatenate([turned[2 * block + i, h * HW : (h + 1) * HW, :] for i in range(2)], axis=1)
                for h in range(NH)
            ]
            scores = [dot32(heads[NH + h, k_rows, :], queries[h], NN) for h in range(NH)]
            chance_grads = [
                dot32(heads[2 * NH + h, k_rows, :], turned_grad[block, h * HW : (h + 1) * HW, :], NN)
                for h in range(NH)
            ]
            chances, score_lows = [], []
            for h in range(NH):
                bias = jnp.concatenate([tiles[h, gap + 5], tiles[h, gap + 4]], axis=1)
                value = jnp.where(allowed, scores[h] + bias, big_negative)
                chance = jnp.exp(value - totals[block, h : h + 1, :])
                score_grad = chance * (chance_grads[h] - row_dots[block, h : h + 1, :])
                tile_acc[h, gap + 5] += score_grad[:, :KB]
                tile_acc[h, gap + 4] += score_grad[:, KB:]
                chances.append(chance.astype(bf16))
                score_lows.append(score_grad.astype(bf16))
            for h in range(NH):
                value_acc[h, k_rows, :] += dot32(chances[h], plain_grad[h, q_rows, :], NN)
            for h in range(NH):
                key_acc[h, k_rows, :] += dot32(score_lows[h], heads[h, q_rows, :], NN)
            for h in range(NH):
                turned_k = turned[key_block, (NH + h) * HW : (NH + h + 1) * HW, :]
                query_acc[h] += dot32(turned_k, score_lows[h], NN)
            return carry

        lax.fori_loop(limits[place], limits[4 + place], key_step, 0)
        for h in range(NH):
            query_all[h, q_rows, :] = (query_acc[h] * 0.125).T
        return carry

    lax.fori_loop(0, SEQ // QT, query_step, 0)
    width = NH * HW
    for g, acc in ((0, query_all), (1, key_acc), (2, value_acc)):
        for h in range(NH):
            at = (g * NH + h) * HW
            grads[:, at : at + HW] = acc[h].astype(bf16)
    tail_out[...] = jnp.zeros(tail_out.shape, f32)
    tail_out[5:11, :] = early[5:11, :] + early_there[5:11, :]
    r = 11 if last else 12
    tail_out[11:12, :] = early[r : r + 1, :] + early_there[r + 2 : r + 3, :]
    for r in range(2):
        sums = jnp.sum(grads[:, 2 * r * width : (2 * r + 1) * width].astype(f32), axis=0, keepdims=True)
        tail_out[NH + r : NH + r + 1, :width] = sums
    for copy in late:
        copy.wait()
    total = dot32(grads[:HALF, :], x_own[...], TN) + dot32(grads[HALF:, :], x_other[...], TN)
    mixed = dot32(attended_own[...], outgoing_own[...], NN) + dot32(
        attended_other[...], outgoing_other[...], NN
    )
    pieces = pieces_out.shape[0]
    first, second = total.shape[0] // pieces, mixed.shape[0] // pieces
    for p in range(pieces):
        pieces_out[p, :first] = total[p * first : (p + 1) * first].astype(bf16)
        pieces_out[p, first:] = mixed[p * second : (p + 1) * second].astype(bf16)
    own = dot32(grads[:HALF, :], weight[...], NN)
    other = dot32(grads[HALF:, :], weight[...], NN)
    if last:
        own = own + before_own[...]
        other = other + before_other[...]
    own_out[...] = own
    other_out[...] = other.astype(other_out.dtype)
    hot = bucket_grid(buckets, 256)
    lines = []
    for h in range(NH):
        spans = [jnp.zeros((1, KB), f32) for _ in range(SPAN // KB)]
        for u in range(TILES):
            wide = jnp.concatenate([tile_acc[h, u], jnp.zeros((KB, KB), f32)], axis=1)
            count = KB // 2
            while count:
                wide = wide[count:] + pltpu.roll(wide[:count], count, 1)
                count //= 2
            at = (640 - 128 * (u - 5)) // KB
            spans[at] = spans[at] + wide[:, :KB]
            spans[at + 1] = spans[at + 1] + wide[:, KB:]
        lines.append(jnp.concatenate(spans, axis=1))
    lines.append(jnp.zeros((8 - NH, SPAN), f32))
    line = jnp.concatenate(lines, axis=0)
    tail_out[:NH, :256] = sum(dot32(part, hot, NT) for part in three_parts(line))[:NH]


def attend_back(limits, *args, pieces, last):
    vm = pl.BlockSpec(memory_space=pltpu.VMEM)
    wide, model = args[13].shape
    rows = args[1].shape[0]
    piece = (wide + wide // 3) // pieces
    return pl.pallas_call(
        functools.partial(backward_kernel, last=last),
        out_shape=(
            jax.ShapeDtypeStruct((pieces, piece, model), bf16),
            (jax.ShapeDtypeStruct if last else pltpu.HBM)((rows, model), f32),
            (jax.ShapeDtypeStruct if last else pltpu.HBM)((rows, model), bf16 if last else f32),
            jax.ShapeDtypeStruct((16, model), f32),
        ),
        in_specs=[pl.BlockSpec(memory_space=pltpu.SMEM)] + [vm] * 3
        + [pl.BlockSpec(memory_space=pltpu.HBM)] * 5 + [vm] * 3
        + [pl.BlockSpec(memory_space=pltpu.HBM)] * 3 + [vm] * 4
        + [pl.BlockSpec(memory_space=pltpu.HBM)] * (2 if last else 0),
        out_specs=tuple([vm] * 4),
        scratch_shapes=[pltpu.VMEM(shape, kind) for shape, kind in saved_shapes()]
        + [
            pltpu.VMEM((SEQ // QT, NH * HW, QT), bf16),
            pltpu.VMEM((NH, SEQ, HW), bf16),
            pltpu.VMEM((SEQ // QT, 8, QT), f32),
            pltpu.VMEM((NH, HW, QT), f32),
            pltpu.VMEM((NH, SEQ, HW), f32),
            pltpu.VMEM((NH, SEQ, HW), f32),
            pltpu.VMEM((NH, SEQ, HW), f32),
            pltpu.VMEM((NH, TILES, KB, KB), f32),
            pltpu.VMEM((SEQ, 3 * NH * HW), bf16),
            pltpu.SemaphoreType.DMA((10,)),
            pltpu.VMEM((rows, model), bf16),
            pltpu.VMEM((rows, model), bf16),
            pltpu.VMEM((wide, model), bf16),
        ]
        + [pltpu.VMEM((rows, model), f32)] * (2 if last else 0),
        compiler_params=pltpu.CompilerParams(vmem_limit_bytes=36 << 20),
        cost_estimate=took(25),
        name="attend_back",
    )(limits, *args[:3], *[in_hbm(arg) for arg in args[3:8]], *args[8:11],
      *[in_hbm(arg) for arg in args[11:14]], *args[14:18], *[in_hbm(arg) for arg in args[18:]])


ROWS = 128
TN = (((0,), (0,)), ((), ()))
norm_eps = 1e-05


def whole(count):
    return [pl.BlockSpec(memory_space=pltpu.VMEM)] * count


def normalise(value):
    centered = value - jnp.mean(value, axis=-1, keepdims=True)
    inverse = lax.rsqrt(jnp.mean(centered * centered, axis=-1, keepdims=True) + norm_eps)
    return centered * inverse, inverse


def normalise_back(scaled, normed, inverse):
    first_mean = jnp.mean(scaled, axis=-1, keepdims=True)
    second_mean = jnp.mean(scaled * normed, axis=-1, keepdims=True)
    return inverse * (scaled - first_mean - normed * second_mean)


def gelu_parts(value):
    cumulative = 0.5 * (1.0 + lax.erf(value * 0.7071067811865476))
    density = jnp.exp(-0.5 * value * value) * 0.3989422804014327
    return (value * cumulative).astype(bf16), cumulative + value * density


def add_column(ref, at, value):
    ref[at] += jnp.sum(value.reshape(-1, 8, value.shape[1]), axis=0)


def first_half_kernel(tokens, own_a, recv_a, own_b, recv_b, mix0, mix1, mix2, mix3, biases, gains,
                      shifts, expand0, contract0, expand1, contract1, small0, small1,
                      normed_out, inverse_out, pair_out, hidden0_out, slope0_out, slope1_out, partial_out):
    def step(r, carry):
        at = pl.multiple_of(r * ROWS, ROWS)
        rows = pl.ds(at, ROWS)
        branch = tokens[rows, :].astype(f32) + biases[0:1, :]
        for attended, mixing in ((own_a, mix0), (recv_a, mix1), (own_b, mix2), (recv_b, mix3)):
            branch = branch + dot32(attended[:, rows], mixing[...], TN)
        normed, inverse = normalise(branch)
        normed_out[rows, :] = normed
        inverse_out[rows, :] = inverse
        low = (normed * gains[0:1, :] + shifts[0:1, :]).astype(bf16)
        pair_out[0, rows, :] = low
        partial = biases[1:2, :]
        for s, expand, contract, small in ((0, expand0, contract0, small0), (1, expand1, contract1, small1)):
            hidden, slope = gelu_parts(dot32(low, expand[...], NN) + small[5:6, :])
            if s == 0:
                hidden0_out[rows, :] = hidden
                slope0_out[rows, :] = slope
            else:
                pair_out[1, rows, :] = hidden
                slope1_out[rows, :] = slope
            partial = partial + dot32(hidden, contract[...], NN)
        partial_out[rows, :] = partial
        return carry

    lax.fori_loop(0, tokens.shape[0] // ROWS, step, 0)


def first_half(*args):
    rows, cols = args[0].shape
    wide = jax.ShapeDtypeStruct((rows, cols), f32)
    return pl.pallas_call(
        first_half_kernel,
        out_shape=(wide, jax.ShapeDtypeStruct((rows, 1), f32),
                   jax.ShapeDtypeStruct((2, rows, cols), bf16),
                   jax.ShapeDtypeStruct((rows, cols), bf16), wide, wide, wide),
        in_specs=whole(len(args)),
        out_specs=tuple(whole(7)),
        compiler_params=pltpu.CompilerParams(vmem_limit_bytes=16 << 20),
        cost_estimate=took(12),
        name="first_half",
    )(*args)


def third_slot_kernel(pair, expand, contract, small, partial_in, hidden_out, slope_out, partial_out):
    def step(r, carry):
        rows = pl.ds(pl.multiple_of(r * ROWS, ROWS), ROWS)
        hidden, slope = gelu_parts(dot32(pair[0, rows, :], expand[...], NN) + small[5:6, :])
        hidden_out[rows, :] = hidden
        slope_out[rows, :] = slope
        partial_out[rows, :] = partial_in[rows, :] + dot32(hidden, contract[...], NN)
        return carry

    lax.fori_loop(0, partial_in.shape[0] // ROWS, step, 0)


def third_slot(*args):
    rows, cols = args[4].shape
    wide = jax.ShapeDtypeStruct((rows, cols), f32)
    return pl.pallas_call(
        third_slot_kernel,
        out_shape=(jax.ShapeDtypeStruct((rows, cols), bf16), wide, wide),
        in_specs=whole(5),
        out_specs=tuple(whole(3)),
        compiler_params=pltpu.CompilerParams(vmem_limit_bytes=16 << 20),
        cost_estimate=took(5),
        name="third_slot",
    )(*args)


def second_half_kernel(normed_in, pair, partial_in, gains, shifts, expand3, contract3, contract1,
                       small, slope1, cotangent,
                       layer_out, grad_two_out, send_out, sums_out):
    sums_out[...] = jnp.zeros(sums_out.shape, f32)

    def step(r, carry):
        rows = pl.ds(pl.multiple_of(r * ROWS, ROWS), ROWS)
        low = pair[0, rows, :]
        total = normed_in[rows, :] * gains[0:1, :] + shifts[0:1, :] + partial_in[rows, :]
        hidden3, slope3 = gelu_parts(dot32(low, expand3[...], NN) + small[5:6, :])
        send_out[3, rows, :] = hidden3
        total = total + dot32(hidden3, contract3[...], NN)
        normed, inverse = normalise(total)
        layer_out[rows, :] = (normed * gains[1:2, :] + shifts[1:2, :]).astype(bf16)
        outer = cotangent[rows, :].astype(f32)
        grad_two = normalise_back(outer * gains[1:2, :], normed, inverse)
        grad_two_out[rows, :] = grad_two
        upstream = grad_two.astype(bf16)
        send_out[0, rows, :] = upstream
        add_column(sums_out, 0, grad_two)
        add_column(sums_out, 1, outer * normed)
        add_column(sums_out, 2, outer)
        for at, contract, slope in ((1, contract1, slope1[rows, :]), (2, contract3, slope3)):
            unit_grad = (dot32(upstream, contract[...], NT) * slope).astype(bf16)
            send_out[at, rows, :] = unit_grad
            add_column(sums_out, 2 + at, unit_grad.astype(f32))
        return carry

    lax.fori_loop(0, normed_in.shape[0] // ROWS, step, 0)


def second_half(*args):
    rows, cols = args[0].shape
    wide = jax.ShapeDtypeStruct((rows, cols), f32)
    low = jax.ShapeDtypeStruct((rows, cols), bf16)
    return pl.pallas_call(
        second_half_kernel,
        out_shape=(low, wide, jax.ShapeDtypeStruct((4, rows, cols), bf16),
                   jax.ShapeDtypeStruct((5, 8, cols), f32)),
        in_specs=whole(len(args)),
        out_specs=tuple(whole(4)),
        compiler_params=pltpu.CompilerParams(vmem_limit_bytes=16 << 20),
        cost_estimate=took(15),
        name="second_half",
    )(*args)


def unit_back_kernel(send, contract0, contract2, slope0, slope2, expand0, expand1, expand2, expand3,
                     grad_two, normed_in, inverse_in, gains, later,
                     grad0_out, grad2_out, grad_one_out, outgoing_out, rows_out, sums_out):
    sums_out[...] = jnp.zeros(sums_out.shape, f32)

    def step(r, carry):
        rows = pl.ds(pl.multiple_of(r * ROWS, ROWS), ROWS)
        upstream = send[0, rows, :]
        total = grad_two[rows, :]
        total = total + dot32(send[1, rows, :], expand1[...], NT)
        total = total + dot32(send[2, rows, :], expand3[...], NT)
        for at, contract, slope, expand, out in ((3, contract0, slope0, expand0, grad0_out),
                                                 (4, contract2, slope2, expand2, grad2_out)):
            unit_grad = (dot32(upstream, contract[...], NT) * slope[rows, :]).astype(bf16)
            out[rows, :] = unit_grad
            add_column(sums_out, at, unit_grad.astype(f32))
            total = total + dot32(unit_grad, expand[...], NT)
        normed = normed_in[rows, :]
        grad_one = normalise_back(total * gains[0:1, :], normed, inverse_in[rows, :])
        grad_one_out[rows, :] = grad_one
        outgoing_out[rows, :] = grad_one.astype(bf16)
        add_column(sums_out, 0, grad_one)
        add_column(sums_out, 1, total * normed)
        add_column(sums_out, 2, total)
        return carry

    lax.fori_loop(0, grad_two.shape[0] // ROWS, step, 0)
    rows_out[...] = jnp.zeros(rows_out.shape, f32)
    order = (sums_out[0], later[0], sums_out[1], later[1], sums_out[2], later[2],
             sums_out[3], sums_out[4], later[3], later[4])
    for r, value in enumerate(order):
        rows_out[5 + r : 6 + r, :] = jnp.sum(value, axis=0, keepdims=True)


def unit_back(*args):
    rows, cols = args[9].shape
    low = jax.ShapeDtypeStruct((rows, cols), bf16)
    return pl.pallas_call(
        unit_back_kernel,
        out_shape=(low, low, jax.ShapeDtypeStruct((rows, cols), f32), low,
                   jax.ShapeDtypeStruct((16, cols), f32)),
        in_specs=whole(len(args)),
        out_specs=tuple(whole(5)),
        scratch_shapes=[pltpu.VMEM((5, 8, cols), f32)],
        compiler_params=pltpu.CompilerParams(vmem_limit_bytes=16 << 20),
        cost_estimate=took(17),
        name="unit_back",
    )(*args)


def pair_grad_kernel(left, left_there, right, right_there, out):
    total = dot32(left[...], right[...], TN) + dot32(left_there[...], right_there[...], TN)
    rows = out.shape[1]
    for p in range(out.shape[0]):
        out[p] = total[p * rows : (p + 1) * rows].astype(bf16)


def both_halves_kernel(digit, two, two_there, own, own_there, right, right_there, keep_out, give_out):
    half, rows, _ = keep_out.shape
    half //= 2
    bits = half.bit_length()
    for slot, (left, left_there) in enumerate(((two, two_there), (own, own_there))):
        total = dot32(left[...], right[...], TN) + dot32(left_there[...], right_there[...], TN)
        for q in range(half):
            first = q if bits < 2 else (q >> bits - 2) | sum(
                (q >> i & 1) << i + 2 for i in range(bits - 2)
            )
            step = 1 if bits < 2 else 2
            low = total[first * rows : (first + 1) * rows]
            high = total[(first + step) * rows : (first + step + 1) * rows]
            keep_out[slot * half + q] = jnp.where(digit[0] == 0, low, high)
            give_out[slot * half + q] = jnp.where(digit[0] == 0, high, low).astype(bf16)


def indexed(operand):
    array, index = operand if isinstance(operand, tuple) else (operand[None], 0)
    return array, pl.BlockSpec((None,) + array.shape[1:], lambda i, index=index: (index, 0, 0))


def both_halves(digit, pieces, *operands):
    arrays, specs = zip(*[indexed(operand) for operand in operands])
    rows, cols = arrays[0].shape[2] // pieces, arrays[4].shape[2]
    return pl.pallas_call(
        both_halves_kernel,
        out_shape=tuple(jax.ShapeDtypeStruct((pieces, rows, cols), kind) for kind in (f32, bf16)),
        grid=(1,),
        in_specs=[pl.BlockSpec(memory_space=pltpu.SMEM)] + list(specs),
        out_specs=tuple(pl.BlockSpec((pieces, rows, cols), lambda i: (0, 0, 0)) for _ in range(2)),
        compiler_params=pltpu.CompilerParams(vmem_limit_bytes=14 << 20),
        cost_estimate=took(4),
        name="both_halves",
    )(digit, *arrays)


def pair_grad(pieces, *operands):
    arrays, specs = zip(*[indexed(operand) for operand in operands])
    rows, cols = arrays[0].shape[2] // pieces, arrays[2].shape[2]
    return pl.pallas_call(
        pair_grad_kernel,
        out_shape=jax.ShapeDtypeStruct((pieces, rows, cols), bf16),
        grid=(1,),
        in_specs=list(specs),
        out_specs=pl.BlockSpec((pieces, rows, cols), lambda i: (0, 0, 0)),
        compiler_params=pltpu.CompilerParams(vmem_limit_bytes=16 << 20),
        cost_estimate=took(4),
        name="pair_grad",
    )(*arrays)


def assemble_kernel(place, mine, theirs, *outs):
    low = place[0] & 1
    high = place[0] >> 1
    for r in range(mine.shape[0]):
        at = (r ^ high) * 2
        start = 0
        for out in outs:
            rows = out.shape[1]
            out[at + low] = mine[r, start : start + rows].astype(f32)
            out[at + 1 - low] = theirs[r, start : start + rows].astype(f32)
            start += rows


def assemble(place, mine, theirs, splits):
    half, rows, cols = mine.shape
    vm = pl.BlockSpec(memory_space=pltpu.VMEM)
    return pl.pallas_call(
        assemble_kernel,
        out_shape=tuple(jax.ShapeDtypeStruct((2 * half, part, cols), f32) for part in splits),
        in_specs=[pl.BlockSpec(memory_space=pltpu.SMEM), vm, vm],
        out_specs=tuple(vm for _ in splits),
        compiler_params=pltpu.CompilerParams(vmem_limit_bytes=32 << 20),
        cost_estimate=took(2),
        name="assemble",
    )(place, mine, theirs)


def small_call(kernel, name, outs, *args):
    vm = pl.BlockSpec(memory_space=pltpu.VMEM)
    return pl.pallas_call(
        kernel,
        out_shape=tuple(jax.ShapeDtypeStruct(shape, kind) for shape, kind in outs),
        in_specs=[pl.BlockSpec(memory_space=pltpu.SMEM)] + [vm] * (len(args) - 1),
        out_specs=tuple(vm for _ in outs),
        compiler_params=pltpu.CompilerParams(vmem_limit_bytes=16 << 20),
        cost_estimate=took(1),
        name=name,
    )(*args)


def split_kernel(digit, first, second, keep_out, give_out):
    for q in range(keep_out.shape[0]):
        keep, give = 2 * q + digit[0], 2 * q + 1 - digit[0]
        if len(second.shape) < 3:
            keep_out[q] = first[keep].astype(f32)
            give_out[q] = first[give]
        else:
            keep_out[q] = first[keep].astype(f32) + second[keep].astype(f32)
            give_out[q] = (first[give].astype(f32) + second[give].astype(f32)).astype(bf16)


def split(digit, first, second):
    shape = (first.shape[0] // 2,) + first.shape[1:]
    second = digit[None] if second is None else second
    return small_call(split_kernel, "split", ((shape, f32), (shape, bf16)), digit, first, second)


def total_kernel(digit, first, second, *rest):
    out = rest[-1]
    total = first[...].astype(f32) + second[...].astype(f32)
    if len(rest) > 1:
        total = total + rest[0][...]
    out[...] = total.astype(out.dtype)


def total_of(digit, first, second, kind, *third):
    return small_call(total_kernel, "total", ((first.shape, kind),), digit, first, second, *third)[0]


def arrange_kernel(digit, first, second, out):
    for q in range(out.shape[0]):
        at = q ^ digit[0]
        out[q] = (first[at].astype(f32) + second[at].astype(f32)).astype(out.dtype)


def arrange(digit, first, second):
    return small_call(arrange_kernel, "arrange", ((first.shape, first.dtype),), digit, first, second)[0]


def join_kernel(digit, first, second, out):
    for q in range(first.shape[0]):
        out[2 * q] = first[q]
        out[2 * q + 1] = second[q]


def join(digit, first, second):
    shape = (2 * first.shape[0],) + first.shape[1:]
    return small_call(join_kernel, "join", ((shape, first.dtype),), digit, first, second)[0]


def make_body(dp_count):
    stages = dp_count.bit_length() - 1

    def swap(value, axis, count, bits):
        return lax.ppermute(value, axis, [(i, i ^ bits) for i in range(count)])

    swap_core = lambda value: swap(value, "tensor", 4, 1)
    swap_y = lambda value: swap(value, "tensor", 4, 2)
    swap_dp = lambda value, bits: swap(value, "dp", dp_count, bits)

    def digit_of(bit):
        if bit == -1:
            return jnp.ones((1,), jnp.int32)
        return (lax.axis_index("dp").astype(jnp.int32) >> bit & 1)[None]

    def exchange(value, bit):
        if bit == -1:
            return swap_y(value)
        return swap_core(value) if bit == -2 else swap_dp(value, 1 << bit)

    def sum_over_dp(keep, came, bits, splits=None):
        bits = list(bits)
        top = stages - 1
        doubled = bits[-1:] == [top]
        for bit in bits[: len(bits) - doubled]:
            keep, give = split(digit_of(bit), keep, came)
            came = yield give, bit
        mine = total_of(digit_of(0), keep, came, bf16)
        if doubled:
            came = yield mine, top
            mine = arrange(digit_of(top), mine, came)
        for bit in range(top - doubled, 0, -1):
            came = yield mine, bit
            mine = join(digit_of(0), mine, came)
        theirs = yield mine, 0
        place = lax.axis_index("dp").astype(jnp.int32)[None]
        parts = assemble(place, mine, theirs, splits or (keep.shape[1],))
        return [part.reshape(-1, part.shape[2]) for part in parts]

    def interleave(order, steps):
        came = {name: None for name in steps}
        results = {}
        token = None
        names = list(order) + [name for name in steps for _ in range(4 * stages)]
        for name in names:
            if name in results:
                continue
            if token is not None and came[name] is not None:
                came[name] = lax.optimization_barrier((came[name], token))[0]
            try:
                value, bit = steps[name].send(came[name])
                if token is not None and came[name] is None:
                    value = lax.optimization_barrier((value, token))[0]
                token = value
                came[name] = exchange(value, bit)
            except StopIteration as stop:
                token = results[name] = stop.value
        return results

    def body(
        tokens,
        segment_ids,
        pad_mask,
        buckets,
        projections,
        projected_bias,
        relative_table,
        mixing_weight,
        residual_biases,
        norm_gains,
        norm_shifts,
        expand_weight,
        expand_bias,
        contract_weight,
        cotangent,
    ):
        rows_here, model_width = tokens.shape
        bucket_count = relative_table.shape[0]
        width = projections.shape[2]
        spot = lax.axis_index("tensor")
        flip = spot % 2

        def after(value, ready):
            return lax.optimization_barrier((value, ready))[0]

        dp_place = lax.axis_index("dp").astype(jnp.int32)
        odd = dp_place & 1
        weight_own = projections.transpose(1, 2, 0).reshape(3 * width, model_width)
        x_other = swap_core(tokens)
        weight_y = swap_y(weight_own)
        place = jnp.stack([flip, spot // 2]).astype(jnp.int32)
        limits, key_code, seg_row, small_own = prepare(
            place, segment_ids, pad_mask, relative_table.T, projected_bias, expand_bias[None]
        )
        mixing_y = swap_y(mixing_weight)
        half_rows = contract_weight.shape[0] // 2
        half_y = swap_y(lax.dynamic_slice_in_dim(contract_weight, odd * half_rows, half_rows, 0))
        small_y = swap_y(small_own)
        bucket_row = buckets[255:1791][::-1][None]

        def forward(weight, small, x_in):
            return attend(limits, x_in, x_other, weight, small, bucket_row, key_code, seg_row)

        own_a, other_a, *saved_a = forward(weight_own, small_own, tokens)
        expand_y = swap_y(after(expand_weight, own_a))
        half_x = swap_dp(after(half_y, own_a), 1)
        recv_a = swap_core(other_a)
        own_b, other_b, *saved_b = forward(weight_y, small_y, after(tokens, (own_a, half_y)))
        mixing_core, expand_core, contract_core, small_core = [
            swap_core(value)
            for value in after((mixing_weight, expand_weight, contract_weight, small_own), own_a)
        ]
        mixing_diag, small_diag = swap_core(after(mixing_y, own_a)), swap_core(after(small_y, own_a))
        recv_b = swap_core(other_b)
        contract_y = jnp.where(
            odd == 0, jnp.concatenate([half_y, half_x]), jnp.concatenate([half_x, half_y])
        )
        contract_diag = swap_core(contract_y)
        normed_one, inverse_one, pair, hidden0, slope0, slope1, partial = first_half(
            tokens, own_a, recv_a, own_b, recv_b, mixing_weight, mixing_core, mixing_y, mixing_diag,
            residual_biases, norm_gains, norm_shifts,
            expand_weight, contract_weight, expand_core, contract_core, small_own, small_core,
        )
        pair_there = swap_core(pair)
        expand_y = after(expand_y, partial)
        expand_diag = swap_core(expand_y)
        hidden2, slope2, partial = third_slot(pair, expand_y, contract_y, small_y, partial)
        layer_out, grad_two, send, later_sums = second_half(
            normed_one, pair, partial, norm_gains, norm_shifts,
            expand_diag, contract_diag, contract_core, small_diag, slope1, cotangent,
        )
        arrived = swap_core(send)
        unit_grad0, unit_grad2, grad_one, outgoing, early = unit_back(
            send, contract_weight, contract_y, slope0, slope2,
            expand_weight, expand_core, expand_y, expand_diag,
            grad_two, normed_one, inverse_one, norm_gains, later_sums,
        )
        outgoing_there = swap_core(outgoing)
        early_there = swap_core(early)

        contract_bits = list(range(1, stages)) + [0, -1]
        contract_keep, contract_give = both_halves(
            digit_of(contract_bits[0]), dp_count, after(hidden2, outgoing), (arrived, 3),
            hidden0, (pair_there, 1), (send, 0), (arrived, 0),
        )
        contract_came = exchange(contract_give, contract_bits[0])
        expand_two = pair_grad(
            dp_count, (after(pair, contract_give), 0), (pair_there, 0), unit_grad2, (arrived, 2)
        )
        expand_across = swap_y(expand_two)
        expand_own = pair_grad(
            dp_count, (after(pair, expand_two), 0), (pair_there, 0), unit_grad0, (arrived, 1)
        )

        def backward(saved, weight, mixing_here, attended, ready, before=()):
            return attend_back(
                limits, mixing_here, after(outgoing, ready), outgoing_there, *saved, bucket_row,
                key_code, seg_row, tokens, x_other, weight, *attended, early, early_there, *before,
                pieces=dp_count, last=bool(before),
            )

        pieces_b, inputs_own, inputs_other, tail_b = backward(
            saved_b, weight_y, mixing_y, (own_b, other_b), expand_own
        )
        pieces_y = swap_y(pieces_b)
        contract_came, expand_across = after((contract_came, expand_across), pieces_b)
        contract_keep, contract_give = split(digit_of(contract_bits[1]), contract_keep, contract_came)
        contract_came = exchange(contract_give, contract_bits[1])
        expand_keep, expand_give = split(digit_of(0), expand_own, expand_across)
        expand_came = swap_dp(expand_give, 1)
        pieces_a, inputs_own, inputs_other, tail_a = backward(
            saved_a, weight_own, mixing_weight, (own_a, other_a),
            (pieces_b, contract_give, expand_give), (inputs_own, inputs_other),
        )
        pieces_y = after(pieces_y, pieces_a)
        expand_came = after(expand_came, pieces_a)
        contract_came = after(contract_came, pieces_a)

        def projection_steps():
            keep, give = split(digit_of(0), pieces_a, pieces_y)
            came = yield give, 0
            splits = (3 * width // dp_count, width // dp_count)
            return (yield from sum_over_dp(keep, came, range(1, stages), splits))

        def small_steps():
            value = tail_a + (yield tail_b, -1)
            for bit in list(range(1, stages)) + [0]:
                value = value + (yield value, bit)
            return value

        def input_steps():
            there = yield inputs_other, -2
            return total_of(digit_of(0), inputs_own, there, f32, grad_one)

        results = interleave(
            "tpecsepctcepecpcpssescps",
            {
                "t": input_steps(),
                "p": projection_steps(),
                "c": sum_over_dp(contract_keep, contract_came, contract_bits[2:]),
                "e": sum_over_dp(expand_keep, expand_came, range(1, stages)),
                "s": small_steps(),
            },
        )
        (contract_total,), (expand_total,) = results["c"], results["e"]
        projection_total, mixing_total = results["p"]
        sums = results["s"]
        tokens_grad = results["t"]

        return (
            layer_out,
            tokens_grad,
            projection_total.reshape(3, width, model_width).transpose(2, 0, 1),
            sums[NH : NH + 2, :width],
            sums[:NH, :bucket_count].T,
            mixing_total,
            sums[5:7],
            sums[7:9],
            sums[9:11],
            expand_total,
            sums[11],
            contract_total,
        )

    return body


def solution(mesh):
    return jax.shard_map(
        make_body(mesh.shape["dp"]),
        mesh=mesh,
        in_specs=(
            P(("dp", "tensor"), None),
            P("dp", None),
            P("dp", None),
            P(),
            P(None, None, "tensor"),
            P(None, "tensor"),
            P(None, "tensor"),
            P("tensor", None),
            P(),
            P(),
            P(),
            P(None, "tensor"),
            P("tensor"),
            P("tensor", None),
            P(("dp", "tensor"), None),
        ),
        out_specs=(
            P(("dp", "tensor"), None),
            P(("dp", "tensor"), None),
            P(None, None, "tensor"),
            P(None, "tensor"),
            P(None, "tensor"),
            P("tensor", None),
            P(),
            P(),
            P(),
            P(None, "tensor"),
            P("tensor"),
            P("tensor", None),
        ),
        check_vma=False,
    )
```

```python
import functools
import jax
import jax.numpy as jnp
from jax import lax
from jax.experimental import pallas as pl
from jax.experimental.pallas import tpu as pltpu
from jax.sharding import PartitionSpec as P

big_negative = -1e30
KB = 128
QT = 256
HALF = 512
SEQ = 1024
HW = 64
NH = 3
TILES = 11
SPAN = 1536
f32 = jnp.float32
bf16 = jnp.bfloat16
dot32 = functools.partial(lax.dot_general, preferred_element_type=f32)
NN = (((1,), (0,)), ((), ()))
NT = (((1,), (1,)), ((), ()))


def took(micros):
    return pl.CostEstimate(flops=int(micros * 8e5), transcendentals=0, bytes_accessed=int(micros * 3e3))


def in_hbm(value):
    return pltpu.with_memory_space_constraint(value, pltpu.HBM)


def three_parts(value):
    high = value.astype(bf16)
    rest = value - high.astype(f32)
    middle = rest.astype(bf16)
    low = (rest - middle.astype(f32)).astype(bf16)
    return high, middle, low


def bucket_grid(bucket_ref, count):
    rows = lax.broadcasted_iota(jnp.int32, (count, SPAN), 0)
    return (rows == bucket_ref[...]).astype(bf16)


def tile_mask(key_code, seg_row, difference, shift):
    codes = jnp.concatenate([key_code, key_code], axis=1)
    return (codes == seg_row) | (difference == shift)


def prepare_kernel(place, seg_scalar, segments, padding, table, pair_bias, unit_bias,
                   limits, key_code, seg_row, small):
    flip = place[0]
    chip = place[1]
    segs = segments[pl.ds(chip, 1), :]
    code = jnp.where(padding[pl.ds(chip, 1), :] == 1, segs, -1).astype(f32)
    wide = segs.astype(f32)
    for b in range(SEQ // QT):
        seg_row[b] = wide[:, b * QT : (b + 1) * QT]
        first = seg_scalar[chip, b * QT]
        last = seg_scalar[chip, b * QT + QT - 1]
        limits[b] = jnp.sum((segs < first).astype(f32)).astype(jnp.int32) // KB
        limits[4 + b] = (jnp.sum((segs <= last).astype(f32)).astype(jnp.int32) + KB - 1) // KB
    limits[8] = flip
    for b in range(SEQ // KB):
        key_code[b] = jnp.broadcast_to(code[:, b * KB : (b + 1) * KB], (KB, KB)).T
    small[...] = jnp.zeros(small.shape, f32)
    small[0:NH, : table.shape[1]] = table[...]
    small[NH : NH + 2, : pair_bias.shape[1]] = pair_bias[...]
    small[NH + 2 : NH + 3, : unit_bias.shape[1]] = unit_bias[...]


def prepare(place, segment_ids, pad_mask, table, pair_bias, unit_bias):
    vm = pl.BlockSpec(memory_space=pltpu.VMEM)
    sm = pl.BlockSpec(memory_space=pltpu.SMEM)
    return pl.pallas_call(
        prepare_kernel,
        out_shape=(
            jax.ShapeDtypeStruct((9,), jnp.int32),
            jax.ShapeDtypeStruct((SEQ // KB, KB, KB), f32),
            jax.ShapeDtypeStruct((SEQ // QT, 1, QT), f32),
            jax.ShapeDtypeStruct((8, unit_bias.shape[1]), f32),
        ),
        in_specs=[sm, sm, vm, vm, vm, vm, vm],
        out_specs=(sm, vm, vm, vm),
        cost_estimate=took(2),
        name="prepare",
    )(place, segment_ids, segment_ids, pad_mask, table, pair_bias, unit_bias)


def forward_kernel(limits, x_own, x_other, weight, small, buckets, key_code, seg_row,
                   own_out, other_out, full_far, totals_far, heads_far, turned_far, tiles_far,
                   out_full, totals, heads_out, turned_out, tiles, best, total, gathered, done):
    flip = limits[8]

    def send(count, *pairs):
        copies = [
            pltpu.make_async_copy(near, far, done.at[count + i]) for i, (near, far) in enumerate(pairs)
        ]
        for copy in copies:
            copy.start()
        return copies

    width = NH * HW
    columns = small[:, :256].T
    for half, x_ref in enumerate((x_own, x_other)):
        plain = dot32(x_ref[...], weight[...], NT)
        across = dot32(weight[...], x_ref[...], NT)
        rows = pl.ds(half * HALF, HALF)
        for c in range(3):
            part, turned = plain[:, c * width : (c + 1) * width], across[c * width : (c + 1) * width]
            if c != 1:
                r = NH + c // 2
                part = part + small[r : r + 1, :width]
                turned = turned + columns[:width, r : r + 1]
            part, turned = part.astype(bf16), turned.astype(bf16)
            if c == 0:
                part, turned = part * 0.125, turned * 0.125
            for h in range(NH):
                heads_out[c * NH + h, rows, :] = part[:, h * HW : (h + 1) * HW]
            for k in range(HALF // KB):
                turned_out[half * (HALF // KB) + k, c * width : (c + 1) * width, :] = turned[
                    :, k * KB : (k + 1) * KB
                ]
    hot = bucket_grid(buckets, 256)
    line = sum(dot32(part, hot, NN) for part in three_parts(small[:, :256]))
    for h in range(NH):
        for u in range(TILES):
            start = 640 - 128 * (u - 5)
            spread = jnp.broadcast_to(line[h : h + 1, start : start + 256], (KB, 256))
            tiles[h, u] = pltpu.roll(spread, 129, 1, stride=1, stride_axis=0)[:, :KB]
    copies = send(0, (heads_out, heads_far), (turned_out, turned_far), (tiles, tiles_far))
    difference = lax.broadcasted_iota(jnp.int32, (KB, QT), 1) - lax.broadcasted_iota(
        jnp.int32, (KB, QT), 0
    )

    def query_step(block, carry):
        place = block ^ (flip * 2)
        best[...] = jnp.full(best.shape, big_negative, f32)
        total[...] = jnp.zeros(total.shape, f32)
        gathered[...] = jnp.zeros(gathered.shape, f32)
        segs = seg_row[place]

        def key_step(key_place, carry):
            key_block = key_place ^ (flip * 4)
            gap = key_place - 2 * place
            allowed = tile_mask(key_code[key_place], segs, difference, gap * KB)
            queries = [
                jnp.concatenate([turned_out[2 * block + i, h * HW : (h + 1) * HW, :] for i in range(2)], axis=1)
                for h in range(NH)
            ]
            k_rows = pl.ds(key_block * KB, KB)
            scores = [dot32(heads_out[NH + h, k_rows, :], queries[h], NN) for h in range(NH)]
            lows, shrinks = [], []
            for h in range(NH):
                bias = jnp.concatenate([tiles[h, gap + 5], tiles[h, gap + 4]], axis=1)
                value = jnp.where(allowed, scores[h] + bias, big_negative)
                old = best[h]
                new = jnp.maximum(old, jnp.max(value, axis=0, keepdims=True))
                value = jnp.exp(value - new)
                shrink = jnp.exp(old - new)
                best[h] = new
                total[h] = shrink * total[h] + jnp.sum(value, axis=0, keepdims=True)
                lows.append(value.astype(bf16))
                shrinks.append(shrink)
            for h in range(NH):
                turned_v = turned_out[key_block, (2 * NH + h) * HW : (2 * NH + h + 1) * HW, :]
                gathered[h] = gathered[h] * shrinks[h] + dot32(turned_v, lows[h], NN)
            return carry

        lax.fori_loop(limits[place], limits[4 + place], key_step, 0)
        for h in range(NH):
            result = gathered[h] / total[h]
            out_full[block, h * HW : (h + 1) * HW, :] = result
            totals[block, h : h + 1, :] = best[h] + jnp.log(total[h])
        return carry

    lax.fori_loop(0, SEQ // QT, query_step, 0)
    copies = copies + send(3, (out_full, full_far), (totals, totals_far))
    for c in range(2):
        own_out[:, c * QT : (c + 1) * QT] = out_full[c].astype(bf16)
        other_out[:, c * QT : (c + 1) * QT] = out_full[2 + c].astype(bf16)
    for copy in copies:
        copy.wait()


def saved_shapes():
    return (
        ((SEQ // QT, NH * HW, QT), f32),
        ((SEQ // QT, 8, QT), f32),
        ((3 * NH, SEQ, HW), bf16),
        ((SEQ // KB, 3 * NH * HW, KB), bf16),
        ((NH, TILES, KB, KB), f32),
    )


def attend(limits, x_own, x_other, weight, small, buckets, key_code, seg_row):
    vm = pl.BlockSpec(memory_space=pltpu.VMEM)
    return pl.pallas_call(
        forward_kernel,
        out_shape=(
            jax.ShapeDtypeStruct((NH * HW, HALF), bf16),
            jax.ShapeDtypeStruct((NH * HW, HALF), bf16),
        )
        + tuple(pltpu.HBM(shape, kind) for shape, kind in saved_shapes()),
        in_specs=[pl.BlockSpec(memory_space=pltpu.SMEM)] + [vm] * 7,
        out_specs=(vm, vm) + (pl.BlockSpec(memory_space=pltpu.HBM),) * 5,
        scratch_shapes=[pltpu.VMEM(shape, kind) for shape, kind in saved_shapes()]
        + [
            pltpu.VMEM((NH, 1, QT), f32),
            pltpu.VMEM((NH, 1, QT), f32),
            pltpu.VMEM((NH, HW, QT), f32),
            pltpu.SemaphoreType.DMA((5,)),
        ],
        compiler_params=pltpu.CompilerParams(vmem_limit_bytes=20 << 20),
        cost_estimate=took(20),
        name="attend",
    )(limits, x_own, x_other, weight, small, buckets, key_code, seg_row)


def backward_kernel(limits, mixing, outgoing_own, outgoing_other, full_far, totals_far, heads_far,
                    turned_far, tiles_far, buckets, key_code, seg_row, x_own_far, x_other_far, weight_far, attended_own,
                    attended_other, early, early_there, *rest, last):
    if last:
        before_own_far, before_other_far, *rest = rest
    (pieces_out, own_out, other_out, tail_out,
     out_full, totals, heads, turned, tiles,
     turned_grad, plain_grad, row_dots, query_acc, query_all, key_acc, value_acc, tile_acc,
     grads, done, *rest) = rest
    flip = limits[8]
    fetched = [
        pltpu.make_async_copy(far, near, done.at[i])
        for i, (far, near) in enumerate(
            ((full_far, out_full), (totals_far, totals), (heads_far, heads), (turned_far, turned),
             (tiles_far, tiles))
        )
    ]
    x_own, x_other, weight, *rest = rest
    pairs = [(x_own_far, x_own), (x_other_far, x_other), (weight_far, weight)]
    if last:
        before_own, before_other = rest
        pairs += [(before_own_far, before_own), (before_other_far, before_other)]
    late = [pltpu.make_async_copy(far, near, done.at[5 + i]) for i, (far, near) in enumerate(pairs)]
    for copy in fetched:
        copy.start()
    key_acc[...] = jnp.zeros(key_acc.shape, f32)
    value_acc[...] = jnp.zeros(value_acc.shape, f32)
    tile_acc[...] = jnp.zeros(tile_acc.shape, f32)
    fetched[0].wait()
    for half, ref in enumerate((outgoing_own, outgoing_other)):
        across = dot32(mixing[...], ref[...], NT).astype(bf16)
        for c in range(2):
            block = 2 * half + c
            piece = across[:, c * QT : (c + 1) * QT]
            turned_grad[block] = piece
            wide = piece.astype(f32)
            product = wide * out_full[block]
            for h in range(NH):
                rows = slice(h * HW, (h + 1) * HW)
                row_dots[block, h : h + 1, :] = jnp.sum(product[rows], axis=0, keepdims=True)
                plain_grad[h, block * QT : (block + 1) * QT, :] = wide[rows].T.astype(bf16)
    for copy in fetched[1:]:
        copy.wait()
    for copy in late:
        copy.start()
    difference = lax.broadcasted_iota(jnp.int32, (KB, QT), 1) - lax.broadcasted_iota(
        jnp.int32, (KB, QT), 0
    )

    def query_step(block, carry):
        place = block ^ (flip * 2)
        query_acc[...] = jnp.zeros(query_acc.shape, f32)
        segs = seg_row[place]
        q_rows = pl.ds(block * QT, QT)

        def key_step(key_place, carry):
            key_block = key_place ^ (flip * 4)
            gap = key_place - 2 * place
            k_rows = pl.ds(key_block * KB, KB)
            allowed = tile_mask(key_code[key_place], segs, difference, gap * KB)
            queries = [
                jnp.concatenate([turned[2 * block + i, h * HW : (h + 1) * HW, :] for i in range(2)], axis=1)
                for h in range(NH)
            ]
            scores = [dot32(heads[NH + h, k_rows, :], queries[h], NN) for h in range(NH)]
            chance_grads = [
                dot32(heads[2 * NH + h, k_rows, :], turned_grad[block, h * HW : (h + 1) * HW, :], NN)
                for h in range(NH)
            ]
            chances, score_lows = [], []
            for h in range(NH):
                bias = jnp.concatenate([tiles[h, gap + 5], tiles[h, gap + 4]], axis=1)
                value = jnp.where(allowed, scores[h] + bias, big_negative)
                chance = jnp.exp(value - totals[block, h : h + 1, :])
                score_grad = chance * (chance_grads[h] - row_dots[block, h : h + 1, :])
                tile_acc[h, gap + 5] += score_grad[:, :KB]
                tile_acc[h, gap + 4] += score_grad[:, KB:]
                chances.append(chance.astype(bf16))
                score_lows.append(score_grad.astype(bf16))
            for h in range(NH):
                value_acc[h, k_rows, :] += dot32(chances[h], plain_grad[h, q_rows, :], NN)
            for h in range(NH):
                key_acc[h, k_rows, :] += dot32(score_lows[h], heads[h, q_rows, :], NN)
            for h in range(NH):
                turned_k = turned[key_block, (NH + h) * HW : (NH + h + 1) * HW, :]
                query_acc[h] += dot32(turned_k, score_lows[h], NN)
            return carry

        lax.fori_loop(limits[place], limits[4 + place], key_step, 0)
        for h in range(NH):
            query_all[h, q_rows, :] = (query_acc[h] * 0.125).T
        return carry

    lax.fori_loop(0, SEQ // QT, query_step, 0)
    width = NH * HW
    for g, acc in ((0, query_all), (1, key_acc), (2, value_acc)):
        for h in range(NH):
            at = (g * NH + h) * HW
            grads[:, at : at + HW] = acc[h].astype(bf16)
    tail_out[...] = jnp.zeros(tail_out.shape, f32)
    tail_out[5:11, :] = early[5:11, :] + early_there[5:11, :]
    r = 11 if last else 12
    tail_out[11:12, :] = early[r : r + 1, :] + early_there[r + 2 : r + 3, :]
    for r in range(2):
        sums = jnp.sum(grads[:, 2 * r * width : (2 * r + 1) * width].astype(f32), axis=0, keepdims=True)
        tail_out[NH + r : NH + r + 1, :width] = sums
    for copy in late:
        copy.wait()
    total = dot32(grads[:HALF, :], x_own[...], TN) + dot32(grads[HALF:, :], x_other[...], TN)
    mixed = dot32(attended_own[...], outgoing_own[...], NN) + dot32(
        attended_other[...], outgoing_other[...], NN
    )
    pieces = pieces_out.shape[0]
    first, second = total.shape[0] // pieces, mixed.shape[0] // pieces
    for p in range(pieces):
        pieces_out[p, :first] = total[p * first : (p + 1) * first].astype(bf16)
        pieces_out[p, first:] = mixed[p * second : (p + 1) * second].astype(bf16)
    own = dot32(grads[:HALF, :], weight[...], NN)
    other = dot32(grads[HALF:, :], weight[...], NN)
    if last:
        own = own + before_own[...]
        other = other + before_other[...]
    own_out[...] = own
    other_out[...] = other.astype(other_out.dtype)
    hot = bucket_grid(buckets, 256)
    lines = []
    for h in range(NH):
        spans = [jnp.zeros((1, KB), f32) for _ in range(SPAN // KB)]
        for u in range(TILES):
            wide = jnp.concatenate([tile_acc[h, u], jnp.zeros((KB, KB), f32)], axis=1)
            count = KB // 2
            while count:
                wide = wide[count:] + pltpu.roll(wide[:count], count, 1)
                count //= 2
            at = (640 - 128 * (u - 5)) // KB
            spans[at] = spans[at] + wide[:, :KB]
            spans[at + 1] = spans[at + 1] + wide[:, KB:]
        lines.append(jnp.concatenate(spans, axis=1))
    lines.append(jnp.zeros((8 - NH, SPAN), f32))
    line = jnp.concatenate(lines, axis=0)
    tail_out[:NH, :256] = sum(dot32(part, hot, NT) for part in three_parts(line))[:NH]


def attend_back(limits, *args, pieces, last):
    vm = pl.BlockSpec(memory_space=pltpu.VMEM)
    wide, model = args[13].shape
    rows = args[1].shape[0]
    piece = (wide + wide // 3) // pieces
    return pl.pallas_call(
        functools.partial(backward_kernel, last=last),
        out_shape=(
            jax.ShapeDtypeStruct((pieces, piece, model), bf16),
            (jax.ShapeDtypeStruct if last else pltpu.HBM)((rows, model), f32),
            (jax.ShapeDtypeStruct if last else pltpu.HBM)((rows, model), bf16 if last else f32),
            jax.ShapeDtypeStruct((16, model), f32),
        ),
        in_specs=[pl.BlockSpec(memory_space=pltpu.SMEM)] + [vm] * 3
        + [pl.BlockSpec(memory_space=pltpu.HBM)] * 5 + [vm] * 3
        + [pl.BlockSpec(memory_space=pltpu.HBM)] * 3 + [vm] * 4
        + [pl.BlockSpec(memory_space=pltpu.HBM)] * (2 if last else 0),
        out_specs=tuple([vm] * 4),
        scratch_shapes=[pltpu.VMEM(shape, kind) for shape, kind in saved_shapes()]
        + [
            pltpu.VMEM((SEQ // QT, NH * HW, QT), bf16),
            pltpu.VMEM((NH, SEQ, HW), bf16),
            pltpu.VMEM((SEQ // QT, 8, QT), f32),
            pltpu.VMEM((NH, HW, QT), f32),
            pltpu.VMEM((NH, SEQ, HW), f32),
            pltpu.VMEM((NH, SEQ, HW), f32),
            pltpu.VMEM((NH, SEQ, HW), f32),
            pltpu.VMEM((NH, TILES, KB, KB), f32),
            pltpu.VMEM((SEQ, 3 * NH * HW), bf16),
            pltpu.SemaphoreType.DMA((10,)),
            pltpu.VMEM((rows, model), bf16),
            pltpu.VMEM((rows, model), bf16),
            pltpu.VMEM((wide, model), bf16),
        ]
        + [pltpu.VMEM((rows, model), f32)] * (2 if last else 0),
        compiler_params=pltpu.CompilerParams(vmem_limit_bytes=36 << 20),
        cost_estimate=took(25),
        name="attend_back",
    )(limits, *args[:3], *[in_hbm(arg) for arg in args[3:8]], *args[8:11],
      *[in_hbm(arg) for arg in args[11:14]], *args[14:18], *[in_hbm(arg) for arg in args[18:]])


ROWS = 128
TN = (((0,), (0,)), ((), ()))
norm_eps = 1e-05


def whole(count):
    return [pl.BlockSpec(memory_space=pltpu.VMEM)] * count


def normalise(value):
    centered = value - jnp.mean(value, axis=-1, keepdims=True)
    inverse = lax.rsqrt(jnp.mean(centered * centered, axis=-1, keepdims=True) + norm_eps)
    return centered * inverse, inverse


def normalise_back(scaled, normed, inverse):
    first_mean = jnp.mean(scaled, axis=-1, keepdims=True)
    second_mean = jnp.mean(scaled * normed, axis=-1, keepdims=True)
    return inverse * (scaled - first_mean - normed * second_mean)


def gelu_parts(value):
    cumulative = 0.5 * (1.0 + lax.erf(value * 0.7071067811865476))
    density = jnp.exp(-0.5 * value * value) * 0.3989422804014327
    return (value * cumulative).astype(bf16), cumulative + value * density


def add_column(ref, at, value):
    ref[at] += jnp.sum(value.reshape(-1, 8, value.shape[1]), axis=0)


def first_half_kernel(tokens, own_a, recv_a, own_b, recv_b, mix0, mix1, mix2, mix3, biases, gains,
                      shifts, expand0, contract0, expand1, contract1, small0, small1,
                      normed_out, inverse_out, pair_out, hidden0_out, slope0_out, slope1_out, partial_out):
    def step(r, carry):
        at = pl.multiple_of(r * ROWS, ROWS)
        rows = pl.ds(at, ROWS)
        branch = tokens[rows, :].astype(f32) + biases[0:1, :]
        for attended, mixing in ((own_a, mix0), (recv_a, mix1), (own_b, mix2), (recv_b, mix3)):
            branch = branch + dot32(attended[:, rows], mixing[...], TN)
        normed, inverse = normalise(branch)
        normed_out[rows, :] = normed
        inverse_out[rows, :] = inverse
        low = (normed * gains[0:1, :] + shifts[0:1, :]).astype(bf16)
        pair_out[0, rows, :] = low
        partial = biases[1:2, :]
        for s, expand, contract, small in ((0, expand0, contract0, small0), (1, expand1, contract1, small1)):
            hidden, slope = gelu_parts(dot32(low, expand[...], NN) + small[5:6, :])
            if s == 0:
                hidden0_out[rows, :] = hidden
                slope0_out[rows, :] = slope
            else:
                pair_out[1, rows, :] = hidden
                slope1_out[rows, :] = slope
            partial = partial + dot32(hidden, contract[...], NN)
        partial_out[rows, :] = partial
        return carry

    lax.fori_loop(0, tokens.shape[0] // ROWS, step, 0)


def first_half(*args):
    rows, cols = args[0].shape
    wide = jax.ShapeDtypeStruct((rows, cols), f32)
    return pl.pallas_call(
        first_half_kernel,
        out_shape=(wide, jax.ShapeDtypeStruct((rows, 1), f32),
                   jax.ShapeDtypeStruct((2, rows, cols), bf16),
                   jax.ShapeDtypeStruct((rows, cols), bf16), wide, wide, wide),
        in_specs=whole(len(args)),
        out_specs=tuple(whole(7)),
        compiler_params=pltpu.CompilerParams(vmem_limit_bytes=16 << 20),
        cost_estimate=took(12),
        name="first_half",
    )(*args)


def third_slot_kernel(pair, expand, contract, small, partial_in, hidden_out, slope_out, partial_out):
    def step(r, carry):
        rows = pl.ds(pl.multiple_of(r * ROWS, ROWS), ROWS)
        hidden, slope = gelu_parts(dot32(pair[0, rows, :], expand[...], NN) + small[5:6, :])
        hidden_out[rows, :] = hidden
        slope_out[rows, :] = slope
        partial_out[rows, :] = partial_in[rows, :] + dot32(hidden, contract[...], NN)
        return carry

    lax.fori_loop(0, partial_in.shape[0] // ROWS, step, 0)


def third_slot(*args):
    rows, cols = args[4].shape
    wide = jax.ShapeDtypeStruct((rows, cols), f32)
    return pl.pallas_call(
        third_slot_kernel,
        out_shape=(jax.ShapeDtypeStruct((rows, cols), bf16), wide, wide),
        in_specs=whole(5),
        out_specs=tuple(whole(3)),
        compiler_params=pltpu.CompilerParams(vmem_limit_bytes=16 << 20),
        cost_estimate=took(5),
        name="third_slot",
    )(*args)


def second_half_kernel(normed_in, pair, partial_in, gains, shifts, expand3, contract3, contract1,
                       small, slope1, cotangent,
                       layer_out, grad_two_out, send_out, sums_out):
    sums_out[...] = jnp.zeros(sums_out.shape, f32)

    def step(r, carry):
        rows = pl.ds(pl.multiple_of(r * ROWS, ROWS), ROWS)
        low = pair[0, rows, :]
        total = normed_in[rows, :] * gains[0:1, :] + shifts[0:1, :] + partial_in[rows, :]
        hidden3, slope3 = gelu_parts(dot32(low, expand3[...], NN) + small[5:6, :])
        send_out[3, rows, :] = hidden3
        total = total + dot32(hidden3, contract3[...], NN)
        normed, inverse = normalise(total)
        layer_out[rows, :] = (normed * gains[1:2, :] + shifts[1:2, :]).astype(bf16)
        outer = cotangent[rows, :].astype(f32)
        grad_two = normalise_back(outer * gains[1:2, :], normed, inverse)
        grad_two_out[rows, :] = grad_two
        upstream = grad_two.astype(bf16)
        send_out[0, rows, :] = upstream
        add_column(sums_out, 0, grad_two)
        add_column(sums_out, 1, outer * normed)
        add_column(sums_out, 2, outer)
        for at, contract, slope in ((1, contract1, slope1[rows, :]), (2, contract3, slope3)):
            unit_grad = (dot32(upstream, contract[...], NT) * slope).astype(bf16)
            send_out[at, rows, :] = unit_grad
            add_column(sums_out, 2 + at, unit_grad.astype(f32))
        return carry

    lax.fori_loop(0, normed_in.shape[0] // ROWS, step, 0)


def second_half(*args):
    rows, cols = args[0].shape
    wide = jax.ShapeDtypeStruct((rows, cols), f32)
    low = jax.ShapeDtypeStruct((rows, cols), bf16)
    return pl.pallas_call(
        second_half_kernel,
        out_shape=(low, wide, jax.ShapeDtypeStruct((4, rows, cols), bf16),
                   jax.ShapeDtypeStruct((5, 8, cols), f32)),
        in_specs=whole(len(args)),
        out_specs=tuple(whole(4)),
        compiler_params=pltpu.CompilerParams(vmem_limit_bytes=16 << 20),
        cost_estimate=took(15),
        name="second_half",
    )(*args)


def unit_back_kernel(send, contract0, contract2, slope0, slope2, expand0, expand1, expand2, expand3,
                     grad_two, normed_in, inverse_in, gains, later,
                     grad0_out, grad2_out, grad_one_out, outgoing_out, rows_out, sums_out):
    sums_out[...] = jnp.zeros(sums_out.shape, f32)

    def step(r, carry):
        rows = pl.ds(pl.multiple_of(r * ROWS, ROWS), ROWS)
        upstream = send[0, rows, :]
        total = grad_two[rows, :]
        total = total + dot32(send[1, rows, :], expand1[...], NT)
        total = total + dot32(send[2, rows, :], expand3[...], NT)
        for at, contract, slope, expand, out in ((3, contract0, slope0, expand0, grad0_out),
                                                 (4, contract2, slope2, expand2, grad2_out)):
            unit_grad = (dot32(upstream, contract[...], NT) * slope[rows, :]).astype(bf16)
            out[rows, :] = unit_grad
            add_column(sums_out, at, unit_grad.astype(f32))
            total = total + dot32(unit_grad, expand[...], NT)
        normed = normed_in[rows, :]
        grad_one = normalise_back(total * gains[0:1, :], normed, inverse_in[rows, :])
        grad_one_out[rows, :] = grad_one
        outgoing_out[rows, :] = grad_one.astype(bf16)
        add_column(sums_out, 0, grad_one)
        add_column(sums_out, 1, total * normed)
        add_column(sums_out, 2, total)
        return carry

    lax.fori_loop(0, grad_two.shape[0] // ROWS, step, 0)
    rows_out[...] = jnp.zeros(rows_out.shape, f32)
    order = (sums_out[0], later[0], sums_out[1], later[1], sums_out[2], later[2],
             sums_out[3], sums_out[4], later[3], later[4])
    for r, value in enumerate(order):
        rows_out[5 + r : 6 + r, :] = jnp.sum(value, axis=0, keepdims=True)


def unit_back(*args):
    rows, cols = args[9].shape
    low = jax.ShapeDtypeStruct((rows, cols), bf16)
    return pl.pallas_call(
        unit_back_kernel,
        out_shape=(low, low, jax.ShapeDtypeStruct((rows, cols), f32), low,
                   jax.ShapeDtypeStruct((16, cols), f32)),
        in_specs=whole(len(args)),
        out_specs=tuple(whole(5)),
        scratch_shapes=[pltpu.VMEM((5, 8, cols), f32)],
        compiler_params=pltpu.CompilerParams(vmem_limit_bytes=16 << 20),
        cost_estimate=took(17),
        name="unit_back",
    )(*args)


def pair_grad_kernel(left, left_there, right, right_there, out):
    total = dot32(left[...], right[...], TN) + dot32(left_there[...], right_there[...], TN)
    rows = out.shape[1]
    for p in range(out.shape[0]):
        out[p] = total[p * rows : (p + 1) * rows].astype(bf16)


def both_halves_kernel(digit, two, two_there, own, own_there, right, right_there, keep_out, give_out):
    half, rows, _ = keep_out.shape
    half //= 2
    bits = half.bit_length()
    for slot, (left, left_there) in enumerate(((two, two_there), (own, own_there))):
        total = dot32(left[...], right[...], TN) + dot32(left_there[...], right_there[...], TN)
        for q in range(half):
            first = q if bits < 2 else (q >> bits - 2) | sum(
                (q >> i & 1) << i + 2 for i in range(bits - 2)
            )
            step = 1 if bits < 2 else 2
            low = total[first * rows : (first + 1) * rows]
            high = total[(first + step) * rows : (first + step + 1) * rows]
            keep_out[slot * half + q] = jnp.where(digit[0] == 0, low, high)
            give_out[slot * half + q] = jnp.where(digit[0] == 0, high, low).astype(bf16)


def indexed(operand):
    array, index = operand if isinstance(operand, tuple) else (operand[None], 0)
    return array, pl.BlockSpec((None,) + array.shape[1:], lambda i, index=index: (index, 0, 0))


def both_halves(digit, pieces, *operands):
    arrays, specs = zip(*[indexed(operand) for operand in operands])
    rows, cols = arrays[0].shape[2] // pieces, arrays[4].shape[2]
    return pl.pallas_call(
        both_halves_kernel,
        out_shape=tuple(jax.ShapeDtypeStruct((pieces, rows, cols), kind) for kind in (f32, bf16)),
        grid=(1,),
        in_specs=[pl.BlockSpec(memory_space=pltpu.SMEM)] + list(specs),
        out_specs=tuple(pl.BlockSpec((pieces, rows, cols), lambda i: (0, 0, 0)) for _ in range(2)),
        compiler_params=pltpu.CompilerParams(vmem_limit_bytes=14 << 20),
        cost_estimate=took(4),
        name="both_halves",
    )(digit, *arrays)


def pair_grad(pieces, *operands):
    arrays, specs = zip(*[indexed(operand) for operand in operands])
    rows, cols = arrays[0].shape[2] // pieces, arrays[2].shape[2]
    return pl.pallas_call(
        pair_grad_kernel,
        out_shape=jax.ShapeDtypeStruct((pieces, rows, cols), bf16),
        grid=(1,),
        in_specs=list(specs),
        out_specs=pl.BlockSpec((pieces, rows, cols), lambda i: (0, 0, 0)),
        compiler_params=pltpu.CompilerParams(vmem_limit_bytes=16 << 20),
        cost_estimate=took(4),
        name="pair_grad",
    )(*arrays)


def assemble_kernel(place, mine, theirs, *outs):
    low = place[0] & 1
    high = place[0] >> 1
    for r in range(mine.shape[0]):
        at = (r ^ high) * 2
        start = 0
        for out in outs:
            rows = out.shape[1]
            out[at + low] = mine[r, start : start + rows].astype(f32)
            out[at + 1 - low] = theirs[r, start : start + rows].astype(f32)
            start += rows


def assemble(place, mine, theirs, splits):
    half, rows, cols = mine.shape
    vm = pl.BlockSpec(memory_space=pltpu.VMEM)
    return pl.pallas_call(
        assemble_kernel,
        out_shape=tuple(jax.ShapeDtypeStruct((2 * half, part, cols), f32) for part in splits),
        in_specs=[pl.BlockSpec(memory_space=pltpu.SMEM), vm, vm],
        out_specs=tuple(vm for _ in splits),
        compiler_params=pltpu.CompilerParams(vmem_limit_bytes=32 << 20),
        cost_estimate=took(2),
        name="assemble",
    )(place, mine, theirs)


def small_call(kernel, name, outs, *args):
    vm = pl.BlockSpec(memory_space=pltpu.VMEM)
    return pl.pallas_call(
        kernel,
        out_shape=tuple(jax.ShapeDtypeStruct(shape, kind) for shape, kind in outs),
        in_specs=[pl.BlockSpec(memory_space=pltpu.SMEM)] + [vm] * (len(args) - 1),
        out_specs=tuple(vm for _ in outs),
        compiler_params=pltpu.CompilerParams(vmem_limit_bytes=16 << 20),
        cost_estimate=took(1),
        name=name,
    )(*args)


def split_kernel(digit, first, second, keep_out, give_out):
    for q in range(keep_out.shape[0]):
        keep, give = 2 * q + digit[0], 2 * q + 1 - digit[0]
        if len(second.shape) < 3:
            keep_out[q] = first[keep].astype(f32)
            give_out[q] = first[give]
        else:
            keep_out[q] = first[keep].astype(f32) + second[keep].astype(f32)
            give_out[q] = (first[give].astype(f32) + second[give].astype(f32)).astype(bf16)


def split(digit, first, second):
    shape = (first.shape[0] // 2,) + first.shape[1:]
    second = digit[None] if second is None else second
    return small_call(split_kernel, "split", ((shape, f32), (shape, bf16)), digit, first, second)


def total_kernel(digit, first, second, *rest):
    out = rest[-1]
    total = first[...].astype(f32) + second[...].astype(f32)
    if len(rest) > 1:
        total = total + rest[0][...]
    out[...] = total.astype(out.dtype)


def total_of(digit, first, second, kind, *third):
    return small_call(total_kernel, "total", ((first.shape, kind),), digit, first, second, *third)[0]


def arrange_kernel(digit, first, second, out):
    for q in range(out.shape[0]):
        at = q ^ digit[0]
        out[q] = (first[at].astype(f32) + second[at].astype(f32)).astype(out.dtype)


def arrange(digit, first, second):
    return small_call(arrange_kernel, "arrange", ((first.shape, first.dtype),), digit, first, second)[0]


def join_kernel(digit, first, second, out):
    for q in range(first.shape[0]):
        out[2 * q] = first[q]
        out[2 * q + 1] = second[q]


def join(digit, first, second):
    shape = (2 * first.shape[0],) + first.shape[1:]
    return small_call(join_kernel, "join", ((shape, first.dtype),), digit, first, second)[0]


def make_body(dp_count):
    stages = dp_count.bit_length() - 1

    def swap(value, axis, count, bits):
        return lax.ppermute(value, axis, [(i, i ^ bits) for i in range(count)])

    swap_core = lambda value: swap(value, "tensor", 4, 1)
    swap_y = lambda value: swap(value, "tensor", 4, 2)
    swap_dp = lambda value, bits: swap(value, "dp", dp_count, bits)

    def digit_of(bit):
        if bit == -1:
            return jnp.ones((1,), jnp.int32)
        return (lax.axis_index("dp").astype(jnp.int32) >> bit & 1)[None]

    def exchange(value, bit):
        if bit == -1:
            return swap_y(value)
        return swap_core(value) if bit == -2 else swap_dp(value, 1 << bit)

    def sum_over_dp(keep, came, bits, splits=None):
        bits = list(bits)
        top = stages - 1
        doubled = bits[-1:] == [top]
        for bit in bits[: len(bits) - doubled]:
            keep, give = split(digit_of(bit), keep, came)
            came = yield give, bit
        mine = total_of(digit_of(0), keep, came, bf16)
        if doubled:
            came = yield mine, top
            mine = arrange(digit_of(top), mine, came)
        for bit in range(top - doubled, 0, -1):
            came = yield mine, bit
            mine = join(digit_of(0), mine, came)
        theirs = yield mine, 0
        place = lax.axis_index("dp").astype(jnp.int32)[None]
        parts = assemble(place, mine, theirs, splits or (keep.shape[1],))
        return [part.reshape(-1, part.shape[2]) for part in parts]

    def interleave(order, steps):
        came = {name: None for name in steps}
        results = {}
        token = None
        names = list(order) + [name for name in steps for _ in range(4 * stages)]
        for name in names:
            if name in results:
                continue
            if token is not None and came[name] is not None:
                came[name] = lax.optimization_barrier((came[name], token))[0]
            try:
                value, bit = steps[name].send(came[name])
                if token is not None and came[name] is None:
                    value = lax.optimization_barrier((value, token))[0]
                token = value
                came[name] = exchange(value, bit)
            except StopIteration as stop:
                token = results[name] = stop.value
        return results

    def body(
        tokens,
        segment_ids,
        pad_mask,
        buckets,
        projections,
        projected_bias,
        relative_table,
        mixing_weight,
        residual_biases,
        norm_gains,
        norm_shifts,
        expand_weight,
        expand_bias,
        contract_weight,
        cotangent,
    ):
        rows_here, model_width = tokens.shape
        bucket_count = relative_table.shape[0]
        width = projections.shape[2]
        spot = lax.axis_index("tensor")
        flip = spot % 2

        def after(value, ready):
            return lax.optimization_barrier((value, ready))[0]

        dp_place = lax.axis_index("dp").astype(jnp.int32)
        odd = dp_place & 1
        weight_own = projections.transpose(1, 2, 0).reshape(3 * width, model_width)
        x_other = swap_core(tokens)
        weight_y = swap_y(weight_own)
        place = jnp.stack([flip, spot // 2]).astype(jnp.int32)
        limits, key_code, seg_row, small_own = prepare(
            place, segment_ids, pad_mask, relative_table.T, projected_bias, expand_bias[None]
        )
        mixing_late = after(mixing_weight, small_own)
        contract_late = after(contract_weight, x_other)
        mixing_y = swap_y(mixing_late)
        half_rows = contract_weight.shape[0] // 2
        half_y = swap_y(lax.dynamic_slice_in_dim(contract_late, odd * half_rows, half_rows, 0))
        small_y = swap_y(small_own)
        bucket_row = buckets[255:1791][::-1][None]

        def forward(weight, small, x_in):
            return attend(limits, x_in, x_other, weight, small, bucket_row, key_code, seg_row)

        own_a, other_a, *saved_a = forward(weight_own, small_own, tokens)
        expand_y = swap_y(after(expand_weight, own_a))
        recv_a = swap_core(other_a)
        own_b, other_b, *saved_b = forward(weight_y, small_y, after(tokens, (own_a, mixing_y)))
        half_x = swap_dp(after(half_y, own_b), 1)
        mixing_core, expand_core, contract_core, small_core = [
            swap_core(value)
            for value in after((mixing_weight, expand_weight, contract_weight, small_own), own_a)
        ]
        mixing_diag, small_diag = swap_core(after(mixing_y, own_a)), swap_core(after(small_y, own_b))
        recv_b = swap_core(other_b)
        contract_y = jnp.where(
            odd == 0, jnp.concatenate([half_y, half_x]), jnp.concatenate([half_x, half_y])
        )
        contract_diag = swap_core(contract_y)
        normed_one, inverse_one, pair, hidden0, slope0, slope1, partial = first_half(
            tokens, own_a, recv_a, own_b, recv_b, mixing_weight, mixing_core, mixing_y, mixing_diag,
            residual_biases, norm_gains, norm_shifts,
            expand_weight, contract_weight, expand_core, contract_core, small_own, small_core,
        )
        pair_there = swap_core(pair)
        expand_y = after(expand_y, partial)
        expand_diag = swap_core(expand_y)
        hidden2, slope2, partial = third_slot(pair, expand_y, contract_y, small_y, partial)
        layer_out, grad_two, send, later_sums = second_half(
            normed_one, pair, partial, norm_gains, norm_shifts,
            expand_diag, contract_diag, contract_core, small_diag, slope1, cotangent,
        )
        arrived = swap_core(send)
        unit_grad0, unit_grad2, grad_one, outgoing, early = unit_back(
            send, contract_weight, contract_y, slope0, slope2,
            expand_weight, expand_core, expand_y, expand_diag,
            grad_two, normed_one, inverse_one, norm_gains, later_sums,
        )
        outgoing_there = swap_core(outgoing)
        early_there = swap_core(early)

        contract_bits = list(range(1, stages)) + [0, -1]
        contract_keep, contract_give = both_halves(
            digit_of(contract_bits[0]), dp_count, after(hidden2, outgoing), (arrived, 3),
            hidden0, (pair_there, 1), (send, 0), (arrived, 0),
        )
        contract_came = exchange(contract_give, contract_bits[0])
        expand_two = pair_grad(
            dp_count, (after(pair, contract_give), 0), (pair_there, 0), unit_grad2, (arrived, 2)
        )
        expand_across = swap_y(expand_two)
        expand_own = pair_grad(
            dp_count, (after(pair, expand_two), 0), (pair_there, 0), unit_grad0, (arrived, 1)
        )

        def backward(saved, weight, mixing_here, attended, ready, before=()):
            return attend_back(
                limits, mixing_here, after(outgoing, ready), outgoing_there, *saved, bucket_row,
                key_code, seg_row, tokens, x_other, weight, *attended, early, early_there, *before,
                pieces=dp_count, last=bool(before),
            )

        pieces_b, inputs_own, inputs_other, tail_b = backward(
            saved_b, weight_y, mixing_y, (own_b, other_b), expand_own
        )
        pieces_y = swap_y(pieces_b)
        contract_came, expand_across = after((contract_came, expand_across), pieces_b)
        contract_keep, contract_give = split(digit_of(contract_bits[1]), contract_keep, contract_came)
        contract_came = exchange(contract_give, contract_bits[1])
        expand_keep, expand_give = split(digit_of(0), expand_own, expand_across)
        expand_came = swap_dp(expand_give, 1)
        pieces_a, inputs_own, inputs_other, tail_a = backward(
            saved_a, weight_own, mixing_weight, (own_a, other_a),
            (pieces_b, contract_give, expand_give), (inputs_own, inputs_other),
        )
        pieces_y = after(pieces_y, pieces_a)
        expand_came = after(expand_came, pieces_a)
        contract_came = after(contract_came, pieces_a)

        def projection_steps():
            keep, give = split(digit_of(0), pieces_a, pieces_y)
            came = yield give, 0
            splits = (3 * width // dp_count, width // dp_count)
            return (yield from sum_over_dp(keep, came, range(1, stages), splits))

        def small_steps():
            value = tail_a + (yield tail_b, -1)
            for bit in list(range(1, stages)) + [0]:
                value = value + (yield value, bit)
            return value

        def input_steps():
            there = yield inputs_other, -2
            return total_of(digit_of(0), inputs_own, there, f32, grad_one)

        results = interleave(
            "tpecsepctcepecpcpssescps",
            {
                "t": input_steps(),
                "p": projection_steps(),
                "c": sum_over_dp(contract_keep, contract_came, contract_bits[2:]),
                "e": sum_over_dp(expand_keep, expand_came, range(1, stages)),
                "s": small_steps(),
            },
        )
        (contract_total,), (expand_total,) = results["c"], results["e"]
        projection_total, mixing_total = results["p"]
        sums = results["s"]
        tokens_grad = results["t"]

        return (
            layer_out,
            tokens_grad,
            projection_total.reshape(3, width, model_width).transpose(2, 0, 1),
            sums[NH : NH + 2, :width],
            sums[:NH, :bucket_count].T,
            mixing_total,
            sums[5:7],
            sums[7:9],
            sums[9:11],
            expand_total,
            sums[11],
            contract_total,
        )

    return body


def solution(mesh):
    return jax.shard_map(
        make_body(mesh.shape["dp"]),
        mesh=mesh,
        in_specs=(
            P(("dp", "tensor"), None),
            P("dp", None),
            P("dp", None),
            P(),
            P(None, None, "tensor"),
            P(None, "tensor"),
            P(None, "tensor"),
            P("tensor", None),
            P(),
            P(),
            P(),
            P(None, "tensor"),
            P("tensor"),
            P("tensor", None),
            P(("dp", "tensor"), None),
        ),
        out_specs=(
            P(("dp", "tensor"), None),
            P(("dp", "tensor"), None),
            P(None, None, "tensor"),
            P(None, "tensor"),
            P(None, "tensor"),
            P("tensor", None),
            P(),
            P(),
            P(),
            P(None, "tensor"),
            P("tensor"),
            P("tensor", None),
        ),
        check_vma=False,
    )
```

```python
import functools
import jax
import jax.numpy as jnp
from jax import lax
from jax.experimental import pallas as pl
from jax.experimental.pallas import tpu as pltpu
from jax.sharding import PartitionSpec as P

big_negative = -1e30
KB = 128
QT = 256
HALF = 512
SEQ = 1024
HW = 64
NH = 3
TILES = 11
SPAN = 1536
f32 = jnp.float32
bf16 = jnp.bfloat16
dot32 = functools.partial(lax.dot_general, preferred_element_type=f32)
NN = (((1,), (0,)), ((), ()))
NT = (((1,), (1,)), ((), ()))


def took(micros):
    return pl.CostEstimate(flops=int(micros * 8e5), transcendentals=0, bytes_accessed=int(micros * 3e3))


def in_hbm(value):
    return pltpu.with_memory_space_constraint(value, pltpu.HBM)


def three_parts(value):
    high = value.astype(bf16)
    rest = value - high.astype(f32)
    middle = rest.astype(bf16)
    low = (rest - middle.astype(f32)).astype(bf16)
    return high, middle, low


def bucket_grid(bucket_ref, count):
    rows = lax.broadcasted_iota(jnp.int32, (count, SPAN), 0)
    return (rows == bucket_ref[...]).astype(bf16)


def tile_mask(key_code, seg_row, difference, shift):
    codes = jnp.concatenate([key_code, key_code], axis=1)
    return (codes == seg_row) | (difference == shift)


def prepare_kernel(place, seg_scalar, segments, padding, table, pair_bias, unit_bias,
                   limits, key_code, seg_row, small):
    flip = place[0]
    chip = place[1]
    segs = segments[pl.ds(chip, 1), :]
    code = jnp.where(padding[pl.ds(chip, 1), :] == 1, segs, -1).astype(f32)
    wide = segs.astype(f32)
    for b in range(SEQ // QT):
        seg_row[b] = wide[:, b * QT : (b + 1) * QT]
        first = seg_scalar[chip, b * QT]
        last = seg_scalar[chip, b * QT + QT - 1]
        limits[b] = jnp.sum((segs < first).astype(f32)).astype(jnp.int32) // KB
        limits[4 + b] = (jnp.sum((segs <= last).astype(f32)).astype(jnp.int32) + KB - 1) // KB
    limits[8] = flip
    for b in range(SEQ // KB):
        key_code[b] = jnp.broadcast_to(code[:, b * KB : (b + 1) * KB], (KB, KB)).T
    small[...] = jnp.zeros(small.shape, f32)
    small[0:NH, : table.shape[1]] = table[...]
    small[NH : NH + 2, : pair_bias.shape[1]] = pair_bias[...]
    small[NH + 2 : NH + 3, : unit_bias.shape[1]] = unit_bias[...]


def prepare(place, segment_ids, pad_mask, table, pair_bias, unit_bias):
    vm = pl.BlockSpec(memory_space=pltpu.VMEM)
    sm = pl.BlockSpec(memory_space=pltpu.SMEM)
    return pl.pallas_call(
        prepare_kernel,
        out_shape=(
            jax.ShapeDtypeStruct((9,), jnp.int32),
            jax.ShapeDtypeStruct((SEQ // KB, KB, KB), f32),
            jax.ShapeDtypeStruct((SEQ // QT, 1, QT), f32),
            jax.ShapeDtypeStruct((8, unit_bias.shape[1]), f32),
        ),
        in_specs=[sm, sm, vm, vm, vm, vm, vm],
        out_specs=(sm, vm, vm, vm),
        cost_estimate=took(2),
        name="prepare",
    )(place, segment_ids, segment_ids, pad_mask, table, pair_bias, unit_bias)


def forward_kernel(limits, x_own, x_other, weight, small, buckets, key_code, seg_row,
                   own_out, other_out, full_far, totals_far, heads_far, turned_far, tiles_far,
                   out_full, totals, heads_out, turned_out, tiles, best, total, gathered, done):
    flip = limits[8]

    def send(count, *pairs):
        copies = [
            pltpu.make_async_copy(near, far, done.at[count + i]) for i, (near, far) in enumerate(pairs)
        ]
        for copy in copies:
            copy.start()
        return copies

    width = NH * HW
    columns = small[:, :256].T
    for half, x_ref in enumerate((x_own, x_other)):
        plain = dot32(x_ref[...], weight[...], NT)
        across = dot32(weight[...], x_ref[...], NT)
        rows = pl.ds(half * HALF, HALF)
        for c in range(3):
            part, turned = plain[:, c * width : (c + 1) * width], across[c * width : (c + 1) * width]
            if c != 1:
                r = NH + c // 2
                part = part + small[r : r + 1, :width]
                turned = turned + columns[:width, r : r + 1]
            part, turned = part.astype(bf16), turned.astype(bf16)
            if c == 0:
                part, turned = part * 0.125, turned * 0.125
            for h in range(NH):
                heads_out[c * NH + h, rows, :] = part[:, h * HW : (h + 1) * HW]
            for k in range(HALF // KB):
                turned_out[half * (HALF // KB) + k, c * width : (c + 1) * width, :] = turned[
                    :, k * KB : (k + 1) * KB
                ]
    hot = bucket_grid(buckets, 256)
    line = sum(dot32(part, hot, NN) for part in three_parts(small[:, :256]))
    for h in range(NH):
        for u in range(TILES):
            start = 640 - 128 * (u - 5)
            spread = jnp.broadcast_to(line[h : h + 1, start : start + 256], (KB, 256))
            tiles[h, u] = pltpu.roll(spread, 129, 1, stride=1, stride_axis=0)[:, :KB]
    copies = send(0, (heads_out, heads_far), (turned_out, turned_far), (tiles, tiles_far))
    difference = lax.broadcasted_iota(jnp.int32, (KB, QT), 1) - lax.broadcasted_iota(
        jnp.int32, (KB, QT), 0
    )

    def query_step(block, carry):
        place = block ^ (flip * 2)
        best[...] = jnp.full(best.shape, big_negative, f32)
        total[...] = jnp.zeros(total.shape, f32)
        gathered[...] = jnp.zeros(gathered.shape, f32)
        segs = seg_row[place]

        def key_step(key_place, carry):
            key_block = key_place ^ (flip * 4)
            gap = key_place - 2 * place
            allowed = tile_mask(key_code[key_place], segs, difference, gap * KB)
            queries = [
                jnp.concatenate([turned_out[2 * block + i, h * HW : (h + 1) * HW, :] for i in range(2)], axis=1)
                for h in range(NH)
            ]
            k_rows = pl.ds(key_block * KB, KB)
            scores = [dot32(heads_out[NH + h, k_rows, :], queries[h], NN) for h in range(NH)]
            lows, shrinks = [], []
            for h in range(NH):
                bias = jnp.concatenate([tiles[h, gap + 5], tiles[h, gap + 4]], axis=1)
                value = jnp.where(allowed, scores[h] + bias, big_negative)
                old = best[h]
                new = jnp.maximum(old, jnp.max(value, axis=0, keepdims=True))
                value = jnp.exp(value - new)
                shrink = jnp.exp(old - new)
                best[h] = new
                total[h] = shrink * total[h] + jnp.sum(value, axis=0, keepdims=True)
                lows.append(value.astype(bf16))
                shrinks.append(shrink)
            for h in range(NH):
                turned_v = turned_out[key_block, (2 * NH + h) * HW : (2 * NH + h + 1) * HW, :]
                gathered[h] = gathered[h] * shrinks[h] + dot32(turned_v, lows[h], NN)
            return carry

        lax.fori_loop(limits[place], limits[4 + place], key_step, 0)
        for h in range(NH):
            result = gathered[h] / total[h]
            out_full[block, h * HW : (h + 1) * HW, :] = result
            totals[block, h : h + 1, :] = best[h] + jnp.log(total[h])
        return carry

    lax.fori_loop(0, SEQ // QT, query_step, 0)
    copies = copies + send(3, (out_full, full_far), (totals, totals_far))
    for c in range(2):
        own_out[:, c * QT : (c + 1) * QT] = out_full[c].astype(bf16)
        other_out[:, c * QT : (c + 1) * QT] = out_full[2 + c].astype(bf16)
    for copy in copies:
        copy.wait()


def saved_shapes():
    return (
        ((SEQ // QT, NH * HW, QT), f32),
        ((SEQ // QT, 8, QT), f32),
        ((3 * NH, SEQ, HW), bf16),
        ((SEQ // KB, 3 * NH * HW, KB), bf16),
        ((NH, TILES, KB, KB), f32),
    )


def attend(limits, x_own, x_other, weight, small, buckets, key_code, seg_row):
    vm = pl.BlockSpec(memory_space=pltpu.VMEM)
    return pl.pallas_call(
        forward_kernel,
        out_shape=(
            jax.ShapeDtypeStruct((NH * HW, HALF), bf16),
            jax.ShapeDtypeStruct((NH * HW, HALF), bf16),
        )
        + tuple(pltpu.HBM(shape, kind) for shape, kind in saved_shapes()),
        in_specs=[pl.BlockSpec(memory_space=pltpu.SMEM)] + [vm] * 7,
        out_specs=(vm, vm) + (pl.BlockSpec(memory_space=pltpu.HBM),) * 5,
        scratch_shapes=[pltpu.VMEM(shape, kind) for shape, kind in saved_shapes()]
        + [
            pltpu.VMEM((NH, 1, QT), f32),
            pltpu.VMEM((NH, 1, QT), f32),
            pltpu.VMEM((NH, HW, QT), f32),
            pltpu.SemaphoreType.DMA((5,)),
        ],
        compiler_params=pltpu.CompilerParams(vmem_limit_bytes=20 << 20),
        cost_estimate=took(20),
        name="attend",
    )(limits, x_own, x_other, weight, small, buckets, key_code, seg_row)


def backward_kernel(limits, mixing, outgoing_own, outgoing_other, full_far, totals_far, heads_far,
                    turned_far, tiles_far, buckets, key_code, seg_row, x_own_far, x_other_far, weight_far, attended_own,
                    attended_other, early, early_there, *rest, last):
    if last:
        before_own_far, before_other_far, *rest = rest
    (pieces_out, own_out, other_out, tail_out,
     out_full, totals, heads, turned, tiles,
     turned_grad, plain_grad, row_dots, query_acc, query_all, key_acc, value_acc, tile_acc,
     grads, done, *rest) = rest
    flip = limits[8]
    fetched = [
        pltpu.make_async_copy(far, near, done.at[i])
        for i, (far, near) in enumerate(
            ((full_far, out_full), (totals_far, totals), (heads_far, heads), (turned_far, turned),
             (tiles_far, tiles))
        )
    ]
    x_own, x_other, weight, *rest = rest
    pairs = [(x_own_far, x_own), (x_other_far, x_other), (weight_far, weight)]
    if last:
        before_own, before_other = rest
        pairs += [(before_own_far, before_own), (before_other_far, before_other)]
    late = [pltpu.make_async_copy(far, near, done.at[5 + i]) for i, (far, near) in enumerate(pairs)]
    for copy in fetched:
        copy.start()
    key_acc[...] = jnp.zeros(key_acc.shape, f32)
    value_acc[...] = jnp.zeros(value_acc.shape, f32)
    tile_acc[...] = jnp.zeros(tile_acc.shape, f32)
    fetched[0].wait()
    for half, ref in enumerate((outgoing_own, outgoing_other)):
        across = dot32(mixing[...], ref[...], NT).astype(bf16)
        for c in range(2):
            block = 2 * half + c
            piece = across[:, c * QT : (c + 1) * QT]
            turned_grad[block] = piece
            wide = piece.astype(f32)
            product = wide * out_full[block]
            for h in range(NH):
                rows = slice(h * HW, (h + 1) * HW)
                row_dots[block, h : h + 1, :] = jnp.sum(product[rows], axis=0, keepdims=True)
                plain_grad[h, block * QT : (block + 1) * QT, :] = wide[rows].T.astype(bf16)
    for copy in fetched[1:]:
        copy.wait()
    for copy in late:
        copy.start()
    difference = lax.broadcasted_iota(jnp.int32, (KB, QT), 1) - lax.broadcasted_iota(
        jnp.int32, (KB, QT), 0
    )

    def query_step(block, carry):
        place = block ^ (flip * 2)
        query_acc[...] = jnp.zeros(query_acc.shape, f32)
        segs = seg_row[place]
        q_rows = pl.ds(block * QT, QT)

        def key_step(key_place, carry):
            key_block = key_place ^ (flip * 4)
            gap = key_place - 2 * place
            k_rows = pl.ds(key_block * KB, KB)
            allowed = tile_mask(key_code[key_place], segs, difference, gap * KB)
            queries = [
                jnp.concatenate([turned[2 * block + i, h * HW : (h + 1) * HW, :] for i in range(2)], axis=1)
                for h in range(NH)
            ]
            scores = [dot32(heads[NH + h, k_rows, :], queries[h], NN) for h in range(NH)]
            chance_grads = [
                dot32(heads[2 * NH + h, k_rows, :], turned_grad[block, h * HW : (h + 1) * HW, :], NN)
                for h in range(NH)
            ]
            chances, score_lows = [], []
            for h in range(NH):
                bias = jnp.concatenate([tiles[h, gap + 5], tiles[h, gap + 4]], axis=1)
                value = jnp.where(allowed, scores[h] + bias, big_negative)
                chance = jnp.exp(value - totals[block, h : h + 1, :])
                score_grad = chance * (chance_grads[h] - row_dots[block, h : h + 1, :])
                tile_acc[h, gap + 5] += score_grad[:, :KB]
                tile_acc[h, gap + 4] += score_grad[:, KB:]
                chances.append(chance.astype(bf16))
                score_lows.append(score_grad.astype(bf16))
            for h in range(NH):
                value_acc[h, k_rows, :] += dot32(chances[h], plain_grad[h, q_rows, :], NN)
            for h in range(NH):
                key_acc[h, k_rows, :] += dot32(score_lows[h], heads[h, q_rows, :], NN)
            for h in range(NH):
                turned_k = turned[key_block, (NH + h) * HW : (NH + h + 1) * HW, :]
                query_acc[h] += dot32(turned_k, score_lows[h], NN)
            return carry

        lax.fori_loop(limits[place], limits[4 + place], key_step, 0)
        for h in range(NH):
            query_all[h, q_rows, :] = (query_acc[h] * 0.125).T
        return carry

    lax.fori_loop(0, SEQ // QT, query_step, 0)
    width = NH * HW
    for g, acc in ((0, query_all), (1, key_acc), (2, value_acc)):
        for h in range(NH):
            at = (g * NH + h) * HW
            grads[:, at : at + HW] = acc[h].astype(bf16)
    tail_out[...] = jnp.zeros(tail_out.shape, f32)
    tail_out[5:11, :] = early[5:11, :] + early_there[5:11, :]
    r = 11 if last else 12
    tail_out[11:12, :] = early[r : r + 1, :] + early_there[r + 2 : r + 3, :]
    for r in range(2):
        sums = jnp.sum(grads[:, 2 * r * width : (2 * r + 1) * width].astype(f32), axis=0, keepdims=True)
        tail_out[NH + r : NH + r + 1, :width] = sums
    for copy in late:
        copy.wait()
    total = dot32(grads[:HALF, :], x_own[...], TN) + dot32(grads[HALF:, :], x_other[...], TN)
    mixed = dot32(attended_own[...], outgoing_own[...], NN) + dot32(
        attended_other[...], outgoing_other[...], NN
    )
    pieces = pieces_out.shape[0]
    first, second = total.shape[0] // pieces, mixed.shape[0] // pieces
    for p in range(pieces):
        pieces_out[p, :first] = total[p * first : (p + 1) * first].astype(bf16)
        pieces_out[p, first:] = mixed[p * second : (p + 1) * second].astype(bf16)
    own = dot32(grads[:HALF, :], weight[...], NN)
    other = dot32(grads[HALF:, :], weight[...], NN)
    if last:
        own = own + before_own[...]
        other = other + before_other[...]
    own_out[...] = own
    other_out[...] = other.astype(other_out.dtype)
    hot = bucket_grid(buckets, 256)
    lines = []
    for h in range(NH):
        spans = [jnp.zeros((1, KB), f32) for _ in range(SPAN // KB)]
        for u in range(TILES):
            wide = jnp.concatenate([tile_acc[h, u], jnp.zeros((KB, KB), f32)], axis=1)
            count = KB // 2
            while count:
                wide = wide[count:] + pltpu.roll(wide[:count], count, 1)
                count //= 2
            at = (640 - 128 * (u - 5)) // KB
            spans[at] = spans[at] + wide[:, :KB]
            spans[at + 1] = spans[at + 1] + wide[:, KB:]
        lines.append(jnp.concatenate(spans, axis=1))
    lines.append(jnp.zeros((8 - NH, SPAN), f32))
    line = jnp.concatenate(lines, axis=0)
    tail_out[:NH, :256] = sum(dot32(part, hot, NT) for part in three_parts(line))[:NH]


def attend_back(limits, *args, pieces, last):
    vm = pl.BlockSpec(memory_space=pltpu.VMEM)
    wide, model = args[13].shape
    rows = args[1].shape[0]
    piece = (wide + wide // 3) // pieces
    return pl.pallas_call(
        functools.partial(backward_kernel, last=last),
        out_shape=(
            jax.ShapeDtypeStruct((pieces, piece, model), bf16),
            (jax.ShapeDtypeStruct if last else pltpu.HBM)((rows, model), f32),
            (jax.ShapeDtypeStruct if last else pltpu.HBM)((rows, model), bf16 if last else f32),
            jax.ShapeDtypeStruct((16, model), f32),
        ),
        in_specs=[pl.BlockSpec(memory_space=pltpu.SMEM)] + [vm] * 3
        + [pl.BlockSpec(memory_space=pltpu.HBM)] * 5 + [vm] * 3
        + [pl.BlockSpec(memory_space=pltpu.HBM)] * 3 + [vm] * 4
        + [pl.BlockSpec(memory_space=pltpu.HBM)] * (2 if last else 0),
        out_specs=tuple([vm] * 4),
        scratch_shapes=[pltpu.VMEM(shape, kind) for shape, kind in saved_shapes()]
        + [
            pltpu.VMEM((SEQ // QT, NH * HW, QT), bf16),
            pltpu.VMEM((NH, SEQ, HW), bf16),
            pltpu.VMEM((SEQ // QT, 8, QT), f32),
            pltpu.VMEM((NH, HW, QT), f32),
            pltpu.VMEM((NH, SEQ, HW), f32),
            pltpu.VMEM((NH, SEQ, HW), f32),
            pltpu.VMEM((NH, SEQ, HW), f32),
            pltpu.VMEM((NH, TILES, KB, KB), f32),
            pltpu.VMEM((SEQ, 3 * NH * HW), bf16),
            pltpu.SemaphoreType.DMA((10,)),
            pltpu.VMEM((rows, model), bf16),
            pltpu.VMEM((rows, model), bf16),
            pltpu.VMEM((wide, model), bf16),
        ]
        + [pltpu.VMEM((rows, model), f32)] * (2 if last else 0),
        compiler_params=pltpu.CompilerParams(vmem_limit_bytes=36 << 20),
        cost_estimate=took(25),
        name="attend_back",
    )(limits, in_hbm(args[0]), *args[1:3], *[in_hbm(arg) for arg in args[3:8]], *args[8:11],
      *[in_hbm(arg) for arg in args[11:16]], *args[16:18], *[in_hbm(arg) for arg in args[18:]])


ROWS = 128
TN = (((0,), (0,)), ((), ()))
norm_eps = 1e-05


def whole(count):
    return [pl.BlockSpec(memory_space=pltpu.VMEM)] * count


def normalise(value):
    centered = value - jnp.mean(value, axis=-1, keepdims=True)
    inverse = lax.rsqrt(jnp.mean(centered * centered, axis=-1, keepdims=True) + norm_eps)
    return centered * inverse, inverse


def normalise_back(scaled, normed, inverse):
    first_mean = jnp.mean(scaled, axis=-1, keepdims=True)
    second_mean = jnp.mean(scaled * normed, axis=-1, keepdims=True)
    return inverse * (scaled - first_mean - normed * second_mean)


def gelu_parts(value):
    cumulative = 0.5 * (1.0 + lax.erf(value * 0.7071067811865476))
    density = jnp.exp(-0.5 * value * value) * 0.3989422804014327
    return (value * cumulative).astype(bf16), cumulative + value * density


def add_column(ref, at, value):
    ref[at] += jnp.sum(value.reshape(-1, 8, value.shape[1]), axis=0)


def first_half_kernel(tokens, own_a, recv_a, own_b, recv_b, mix0, mix1, mix2, mix3, biases, gains,
                      shifts, expand0, contract0, expand1, contract1, small0, small1,
                      normed_out, inverse_out, pair_out, hidden0_out, slope0_out, slope1_out, partial_out):
    def step(r, carry):
        at = pl.multiple_of(r * ROWS, ROWS)
        rows = pl.ds(at, ROWS)
        branch = tokens[rows, :].astype(f32) + biases[0:1, :]
        for attended, mixing in ((own_a, mix0), (recv_a, mix1), (own_b, mix2), (recv_b, mix3)):
            branch = branch + dot32(attended[:, rows], mixing[...], TN)
        normed, inverse = normalise(branch)
        normed_out[rows, :] = normed
        inverse_out[rows, :] = inverse
        low = (normed * gains[0:1, :] + shifts[0:1, :]).astype(bf16)
        pair_out[0, rows, :] = low
        partial = biases[1:2, :]
        for s, expand, contract, small in ((0, expand0, contract0, small0), (1, expand1, contract1, small1)):
            hidden, slope = gelu_parts(dot32(low, expand[...], NN) + small[5:6, :])
            if s == 0:
                hidden0_out[rows, :] = hidden
                slope0_out[rows, :] = slope
            else:
                pair_out[1, rows, :] = hidden
                slope1_out[rows, :] = slope
            partial = partial + dot32(hidden, contract[...], NN)
        partial_out[rows, :] = partial
        return carry

    lax.fori_loop(0, tokens.shape[0] // ROWS, step, 0)


def first_half(*args):
    rows, cols = args[0].shape
    wide = jax.ShapeDtypeStruct((rows, cols), f32)
    return pl.pallas_call(
        first_half_kernel,
        out_shape=(wide, jax.ShapeDtypeStruct((rows, 1), f32),
                   jax.ShapeDtypeStruct((2, rows, cols), bf16),
                   jax.ShapeDtypeStruct((rows, cols), bf16), wide, wide, wide),
        in_specs=whole(len(args)),
        out_specs=tuple(whole(7)),
        compiler_params=pltpu.CompilerParams(vmem_limit_bytes=16 << 20),
        cost_estimate=took(12),
        name="first_half",
    )(*[in_hbm(arg) if 1 <= i <= 8 else arg for i, arg in enumerate(args)])


def third_slot_kernel(pair, expand, contract, small, partial_in, hidden_out, slope_out, partial_out):
    def step(r, carry):
        rows = pl.ds(pl.multiple_of(r * ROWS, ROWS), ROWS)
        hidden, slope = gelu_parts(dot32(pair[0, rows, :], expand[...], NN) + small[5:6, :])
        hidden_out[rows, :] = hidden
        slope_out[rows, :] = slope
        partial_out[rows, :] = partial_in[rows, :] + dot32(hidden, contract[...], NN)
        return carry

    lax.fori_loop(0, partial_in.shape[0] // ROWS, step, 0)


def third_slot(*args):
    rows, cols = args[4].shape
    wide = jax.ShapeDtypeStruct((rows, cols), f32)
    return pl.pallas_call(
        third_slot_kernel,
        out_shape=(jax.ShapeDtypeStruct((rows, cols), bf16), wide, wide),
        in_specs=whole(5),
        out_specs=tuple(whole(3)),
        compiler_params=pltpu.CompilerParams(vmem_limit_bytes=16 << 20),
        cost_estimate=took(5),
        name="third_slot",
    )(*args)


def second_half_kernel(normed_in, pair, partial_in, gains, shifts, expand3, contract3, contract1,
                       small, slope1, cotangent,
                       layer_out, grad_two_out, send_out, sums_out):
    sums_out[...] = jnp.zeros(sums_out.shape, f32)

    def step(r, carry):
        rows = pl.ds(pl.multiple_of(r * ROWS, ROWS), ROWS)
        low = pair[0, rows, :]
        total = normed_in[rows, :] * gains[0:1, :] + shifts[0:1, :] + partial_in[rows, :]
        hidden3, slope3 = gelu_parts(dot32(low, expand3[...], NN) + small[5:6, :])
        send_out[3, rows, :] = hidden3
        total = total + dot32(hidden3, contract3[...], NN)
        normed, inverse = normalise(total)
        layer_out[rows, :] = (normed * gains[1:2, :] + shifts[1:2, :]).astype(bf16)
        outer = cotangent[rows, :].astype(f32)
        grad_two = normalise_back(outer * gains[1:2, :], normed, inverse)
        grad_two_out[rows, :] = grad_two
        upstream = grad_two.astype(bf16)
        send_out[0, rows, :] = upstream
        add_column(sums_out, 0, grad_two)
        add_column(sums_out, 1, outer * normed)
        add_column(sums_out, 2, outer)
        for at, contract, slope in ((1, contract1, slope1[rows, :]), (2, contract3, slope3)):
            unit_grad = (dot32(upstream, contract[...], NT) * slope).astype(bf16)
            send_out[at, rows, :] = unit_grad
            add_column(sums_out, 2 + at, unit_grad.astype(f32))
        return carry

    lax.fori_loop(0, normed_in.shape[0] // ROWS, step, 0)


def second_half(*args):
    rows, cols = args[0].shape
    wide = jax.ShapeDtypeStruct((rows, cols), f32)
    low = jax.ShapeDtypeStruct((rows, cols), bf16)
    return pl.pallas_call(
        second_half_kernel,
        out_shape=(low, wide, jax.ShapeDtypeStruct((4, rows, cols), bf16),
                   jax.ShapeDtypeStruct((5, 8, cols), f32)),
        in_specs=whole(len(args)),
        out_specs=tuple(whole(4)),
        compiler_params=pltpu.CompilerParams(vmem_limit_bytes=16 << 20),
        cost_estimate=took(15),
        name="second_half",
    )(*args)


def unit_back_kernel(send, contract0, contract2, slope0, slope2, expand0, expand1, expand2, expand3,
                     grad_two, normed_in, inverse_in, gains, later,
                     grad0_out, grad2_out, grad_one_out, outgoing_out, rows_out, sums_out):
    sums_out[...] = jnp.zeros(sums_out.shape, f32)

    def step(r, carry):
        rows = pl.ds(pl.multiple_of(r * ROWS, ROWS), ROWS)
        upstream = send[0, rows, :]
        total = grad_two[rows, :]
        total = total + dot32(send[1, rows, :], expand1[...], NT)
        total = total + dot32(send[2, rows, :], expand3[...], NT)
        for at, contract, slope, expand, out in ((3, contract0, slope0, expand0, grad0_out),
                                                 (4, contract2, slope2, expand2, grad2_out)):
            unit_grad = (dot32(upstream, contract[...], NT) * slope[rows, :]).astype(bf16)
            out[rows, :] = unit_grad
            add_column(sums_out, at, unit_grad.astype(f32))
            total = total + dot32(unit_grad, expand[...], NT)
        normed = normed_in[rows, :]
        grad_one = normalise_back(total * gains[0:1, :], normed, inverse_in[rows, :])
        grad_one_out[rows, :] = grad_one
        outgoing_out[rows, :] = grad_one.astype(bf16)
        add_column(sums_out, 0, grad_one)
        add_column(sums_out, 1, total * normed)
        add_column(sums_out, 2, total)
        return carry

    lax.fori_loop(0, grad_two.shape[0] // ROWS, step, 0)
    rows_out[...] = jnp.zeros(rows_out.shape, f32)
    order = (sums_out[0], later[0], sums_out[1], later[1], sums_out[2], later[2],
             sums_out[3], sums_out[4], later[3], later[4])
    for r, value in enumerate(order):
        rows_out[5 + r : 6 + r, :] = jnp.sum(value, axis=0, keepdims=True)


def unit_back(*args):
    rows, cols = args[9].shape
    low = jax.ShapeDtypeStruct((rows, cols), bf16)
    return pl.pallas_call(
        unit_back_kernel,
        out_shape=(low, low, jax.ShapeDtypeStruct((rows, cols), f32), low,
                   jax.ShapeDtypeStruct((16, cols), f32)),
        in_specs=whole(len(args)),
        out_specs=tuple(whole(5)),
        scratch_shapes=[pltpu.VMEM((5, 8, cols), f32)],
        compiler_params=pltpu.CompilerParams(vmem_limit_bytes=16 << 20),
        cost_estimate=took(17),
        name="unit_back",
    )(*args)


def pair_grad_kernel(left, left_there, right, right_there, out):
    total = dot32(left[...], right[...], TN) + dot32(left_there[...], right_there[...], TN)
    rows = out.shape[1]
    for p in range(out.shape[0]):
        out[p] = total[p * rows : (p + 1) * rows].astype(bf16)


def both_halves_kernel(digit, two, two_there, own, own_there, right, right_there, keep_out, give_out):
    half, rows, _ = keep_out.shape
    half //= 2
    bits = half.bit_length()
    for slot, (left, left_there) in enumerate(((two, two_there), (own, own_there))):
        total = dot32(left[...], right[...], TN) + dot32(left_there[...], right_there[...], TN)
        for q in range(half):
            first = q if bits < 2 else (q >> bits - 2) | sum(
                (q >> i & 1) << i + 2 for i in range(bits - 2)
            )
            step = 1 if bits < 2 else 2
            low = total[first * rows : (first + 1) * rows]
            high = total[(first + step) * rows : (first + step + 1) * rows]
            keep_out[slot * half + q] = jnp.where(digit[0] == 0, low, high)
            give_out[slot * half + q] = jnp.where(digit[0] == 0, high, low).astype(bf16)


def indexed(operand):
    array, index = operand if isinstance(operand, tuple) else (operand[None], 0)
    return array, pl.BlockSpec((None,) + array.shape[1:], lambda i, index=index: (index, 0, 0))


def both_halves(digit, pieces, *operands):
    arrays, specs = zip(*[indexed(operand) for operand in operands])
    rows, cols = arrays[0].shape[2] // pieces, arrays[4].shape[2]
    return pl.pallas_call(
        both_halves_kernel,
        out_shape=tuple(jax.ShapeDtypeStruct((pieces, rows, cols), kind) for kind in (f32, bf16)),
        grid=(1,),
        in_specs=[pl.BlockSpec(memory_space=pltpu.SMEM)] + list(specs),
        out_specs=tuple(pl.BlockSpec((pieces, rows, cols), lambda i: (0, 0, 0)) for _ in range(2)),
        compiler_params=pltpu.CompilerParams(vmem_limit_bytes=14 << 20),
        cost_estimate=took(4),
        name="both_halves",
    )(digit, *arrays)


def pair_grad(pieces, *operands):
    arrays, specs = zip(*[indexed(operand) for operand in operands])
    rows, cols = arrays[0].shape[2] // pieces, arrays[2].shape[2]
    return pl.pallas_call(
        pair_grad_kernel,
        out_shape=jax.ShapeDtypeStruct((pieces, rows, cols), bf16),
        grid=(1,),
        in_specs=list(specs),
        out_specs=pl.BlockSpec((pieces, rows, cols), lambda i: (0, 0, 0)),
        compiler_params=pltpu.CompilerParams(vmem_limit_bytes=16 << 20),
        cost_estimate=took(4),
        name="pair_grad",
    )(*arrays)


def assemble_kernel(place, mine, theirs, *outs):
    low = place[0] & 1
    high = place[0] >> 1
    for r in range(mine.shape[0]):
        at = (r ^ high) * 2
        start = 0
        for out in outs:
            rows = out.shape[1]
            out[at + low] = mine[r, start : start + rows].astype(f32)
            out[at + 1 - low] = theirs[r, start : start + rows].astype(f32)
            start += rows


def assemble(place, mine, theirs, splits):
    half, rows, cols = mine.shape
    vm = pl.BlockSpec(memory_space=pltpu.VMEM)
    return pl.pallas_call(
        assemble_kernel,
        out_shape=tuple(jax.ShapeDtypeStruct((2 * half, part, cols), f32) for part in splits),
        in_specs=[pl.BlockSpec(memory_space=pltpu.SMEM), vm, vm],
        out_specs=tuple(vm for _ in splits),
        compiler_params=pltpu.CompilerParams(vmem_limit_bytes=32 << 20),
        cost_estimate=took(2),
        name="assemble",
    )(place, mine, theirs)


def small_call(kernel, name, outs, *args):
    vm = pl.BlockSpec(memory_space=pltpu.VMEM)
    return pl.pallas_call(
        kernel,
        out_shape=tuple(jax.ShapeDtypeStruct(shape, kind) for shape, kind in outs),
        in_specs=[pl.BlockSpec(memory_space=pltpu.SMEM)] + [vm] * (len(args) - 1),
        out_specs=tuple(vm for _ in outs),
        compiler_params=pltpu.CompilerParams(vmem_limit_bytes=16 << 20),
        cost_estimate=took(1),
        name=name,
    )(*args)


def split_kernel(digit, first, second, keep_out, give_out):
    for q in range(keep_out.shape[0]):
        keep, give = 2 * q + digit[0], 2 * q + 1 - digit[0]
        if len(second.shape) < 3:
            keep_out[q] = first[keep].astype(f32)
            give_out[q] = first[give]
        else:
            keep_out[q] = first[keep].astype(f32) + second[keep].astype(f32)
            give_out[q] = (first[give].astype(f32) + second[give].astype(f32)).astype(bf16)


def split(digit, first, second):
    shape = (first.shape[0] // 2,) + first.shape[1:]
    second = digit[None] if second is None else second
    return small_call(split_kernel, "split", ((shape, f32), (shape, bf16)), digit, first, second)


def total_kernel(digit, first, second, *rest):
    out = rest[-1]
    total = first[...].astype(f32) + second[...].astype(f32)
    if len(rest) > 1:
        total = total + rest[0][...]
    out[...] = total.astype(out.dtype)


def total_of(digit, first, second, kind, *third):
    return small_call(total_kernel, "total", ((first.shape, kind),), digit, first, second, *third)[0]


def arrange_kernel(digit, first, second, out):
    for q in range(out.shape[0]):
        at = q ^ digit[0]
        out[q] = (first[at].astype(f32) + second[at].astype(f32)).astype(out.dtype)


def arrange(digit, first, second):
    return small_call(arrange_kernel, "arrange", ((first.shape, first.dtype),), digit, first, second)[0]


def join_kernel(digit, first, second, out):
    for q in range(first.shape[0]):
        out[2 * q] = first[q]
        out[2 * q + 1] = second[q]


def join(digit, first, second):
    shape = (2 * first.shape[0],) + first.shape[1:]
    return small_call(join_kernel, "join", ((shape, first.dtype),), digit, first, second)[0]


def make_body(dp_count):
    stages = dp_count.bit_length() - 1

    def swap(value, axis, count, bits):
        return lax.ppermute(value, axis, [(i, i ^ bits) for i in range(count)])

    swap_core = lambda value: swap(value, "tensor", 4, 1)
    swap_y = lambda value: swap(value, "tensor", 4, 2)
    swap_dp = lambda value, bits: swap(value, "dp", dp_count, bits)

    def digit_of(bit):
        if bit == -1:
            return jnp.ones((1,), jnp.int32)
        return (lax.axis_index("dp").astype(jnp.int32) >> bit & 1)[None]

    def exchange(value, bit):
        if bit == -1:
            return swap_y(value)
        return swap_core(value) if bit == -2 else swap_dp(value, 1 << bit)

    def sum_over_dp(keep, came, bits, splits=None):
        bits = list(bits)
        top = stages - 1
        doubled = bits[-1:] == [top]
        for bit in bits[: len(bits) - doubled]:
            keep, give = split(digit_of(bit), keep, came)
            came = yield give, bit
        mine = total_of(digit_of(0), keep, came, bf16)
        if doubled:
            came = yield mine, top
            mine = arrange(digit_of(top), mine, came)
        for bit in range(top - doubled, 0, -1):
            came = yield mine, bit
            mine = join(digit_of(0), mine, came)
        theirs = yield mine, 0
        place = lax.axis_index("dp").astype(jnp.int32)[None]
        parts = assemble(place, mine, theirs, splits or (keep.shape[1],))
        return [part.reshape(-1, part.shape[2]) for part in parts]

    def interleave(order, steps):
        came = {name: None for name in steps}
        results = {}
        token = None
        names = list(order) + [name for name in steps for _ in range(4 * stages)]
        for name in names:
            if name in results:
                continue
            if token is not None and came[name] is not None:
                came[name] = lax.optimization_barrier((came[name], token))[0]
            try:
                value, bit = steps[name].send(came[name])
                if token is not None and came[name] is None:
                    value = lax.optimization_barrier((value, token))[0]
                token = value
                came[name] = exchange(value, bit)
            except StopIteration as stop:
                token = results[name] = stop.value
        return results

    def body(
        tokens,
        segment_ids,
        pad_mask,
        buckets,
        projections,
        projected_bias,
        relative_table,
        mixing_weight,
        residual_biases,
        norm_gains,
        norm_shifts,
        expand_weight,
        expand_bias,
        contract_weight,
        cotangent,
    ):
        rows_here, model_width = tokens.shape
        bucket_count = relative_table.shape[0]
        width = projections.shape[2]
        spot = lax.axis_index("tensor")
        flip = spot % 2

        def after(value, ready):
            return lax.optimization_barrier((value, ready))[0]

        dp_place = lax.axis_index("dp").astype(jnp.int32)
        odd = dp_place & 1
        weight_own = projections.transpose(1, 2, 0).reshape(3 * width, model_width)
        x_other = swap_core(tokens)
        weight_y = swap_y(weight_own)
        place = jnp.stack([flip, spot // 2]).astype(jnp.int32)
        limits, key_code, seg_row, small_own = prepare(
            place, segment_ids, pad_mask, relative_table.T, projected_bias, expand_bias[None]
        )
        mixing_late = after(mixing_weight, small_own)
        contract_late = after(contract_weight, x_other)
        mixing_y = swap_y(mixing_late)
        half_rows = contract_weight.shape[0] // 2
        half_y = swap_y(lax.dynamic_slice_in_dim(contract_late, odd * half_rows, half_rows, 0))
        small_y = swap_y(small_own)
        bucket_row = buckets[255:1791][::-1][None]

        def forward(weight, small, x_in):
            return attend(limits, x_in, x_other, weight, small, bucket_row, key_code, seg_row)

        own_a, other_a, *saved_a = forward(weight_own, small_own, tokens)
        expand_y = swap_y(after(expand_weight, own_a))
        recv_a = swap_core(other_a)
        own_b, other_b, *saved_b = forward(weight_y, small_y, after(tokens, (own_a, mixing_y)))
        half_x = swap_dp(after(half_y, own_b), 1)
        mixing_core, expand_core, contract_core, small_core = [
            swap_core(value)
            for value in after((mixing_weight, expand_weight, contract_weight, small_own), own_a)
        ]
        mixing_diag, small_diag = swap_core(after(mixing_y, own_a)), swap_core(after(small_y, own_b))
        recv_b = swap_core(other_b)
        contract_y = jnp.where(
            odd == 0, jnp.concatenate([half_y, half_x]), jnp.concatenate([half_x, half_y])
        )
        contract_diag = swap_core(contract_y)
        normed_one, inverse_one, pair, hidden0, slope0, slope1, partial = first_half(
            tokens, own_a, recv_a, own_b, recv_b, mixing_weight, mixing_core, mixing_y, mixing_diag,
            residual_biases, norm_gains, norm_shifts,
            expand_weight, contract_weight, expand_core, contract_core, small_own, small_core,
        )
        pair_there = swap_core(pair)
        expand_y = after(expand_y, partial)
        expand_diag = swap_core(expand_y)
        hidden2, slope2, partial = third_slot(pair, expand_y, contract_y, small_y, partial)
        layer_out, grad_two, send, later_sums = second_half(
            normed_one, pair, partial, norm_gains, norm_shifts,
            expand_diag, contract_diag, contract_core, small_diag, slope1, cotangent,
        )
        arrived = swap_core(send)
        unit_grad0, unit_grad2, grad_one, outgoing, early = unit_back(
            send, contract_weight, contract_y, slope0, slope2,
            expand_weight, expand_core, expand_y, expand_diag,
            grad_two, normed_one, inverse_one, norm_gains, later_sums,
        )
        outgoing_there = swap_core(outgoing)
        early_there = swap_core(early)

        contract_bits = list(range(1, stages)) + [0, -1]
        contract_keep, contract_give = both_halves(
            digit_of(contract_bits[0]), dp_count, after(hidden2, outgoing), (arrived, 3),
            hidden0, (pair_there, 1), (send, 0), (arrived, 0),
        )
        contract_came = exchange(contract_give, contract_bits[0])
        expand_two = pair_grad(
            dp_count, (after(pair, contract_give), 0), (pair_there, 0), unit_grad2, (arrived, 2)
        )
        expand_across = swap_y(expand_two)
        expand_own = pair_grad(
            dp_count, (after(pair, expand_two), 0), (pair_there, 0), unit_grad0, (arrived, 1)
        )

        def backward(saved, weight, mixing_here, attended, ready, before=()):
            return attend_back(
                limits, mixing_here, after(outgoing, ready), outgoing_there, *saved, bucket_row,
                key_code, seg_row, tokens, x_other, weight, *attended, early, early_there, *before,
                pieces=dp_count, last=bool(before),
            )

        pieces_b, inputs_own, inputs_other, tail_b = backward(
            saved_b, weight_y, mixing_y, (own_b, other_b), expand_own
        )
        pieces_y = swap_y(pieces_b)
        contract_came, expand_across = after((contract_came, expand_across), pieces_b)
        contract_keep, contract_give = split(digit_of(contract_bits[1]), contract_keep, contract_came)
        contract_came = exchange(contract_give, contract_bits[1])
        expand_keep, expand_give = split(digit_of(0), expand_own, expand_across)
        expand_came = swap_dp(expand_give, 1)
        pieces_a, inputs_own, inputs_other, tail_a = backward(
            saved_a, weight_own, mixing_weight, (own_a, other_a),
            (pieces_b, contract_give, expand_give), (inputs_own, inputs_other),
        )
        pieces_y = after(pieces_y, pieces_a)
        expand_came = after(expand_came, pieces_a)
        contract_came = after(contract_came, pieces_a)

        def projection_steps():
            keep, give = split(digit_of(0), pieces_a, pieces_y)
            came = yield give, 0
            splits = (3 * width // dp_count, width // dp_count)
            return (yield from sum_over_dp(keep, came, range(1, stages), splits))

        def small_steps():
            value = tail_a + (yield tail_b, -1)
            for bit in list(range(1, stages)) + [0]:
                value = value + (yield value, bit)
            return value

        def input_steps():
            there = yield inputs_other, -2
            return total_of(digit_of(0), inputs_own, there, f32, grad_one)

        results = interleave(
            "tpecsepctcepecpcpssescps",
            {
                "t": input_steps(),
                "p": projection_steps(),
                "c": sum_over_dp(contract_keep, contract_came, contract_bits[2:]),
                "e": sum_over_dp(expand_keep, expand_came, range(1, stages)),
                "s": small_steps(),
            },
        )
        (contract_total,), (expand_total,) = results["c"], results["e"]
        projection_total, mixing_total = results["p"]
        sums = results["s"]
        tokens_grad = results["t"]

        return (
            layer_out,
            tokens_grad,
            projection_total.reshape(3, width, model_width).transpose(2, 0, 1),
            sums[NH : NH + 2, :width],
            sums[:NH, :bucket_count].T,
            mixing_total,
            sums[5:7],
            sums[7:9],
            sums[9:11],
            expand_total,
            sums[11],
            contract_total,
        )

    return body


def solution(mesh):
    return jax.shard_map(
        make_body(mesh.shape["dp"]),
        mesh=mesh,
        in_specs=(
            P(("dp", "tensor"), None),
            P("dp", None),
            P("dp", None),
            P(),
            P(None, None, "tensor"),
            P(None, "tensor"),
            P(None, "tensor"),
            P("tensor", None),
            P(),
            P(),
            P(),
            P(None, "tensor"),
            P("tensor"),
            P("tensor", None),
            P(("dp", "tensor"), None),
        ),
        out_specs=(
            P(("dp", "tensor"), None),
            P(("dp", "tensor"), None),
            P(None, None, "tensor"),
            P(None, "tensor"),
            P(None, "tensor"),
            P("tensor", None),
            P(),
            P(),
            P(),
            P(None, "tensor"),
            P("tensor"),
            P("tensor", None),
        ),
        check_vma=False,
    )
```

```python
import functools
import jax
import jax.numpy as jnp
from jax import lax
from jax.experimental import pallas as pl
from jax.experimental.pallas import tpu as pltpu
from jax.sharding import PartitionSpec as P

big_negative = -1e30
KB = 128
QT = 256
HALF = 512
SEQ = 1024
HW = 64
NH = 3
TILES = 11
SPAN = 1536
f32 = jnp.float32
bf16 = jnp.bfloat16
dot32 = functools.partial(lax.dot_general, preferred_element_type=f32)
NN = (((1,), (0,)), ((), ()))
NT = (((1,), (1,)), ((), ()))


def took(micros):
    return pl.CostEstimate(flops=int(micros * 8e5), transcendentals=0, bytes_accessed=int(micros * 3e3))


def in_hbm(value):
    return pltpu.with_memory_space_constraint(value, pltpu.HBM)


def three_parts(value):
    high = value.astype(bf16)
    rest = value - high.astype(f32)
    middle = rest.astype(bf16)
    low = (rest - middle.astype(f32)).astype(bf16)
    return high, middle, low


def bucket_grid(bucket_ref, count):
    rows = lax.broadcasted_iota(jnp.int32, (count, SPAN), 0)
    return (rows == bucket_ref[...]).astype(bf16)


def tile_mask(key_code, seg_row, difference, shift):
    codes = jnp.concatenate([key_code, key_code], axis=1)
    return (codes == seg_row) | (difference == shift)


def prepare_kernel(place, seg_scalar, segments, padding, table, pair_bias, unit_bias,
                   limits, key_code, seg_row, small):
    flip = place[0]
    chip = place[1]
    segs = segments[pl.ds(chip, 1), :]
    code = jnp.where(padding[pl.ds(chip, 1), :] == 1, segs, -1).astype(f32)
    wide = segs.astype(f32)
    for b in range(SEQ // QT):
        seg_row[b] = wide[:, b * QT : (b + 1) * QT]
        first = seg_scalar[chip, b * QT]
        last = seg_scalar[chip, b * QT + QT - 1]
        limits[b] = jnp.sum((segs < first).astype(f32)).astype(jnp.int32) // KB
        limits[4 + b] = (jnp.sum((segs <= last).astype(f32)).astype(jnp.int32) + KB - 1) // KB
    limits[8] = flip
    for b in range(SEQ // KB):
        key_code[b] = jnp.broadcast_to(code[:, b * KB : (b + 1) * KB], (KB, KB)).T
    small[...] = jnp.zeros(small.shape, f32)
    small[0:NH, : table.shape[1]] = table[...]
    small[NH : NH + 2, : pair_bias.shape[1]] = pair_bias[...]
    small[NH + 2 : NH + 3, : unit_bias.shape[1]] = unit_bias[...]


def prepare(place, segment_ids, pad_mask, table, pair_bias, unit_bias):
    vm = pl.BlockSpec(memory_space=pltpu.VMEM)
    sm = pl.BlockSpec(memory_space=pltpu.SMEM)
    return pl.pallas_call(
        prepare_kernel,
        out_shape=(
            jax.ShapeDtypeStruct((9,), jnp.int32),
            jax.ShapeDtypeStruct((SEQ // KB, KB, KB), f32),
            jax.ShapeDtypeStruct((SEQ // QT, 1, QT), f32),
            jax.ShapeDtypeStruct((8, unit_bias.shape[1]), f32),
        ),
        in_specs=[sm, sm, vm, vm, vm, vm, vm],
        out_specs=(sm, vm, vm, vm),
        cost_estimate=took(2),
        name="prepare",
    )(place, segment_ids, segment_ids, pad_mask, table, pair_bias, unit_bias)


def forward_kernel(limits, x_own, x_other, weight, small, buckets, key_code, seg_row,
                   own_out, other_out, full_far, totals_far, heads_far, turned_far, tiles_far,
                   out_full, totals, heads_out, turned_out, tiles, best, total, gathered, done):
    flip = limits[8]

    def send(count, *pairs):
        copies = [
            pltpu.make_async_copy(near, far, done.at[count + i]) for i, (near, far) in enumerate(pairs)
        ]
        for copy in copies:
            copy.start()
        return copies

    width = NH * HW
    columns = small[:, :256].T
    for half, x_ref in enumerate((x_own, x_other)):
        plain = dot32(x_ref[...], weight[...], NT)
        across = dot32(weight[...], x_ref[...], NT)
        rows = pl.ds(half * HALF, HALF)
        for c in range(3):
            part, turned = plain[:, c * width : (c + 1) * width], across[c * width : (c + 1) * width]
            if c != 1:
                r = NH + c // 2
                part = part + small[r : r + 1, :width]
                turned = turned + columns[:width, r : r + 1]
            part, turned = part.astype(bf16), turned.astype(bf16)
            if c == 0:
                part, turned = part * 0.125, turned * 0.125
            for h in range(NH):
                heads_out[c * NH + h, rows, :] = part[:, h * HW : (h + 1) * HW]
            for k in range(HALF // KB):
                turned_out[half * (HALF // KB) + k, c * width : (c + 1) * width, :] = turned[
                    :, k * KB : (k + 1) * KB
                ]
    hot = bucket_grid(buckets, 256)
    line = sum(dot32(part, hot, NN) for part in three_parts(small[:, :256]))
    for h in range(NH):
        for u in range(TILES):
            start = 640 - 128 * (u - 5)
            spread = jnp.broadcast_to(line[h : h + 1, start : start + 256], (KB, 256))
            tiles[h, u] = pltpu.roll(spread, 129, 1, stride=1, stride_axis=0)[:, :KB]
    copies = send(0, (heads_out, heads_far), (turned_out, turned_far), (tiles, tiles_far))
    difference = lax.broadcasted_iota(jnp.int32, (KB, QT), 1) - lax.broadcasted_iota(
        jnp.int32, (KB, QT), 0
    )

    def query_step(block, carry):
        place = block ^ (flip * 2)
        best[...] = jnp.full(best.shape, big_negative, f32)
        total[...] = jnp.zeros(total.shape, f32)
        gathered[...] = jnp.zeros(gathered.shape, f32)
        segs = seg_row[place]

        def key_step(key_place, carry):
            key_block = key_place ^ (flip * 4)
            gap = key_place - 2 * place
            allowed = tile_mask(key_code[key_place], segs, difference, gap * KB)
            queries = [
                jnp.concatenate([turned_out[2 * block + i, h * HW : (h + 1) * HW, :] for i in range(2)], axis=1)
                for h in range(NH)
            ]
            k_rows = pl.ds(key_block * KB, KB)
            scores = [dot32(heads_out[NH + h, k_rows, :], queries[h], NN) for h in range(NH)]
            lows, shrinks = [], []
            for h in range(NH):
                bias = jnp.concatenate([tiles[h, gap + 5], tiles[h, gap + 4]], axis=1)
                value = jnp.where(allowed, scores[h] + bias, big_negative)
                old = best[h]
                new = jnp.maximum(old, jnp.max(value, axis=0, keepdims=True))
                value = jnp.exp(value - new)
                shrink = jnp.exp(old - new)
                best[h] = new
                total[h] = shrink * total[h] + jnp.sum(value, axis=0, keepdims=True)
                lows.append(value.astype(bf16))
                shrinks.append(shrink)
            for h in range(NH):
                turned_v = turned_out[key_block, (2 * NH + h) * HW : (2 * NH + h + 1) * HW, :]
                gathered[h] = gathered[h] * shrinks[h] + dot32(turned_v, lows[h], NN)
            return carry

        lax.fori_loop(limits[place], limits[4 + place], key_step, 0)
        for h in range(NH):
            result = gathered[h] / total[h]
            out_full[block, h * HW : (h + 1) * HW, :] = result
            totals[block, h : h + 1, :] = best[h] + jnp.log(total[h])
        return carry

    lax.fori_loop(0, SEQ // QT, query_step, 0)
    copies = copies + send(3, (out_full, full_far), (totals, totals_far))
    for c in range(2):
        own_out[:, c * QT : (c + 1) * QT] = out_full[c].astype(bf16)
        other_out[:, c * QT : (c + 1) * QT] = out_full[2 + c].astype(bf16)
    for copy in copies:
        copy.wait()


def saved_shapes():
    return (
        ((SEQ // QT, NH * HW, QT), f32),
        ((SEQ // QT, 8, QT), f32),
        ((3 * NH, SEQ, HW), bf16),
        ((SEQ // KB, 3 * NH * HW, KB), bf16),
        ((NH, TILES, KB, KB), f32),
    )


def attend(limits, x_own, x_other, weight, small, buckets, key_code, seg_row):
    vm = pl.BlockSpec(memory_space=pltpu.VMEM)
    return pl.pallas_call(
        forward_kernel,
        out_shape=(
            jax.ShapeDtypeStruct((NH * HW, HALF), bf16),
            jax.ShapeDtypeStruct((NH * HW, HALF), bf16),
        )
        + tuple(pltpu.HBM(shape, kind) for shape, kind in saved_shapes()),
        in_specs=[pl.BlockSpec(memory_space=pltpu.SMEM)] + [vm] * 7,
        out_specs=(vm, vm) + (pl.BlockSpec(memory_space=pltpu.HBM),) * 5,
        scratch_shapes=[pltpu.VMEM(shape, kind) for shape, kind in saved_shapes()]
        + [
            pltpu.VMEM((NH, 1, QT), f32),
            pltpu.VMEM((NH, 1, QT), f32),
            pltpu.VMEM((NH, HW, QT), f32),
            pltpu.SemaphoreType.DMA((5,)),
        ],
        compiler_params=pltpu.CompilerParams(vmem_limit_bytes=20 << 20),
        cost_estimate=took(20),
        name="attend",
    )(limits, x_own, x_other, weight, small, buckets, key_code, seg_row)


def backward_kernel(limits, mixing, outgoing_own, outgoing_other, full_far, totals_far, heads_far,
                    turned_far, tiles_far, buckets, key_code, seg_row, x_own_far, x_other_far, weight_far, attended_own,
                    attended_other, early, early_there, *rest, last):
    if last:
        before_own_far, before_other_far, *rest = rest
    (pieces_out, own_out, other_out, tail_out,
     out_full, totals, heads, turned, tiles,
     turned_grad, plain_grad, row_dots, query_acc, query_all, key_acc, value_acc, tile_acc,
     grads, done, *rest) = rest
    flip = limits[8]
    fetched = [
        pltpu.make_async_copy(far, near, done.at[i])
        for i, (far, near) in enumerate(
            ((full_far, out_full), (totals_far, totals), (heads_far, heads), (turned_far, turned),
             (tiles_far, tiles))
        )
    ]
    x_own, x_other, weight, *rest = rest
    pairs = [(x_own_far, x_own), (x_other_far, x_other), (weight_far, weight)]
    if last:
        before_own, before_other = rest
        pairs += [(before_own_far, before_own), (before_other_far, before_other)]
    late = [pltpu.make_async_copy(far, near, done.at[5 + i]) for i, (far, near) in enumerate(pairs)]
    for copy in fetched:
        copy.start()
    key_acc[...] = jnp.zeros(key_acc.shape, f32)
    value_acc[...] = jnp.zeros(value_acc.shape, f32)
    tile_acc[...] = jnp.zeros(tile_acc.shape, f32)
    fetched[0].wait()
    for half, ref in enumerate((outgoing_own, outgoing_other)):
        across = dot32(mixing[...], ref[...], NT).astype(bf16)
        for c in range(2):
            block = 2 * half + c
            piece = across[:, c * QT : (c + 1) * QT]
            turned_grad[block] = piece
            wide = piece.astype(f32)
            product = wide * out_full[block]
            for h in range(NH):
                rows = slice(h * HW, (h + 1) * HW)
                row_dots[block, h : h + 1, :] = jnp.sum(product[rows], axis=0, keepdims=True)
                plain_grad[h, block * QT : (block + 1) * QT, :] = wide[rows].T.astype(bf16)
    for copy in fetched[1:]:
        copy.wait()
    for copy in late:
        copy.start()
    difference = lax.broadcasted_iota(jnp.int32, (KB, QT), 1) - lax.broadcasted_iota(
        jnp.int32, (KB, QT), 0
    )

    def query_step(block, carry):
        place = block ^ (flip * 2)
        query_acc[...] = jnp.zeros(query_acc.shape, f32)
        segs = seg_row[place]
        q_rows = pl.ds(block * QT, QT)

        def key_step(key_place, carry):
            key_block = key_place ^ (flip * 4)
            gap = key_place - 2 * place
            k_rows = pl.ds(key_block * KB, KB)
            allowed = tile_mask(key_code[key_place], segs, difference, gap * KB)
            queries = [
                jnp.concatenate([turned[2 * block + i, h * HW : (h + 1) * HW, :] for i in range(2)], axis=1)
                for h in range(NH)
            ]
            scores = [dot32(heads[NH + h, k_rows, :], queries[h], NN) for h in range(NH)]
            chance_grads = [
                dot32(heads[2 * NH + h, k_rows, :], turned_grad[block, h * HW : (h + 1) * HW, :], NN)
                for h in range(NH)
            ]
            chances, score_lows = [], []
            for h in range(NH):
                bias = jnp.concatenate([tiles[h, gap + 5], tiles[h, gap + 4]], axis=1)
                value = jnp.where(allowed, scores[h] + bias, big_negative)
                chance = jnp.exp(value - totals[block, h : h + 1, :])
                score_grad = chance * (chance_grads[h] - row_dots[block, h : h + 1, :])
                tile_acc[h, gap + 5] += score_grad[:, :KB]
                tile_acc[h, gap + 4] += score_grad[:, KB:]
                chances.append(chance.astype(bf16))
                score_lows.append(score_grad.astype(bf16))
            for h in range(NH):
                value_acc[h, k_rows, :] += dot32(chances[h], plain_grad[h, q_rows, :], NN)
            for h in range(NH):
                key_acc[h, k_rows, :] += dot32(score_lows[h], heads[h, q_rows, :], NN)
            for h in range(NH):
                turned_k = turned[key_block, (NH + h) * HW : (NH + h + 1) * HW, :]
                query_acc[h] += dot32(turned_k, score_lows[h], NN)
            return carry

        lax.fori_loop(limits[place], limits[4 + place], key_step, 0)
        for h in range(NH):
            query_all[h, q_rows, :] = (query_acc[h] * 0.125).T
        return carry

    lax.fori_loop(0, SEQ // QT, query_step, 0)
    width = NH * HW
    for g, acc in ((0, query_all), (1, key_acc), (2, value_acc)):
        for h in range(NH):
            at = (g * NH + h) * HW
            grads[:, at : at + HW] = acc[h].astype(bf16)
    tail_out[...] = jnp.zeros(tail_out.shape, f32)
    tail_out[5:11, :] = early[5:11, :] + early_there[5:11, :]
    r = 11 if last else 12
    tail_out[11:12, :] = early[r : r + 1, :] + early_there[r + 2 : r + 3, :]
    for r in range(2):
        sums = jnp.sum(grads[:, 2 * r * width : (2 * r + 1) * width].astype(f32), axis=0, keepdims=True)
        tail_out[NH + r : NH + r + 1, :width] = sums
    for copy in late:
        copy.wait()
    total = dot32(grads[:HALF, :], x_own[...], TN) + dot32(grads[HALF:, :], x_other[...], TN)
    mixed = dot32(attended_own[...], outgoing_own[...], NN) + dot32(
        attended_other[...], outgoing_other[...], NN
    )
    pieces = pieces_out.shape[0]
    first, second = total.shape[0] // pieces, mixed.shape[0] // pieces
    for p in range(pieces):
        pieces_out[p, :first] = total[p * first : (p + 1) * first].astype(bf16)
        pieces_out[p, first:] = mixed[p * second : (p + 1) * second].astype(bf16)
    own = dot32(grads[:HALF, :], weight[...], NN)
    other = dot32(grads[HALF:, :], weight[...], NN)
    if last:
        own = own + before_own[...]
        other = other + before_other[...]
    own_out[...] = own
    other_out[...] = other.astype(other_out.dtype)
    hot = bucket_grid(buckets, 256)
    lines = []
    for h in range(NH):
        spans = [jnp.zeros((1, KB), f32) for _ in range(SPAN // KB)]
        for u in range(TILES):
            wide = jnp.concatenate([tile_acc[h, u], jnp.zeros((KB, KB), f32)], axis=1)
            count = KB // 2
            while count:
                wide = wide[count:] + pltpu.roll(wide[:count], count, 1)
                count //= 2
            at = (640 - 128 * (u - 5)) // KB
            spans[at] = spans[at] + wide[:, :KB]
            spans[at + 1] = spans[at + 1] + wide[:, KB:]
        lines.append(jnp.concatenate(spans, axis=1))
    lines.append(jnp.zeros((8 - NH, SPAN), f32))
    line = jnp.concatenate(lines, axis=0)
    tail_out[:NH, :256] = sum(dot32(part, hot, NT) for part in three_parts(line))[:NH]


def attend_back(limits, *args, pieces, last):
    vm = pl.BlockSpec(memory_space=pltpu.VMEM)
    wide, model = args[13].shape
    rows = args[1].shape[0]
    piece = (wide + wide // 3) // pieces
    return pl.pallas_call(
        functools.partial(backward_kernel, last=last),
        out_shape=(
            jax.ShapeDtypeStruct((pieces, piece, model), bf16),
            (jax.ShapeDtypeStruct if last else pltpu.HBM)((rows, model), f32),
            (jax.ShapeDtypeStruct if last else pltpu.HBM)((rows, model), bf16 if last else f32),
            jax.ShapeDtypeStruct((16, model), f32),
        ),
        in_specs=[pl.BlockSpec(memory_space=pltpu.SMEM)] + [vm] * 3
        + [pl.BlockSpec(memory_space=pltpu.HBM)] * 5 + [vm] * 3
        + [pl.BlockSpec(memory_space=pltpu.HBM)] * 3 + [vm] * 4
        + [pl.BlockSpec(memory_space=pltpu.HBM)] * (2 if last else 0),
        out_specs=tuple([vm] * 4),
        scratch_shapes=[pltpu.VMEM(shape, kind) for shape, kind in saved_shapes()]
        + [
            pltpu.VMEM((SEQ // QT, NH * HW, QT), bf16),
            pltpu.VMEM((NH, SEQ, HW), bf16),
            pltpu.VMEM((SEQ // QT, 8, QT), f32),
            pltpu.VMEM((NH, HW, QT), f32),
            pltpu.VMEM((NH, SEQ, HW), f32),
            pltpu.VMEM((NH, SEQ, HW), f32),
            pltpu.VMEM((NH, SEQ, HW), f32),
            pltpu.VMEM((NH, TILES, KB, KB), f32),
            pltpu.VMEM((SEQ, 3 * NH * HW), bf16),
            pltpu.SemaphoreType.DMA((10,)),
            pltpu.VMEM((rows, model), bf16),
            pltpu.VMEM((rows, model), bf16),
            pltpu.VMEM((wide, model), bf16),
        ]
        + [pltpu.VMEM((rows, model), f32)] * (2 if last else 0),
        compiler_params=pltpu.CompilerParams(vmem_limit_bytes=36 << 20),
        cost_estimate=took(25),
        name="attend_back",
    )(limits, *args[:3], *[in_hbm(arg) for arg in args[3:8]], *args[8:11],
      *[in_hbm(arg) for arg in args[11:14]], *args[14:18], *[in_hbm(arg) for arg in args[18:]])


ROWS = 128
TN = (((0,), (0,)), ((), ()))
norm_eps = 1e-05


def whole(count):
    return [pl.BlockSpec(memory_space=pltpu.VMEM)] * count


def normalise(value):
    centered = value - jnp.mean(value, axis=-1, keepdims=True)
    inverse = lax.rsqrt(jnp.mean(centered * centered, axis=-1, keepdims=True) + norm_eps)
    return centered * inverse, inverse


def normalise_back(scaled, normed, inverse):
    first_mean = jnp.mean(scaled, axis=-1, keepdims=True)
    second_mean = jnp.mean(scaled * normed, axis=-1, keepdims=True)
    return inverse * (scaled - first_mean - normed * second_mean)


def gelu_parts(value):
    cumulative = 0.5 * (1.0 + lax.erf(value * 0.7071067811865476))
    density = jnp.exp(-0.5 * value * value) * 0.3989422804014327
    return (value * cumulative).astype(bf16), cumulative + value * density


def add_column(ref, at, value):
    ref[at] += jnp.sum(value.reshape(-1, 8, value.shape[1]), axis=0)


def first_half_kernel(tokens, own_a, recv_a, own_b, recv_b, mix0, mix1, mix2, mix3, biases, gains,
                      shifts, expand0, contract0, expand1, contract1, small0, small1,
                      normed_out, inverse_out, pair_out, hidden0_out, slope0_out, slope1_out, partial_out):
    def step(r, carry):
        at = pl.multiple_of(r * ROWS, ROWS)
        rows = pl.ds(at, ROWS)
        branch = tokens[rows, :].astype(f32) + biases[0:1, :]
        for attended, mixing in ((own_a, mix0), (recv_a, mix1), (own_b, mix2), (recv_b, mix3)):
            branch = branch + dot32(attended[:, rows], mixing[...], TN)
        normed, inverse = normalise(branch)
        normed_out[rows, :] = normed
        inverse_out[rows, :] = inverse
        low = (normed * gains[0:1, :] + shifts[0:1, :]).astype(bf16)
        pair_out[0, rows, :] = low
        partial = biases[1:2, :]
        for s, expand, contract, small in ((0, expand0, contract0, small0), (1, expand1, contract1, small1)):
            hidden, slope = gelu_parts(dot32(low, expand[...], NN) + small[5:6, :])
            if s == 0:
                hidden0_out[rows, :] = hidden
                slope0_out[rows, :] = slope
            else:
                pair_out[1, rows, :] = hidden
                slope1_out[rows, :] = slope
            partial = partial + dot32(hidden, contract[...], NN)
        partial_out[rows, :] = partial
        return carry

    lax.fori_loop(0, tokens.shape[0] // ROWS, step, 0)


def first_half(*args):
    rows, cols = args[0].shape
    wide = jax.ShapeDtypeStruct((rows, cols), f32)
    return pl.pallas_call(
        first_half_kernel,
        out_shape=(wide, jax.ShapeDtypeStruct((rows, 1), f32),
                   jax.ShapeDtypeStruct((2, rows, cols), bf16),
                   jax.ShapeDtypeStruct((rows, cols), bf16), wide, wide, wide),
        in_specs=whole(len(args)),
        out_specs=tuple(whole(7)),
        compiler_params=pltpu.CompilerParams(vmem_limit_bytes=16 << 20),
        cost_estimate=took(12),
        name="first_half",
    )(*args)


def third_slot_kernel(pair, expand, contract, small, partial_in, hidden_out, slope_out, partial_out):
    def step(r, carry):
        rows = pl.ds(pl.multiple_of(r * ROWS, ROWS), ROWS)
        hidden, slope = gelu_parts(dot32(pair[0, rows, :], expand[...], NN) + small[5:6, :])
        hidden_out[rows, :] = hidden
        slope_out[rows, :] = slope
        partial_out[rows, :] = partial_in[rows, :] + dot32(hidden, contract[...], NN)
        return carry

    lax.fori_loop(0, partial_in.shape[0] // ROWS, step, 0)


def third_slot(*args):
    rows, cols = args[4].shape
    wide = jax.ShapeDtypeStruct((rows, cols), f32)
    return pl.pallas_call(
        third_slot_kernel,
        out_shape=(jax.ShapeDtypeStruct((rows, cols), bf16), wide, wide),
        in_specs=whole(5),
        out_specs=tuple(whole(3)),
        compiler_params=pltpu.CompilerParams(vmem_limit_bytes=16 << 20),
        cost_estimate=took(5),
        name="third_slot",
    )(*args)


def second_half_kernel(normed_in, pair, partial_in, gains, shifts, expand3, contract3, contract1,
                       small, slope1, cotangent,
                       layer_out, grad_two_out, send_out, sums_out):
    sums_out[...] = jnp.zeros(sums_out.shape, f32)

    def step(r, carry):
        rows = pl.ds(pl.multiple_of(r * ROWS, ROWS), ROWS)
        low = pair[0, rows, :]
        total = normed_in[rows, :] * gains[0:1, :] + shifts[0:1, :] + partial_in[rows, :]
        hidden3, slope3 = gelu_parts(dot32(low, expand3[...], NN) + small[5:6, :])
        send_out[3, rows, :] = hidden3
        total = total + dot32(hidden3, contract3[...], NN)
        normed, inverse = normalise(total)
        layer_out[rows, :] = (normed * gains[1:2, :] + shifts[1:2, :]).astype(bf16)
        outer = cotangent[rows, :].astype(f32)
        grad_two = normalise_back(outer * gains[1:2, :], normed, inverse)
        grad_two_out[rows, :] = grad_two
        upstream = grad_two.astype(bf16)
        send_out[0, rows, :] = upstream
        add_column(sums_out, 0, grad_two)
        add_column(sums_out, 1, outer * normed)
        add_column(sums_out, 2, outer)
        for at, contract, slope in ((1, contract1, slope1[rows, :]), (2, contract3, slope3)):
            unit_grad = (dot32(upstream, contract[...], NT) * slope).astype(bf16)
            send_out[at, rows, :] = unit_grad
            add_column(sums_out, 2 + at, unit_grad.astype(f32))
        return carry

    lax.fori_loop(0, normed_in.shape[0] // ROWS, step, 0)


def second_half(*args):
    rows, cols = args[0].shape
    wide = jax.ShapeDtypeStruct((rows, cols), f32)
    low = jax.ShapeDtypeStruct((rows, cols), bf16)
    return pl.pallas_call(
        second_half_kernel,
        out_shape=(low, wide, jax.ShapeDtypeStruct((4, rows, cols), bf16),
                   jax.ShapeDtypeStruct((5, 8, cols), f32)),
        in_specs=whole(len(args)),
        out_specs=tuple(whole(4)),
        compiler_params=pltpu.CompilerParams(vmem_limit_bytes=16 << 20),
        cost_estimate=took(15),
        name="second_half",
    )(*args)


def unit_back_kernel(send, contract0, contract2, slope0, slope2, expand0, expand1, expand2, expand3,
                     grad_two, normed_in, inverse_in, gains, later,
                     grad0_out, grad2_out, grad_one_out, outgoing_out, rows_out, sums_out):
    sums_out[...] = jnp.zeros(sums_out.shape, f32)

    def step(r, carry):
        rows = pl.ds(pl.multiple_of(r * ROWS, ROWS), ROWS)
        upstream = send[0, rows, :]
        total = grad_two[rows, :]
        total = total + dot32(send[1, rows, :], expand1[...], NT)
        total = total + dot32(send[2, rows, :], expand3[...], NT)
        for at, contract, slope, expand, out in ((3, contract0, slope0, expand0, grad0_out),
                                                 (4, contract2, slope2, expand2, grad2_out)):
            unit_grad = (dot32(upstream, contract[...], NT) * slope[rows, :]).astype(bf16)
            out[rows, :] = unit_grad
            add_column(sums_out, at, unit_grad.astype(f32))
            total = total + dot32(unit_grad, expand[...], NT)
        normed = normed_in[rows, :]
        grad_one = normalise_back(total * gains[0:1, :], normed, inverse_in[rows, :])
        grad_one_out[rows, :] = grad_one
        outgoing_out[rows, :] = grad_one.astype(bf16)
        add_column(sums_out, 0, grad_one)
        add_column(sums_out, 1, total * normed)
        add_column(sums_out, 2, total)
        return carry

    lax.fori_loop(0, grad_two.shape[0] // ROWS, step, 0)
    rows_out[...] = jnp.zeros(rows_out.shape, f32)
    order = (sums_out[0], later[0], sums_out[1], later[1], sums_out[2], later[2],
             sums_out[3], sums_out[4], later[3], later[4])
    for r, value in enumerate(order):
        rows_out[5 + r : 6 + r, :] = jnp.sum(value, axis=0, keepdims=True)


def unit_back(*args):
    rows, cols = args[9].shape
    low = jax.ShapeDtypeStruct((rows, cols), bf16)
    return pl.pallas_call(
        unit_back_kernel,
        out_shape=(low, low, jax.ShapeDtypeStruct((rows, cols), f32), low,
                   jax.ShapeDtypeStruct((16, cols), f32)),
        in_specs=whole(len(args)),
        out_specs=tuple(whole(5)),
        scratch_shapes=[pltpu.VMEM((5, 8, cols), f32)],
        compiler_params=pltpu.CompilerParams(vmem_limit_bytes=16 << 20),
        cost_estimate=took(17),
        name="unit_back",
    )(*args)


def pair_grad_kernel(left, left_there, right, right_there, out):
    total = dot32(left[...], right[...], TN) + dot32(left_there[...], right_there[...], TN)
    rows = out.shape[1]
    for p in range(out.shape[0]):
        out[p] = total[p * rows : (p + 1) * rows].astype(bf16)


def both_halves_kernel(digit, two, two_there, own, own_there, right, right_there, keep_out, give_out):
    half, rows, _ = keep_out.shape
    half //= 2
    bits = half.bit_length()
    for slot, (left, left_there) in enumerate(((two, two_there), (own, own_there))):
        total = dot32(left[...], right[...], TN) + dot32(left_there[...], right_there[...], TN)
        for q in range(half):
            first = q if bits < 2 else (q >> bits - 2) | sum(
                (q >> i & 1) << i + 2 for i in range(bits - 2)
            )
            step = 1 if bits < 2 else 2
            low = total[first * rows : (first + 1) * rows]
            high = total[(first + step) * rows : (first + step + 1) * rows]
            keep_out[slot * half + q] = jnp.where(digit[0] == 0, low, high)
            give_out[slot * half + q] = jnp.where(digit[0] == 0, high, low).astype(bf16)


def indexed(operand):
    array, index = operand if isinstance(operand, tuple) else (operand[None], 0)
    return array, pl.BlockSpec((None,) + array.shape[1:], lambda i, index=index: (index, 0, 0))


def both_halves(digit, pieces, *operands):
    arrays, specs = zip(*[indexed(operand) for operand in operands])
    rows, cols = arrays[0].shape[2] // pieces, arrays[4].shape[2]
    return pl.pallas_call(
        both_halves_kernel,
        out_shape=tuple(jax.ShapeDtypeStruct((pieces, rows, cols), kind) for kind in (f32, bf16)),
        grid=(1,),
        in_specs=[pl.BlockSpec(memory_space=pltpu.SMEM)] + list(specs),
        out_specs=tuple(pl.BlockSpec((pieces, rows, cols), lambda i: (0, 0, 0)) for _ in range(2)),
        compiler_params=pltpu.CompilerParams(vmem_limit_bytes=14 << 20),
        cost_estimate=took(4),
        name="both_halves",
    )(digit, *arrays)


def pair_grad(pieces, *operands):
    arrays, specs = zip(*[indexed(operand) for operand in operands])
    rows, cols = arrays[0].shape[2] // pieces, arrays[2].shape[2]
    return pl.pallas_call(
        pair_grad_kernel,
        out_shape=jax.ShapeDtypeStruct((pieces, rows, cols), bf16),
        grid=(1,),
        in_specs=list(specs),
        out_specs=pl.BlockSpec((pieces, rows, cols), lambda i: (0, 0, 0)),
        compiler_params=pltpu.CompilerParams(vmem_limit_bytes=16 << 20),
        cost_estimate=took(4),
        name="pair_grad",
    )(*arrays)


def assemble_kernel(place, mine, theirs, *outs):
    low = place[0] & 1
    high = place[0] >> 1
    for r in range(mine.shape[0]):
        at = (r ^ high) * 2
        start = 0
        for out in outs:
            rows = out.shape[1]
            out[at + low] = mine[r, start : start + rows].astype(f32)
            out[at + 1 - low] = theirs[r, start : start + rows].astype(f32)
            start += rows


def assemble(place, mine, theirs, splits):
    half, rows, cols = mine.shape
    vm = pl.BlockSpec(memory_space=pltpu.VMEM)
    return pl.pallas_call(
        assemble_kernel,
        out_shape=tuple(jax.ShapeDtypeStruct((2 * half, part, cols), f32) for part in splits),
        in_specs=[pl.BlockSpec(memory_space=pltpu.SMEM), vm, vm],
        out_specs=tuple(vm for _ in splits),
        compiler_params=pltpu.CompilerParams(vmem_limit_bytes=32 << 20),
        cost_estimate=took(2),
        name="assemble",
    )(place, mine, theirs)


def small_call(kernel, name, outs, *args):
    vm = pl.BlockSpec(memory_space=pltpu.VMEM)
    return pl.pallas_call(
        kernel,
        out_shape=tuple(jax.ShapeDtypeStruct(shape, kind) for shape, kind in outs),
        in_specs=[pl.BlockSpec(memory_space=pltpu.SMEM)] + [vm] * (len(args) - 1),
        out_specs=tuple(vm for _ in outs),
        compiler_params=pltpu.CompilerParams(vmem_limit_bytes=16 << 20),
        cost_estimate=took(1),
        name=name,
    )(*args)


def split_kernel(digit, first, second, keep_out, give_out):
    for q in range(keep_out.shape[0]):
        keep, give = 2 * q + digit[0], 2 * q + 1 - digit[0]
        if len(second.shape) < 3:
            keep_out[q] = first[keep].astype(f32)
            give_out[q] = first[give]
        else:
            keep_out[q] = first[keep].astype(f32) + second[keep].astype(f32)
            give_out[q] = (first[give].astype(f32) + second[give].astype(f32)).astype(bf16)


def split(digit, first, second):
    shape = (first.shape[0] // 2,) + first.shape[1:]
    second = digit[None] if second is None else second
    return small_call(split_kernel, "split", ((shape, f32), (shape, bf16)), digit, first, second)


def total_kernel(digit, first, second, *rest):
    out = rest[-1]
    total = first[...].astype(f32) + second[...].astype(f32)
    if len(rest) > 1:
        total = total + rest[0][...]
    out[...] = total.astype(out.dtype)


def total_of(digit, first, second, kind, *third):
    return small_call(total_kernel, "total", ((first.shape, kind),), digit, first, second, *third)[0]


def arrange_kernel(digit, first, second, out):
    for q in range(out.shape[0]):
        at = q ^ digit[0]
        out[q] = (first[at].astype(f32) + second[at].astype(f32)).astype(out.dtype)


def arrange(digit, first, second):
    return small_call(arrange_kernel, "arrange", ((first.shape, first.dtype),), digit, first, second)[0]


def join_kernel(digit, first, second, out):
    for q in range(first.shape[0]):
        out[2 * q] = first[q]
        out[2 * q + 1] = second[q]


def join(digit, first, second):
    shape = (2 * first.shape[0],) + first.shape[1:]
    return small_call(join_kernel, "join", ((shape, first.dtype),), digit, first, second)[0]


def make_body(dp_count):
    stages = dp_count.bit_length() - 1

    def swap(value, axis, count, bits):
        return lax.ppermute(value, axis, [(i, i ^ bits) for i in range(count)])

    swap_core = lambda value: swap(value, "tensor", 4, 1)
    swap_y = lambda value: swap(value, "tensor", 4, 2)
    swap_dp = lambda value, bits: swap(value, "dp", dp_count, bits)

    def digit_of(bit):
        if bit == -1:
            return jnp.ones((1,), jnp.int32)
        return (lax.axis_index("dp").astype(jnp.int32) >> bit & 1)[None]

    def exchange(value, bit):
        if bit == -1:
            return swap_y(value)
        return swap_core(value) if bit == -2 else swap_dp(value, 1 << bit)

    def sum_over_dp(keep, came, bits, splits=None):
        bits = list(bits)
        top = stages - 1
        doubled = bits[-1:] == [top]
        for bit in bits[: len(bits) - doubled]:
            keep, give = split(digit_of(bit), keep, came)
            came = yield give, bit
        mine = total_of(digit_of(0), keep, came, bf16)
        if doubled:
            came = yield mine, top
            mine = arrange(digit_of(top), mine, came)
        for bit in range(top - doubled, 0, -1):
            came = yield mine, bit
            mine = join(digit_of(0), mine, came)
        theirs = yield mine, 0
        place = lax.axis_index("dp").astype(jnp.int32)[None]
        parts = assemble(place, mine, theirs, splits or (keep.shape[1],))
        return [part.reshape(-1, part.shape[2]) for part in parts]

    def interleave(order, steps):
        came = {name: None for name in steps}
        results = {}
        token = None
        names = list(order) + [name for name in steps for _ in range(4 * stages)]
        for name in names:
            if name in results:
                continue
            if token is not None and came[name] is not None:
                came[name] = lax.optimization_barrier((came[name], token))[0]
            try:
                value, bit = steps[name].send(came[name])
                if token is not None and came[name] is None:
                    value = lax.optimization_barrier((value, token))[0]
                token = value
                came[name] = exchange(value, bit)
            except StopIteration as stop:
                token = results[name] = stop.value
        return results

    def body(
        tokens,
        segment_ids,
        pad_mask,
        buckets,
        projections,
        projected_bias,
        relative_table,
        mixing_weight,
        residual_biases,
        norm_gains,
        norm_shifts,
        expand_weight,
        expand_bias,
        contract_weight,
        cotangent,
    ):
        rows_here, model_width = tokens.shape
        bucket_count = relative_table.shape[0]
        width = projections.shape[2]
        spot = lax.axis_index("tensor")
        flip = spot % 2

        def after(value, ready):
            return lax.optimization_barrier((value, ready))[0]

        dp_place = lax.axis_index("dp").astype(jnp.int32)
        odd = dp_place & 1
        weight_own = projections.transpose(1, 2, 0).reshape(3 * width, model_width)
        x_other = swap_core(tokens)
        weight_y = swap_y(weight_own)
        place = jnp.stack([flip, spot // 2]).astype(jnp.int32)
        limits, key_code, seg_row, small_own = prepare(
            place, segment_ids, pad_mask, relative_table.T, projected_bias, expand_bias[None]
        )
        mixing_late = after(mixing_weight, small_own)
        contract_late = after(contract_weight, x_other)
        mixing_y = swap_y(mixing_late)
        half_rows = contract_weight.shape[0] // 2
        half_y = swap_y(lax.dynamic_slice_in_dim(contract_late, odd * half_rows, half_rows, 0))
        small_y = swap_y(small_own)
        bucket_row = buckets[255:1791][::-1][None]

        def forward(weight, small, x_in):
            return attend(limits, x_in, x_other, weight, small, bucket_row, key_code, seg_row)

        own_a, other_a, *saved_a = forward(weight_own, small_own, tokens)
        expand_y = swap_y(after(expand_weight, own_a))
        recv_a = swap_core(other_a)
        own_b, other_b, *saved_b = forward(weight_y, small_y, after(tokens, (own_a, mixing_y)))
        half_x = swap_dp(after(half_y, own_b), 1)
        mixing_core, expand_core, contract_core, small_core = [
            swap_core(value)
            for value in after((mixing_weight, expand_weight, contract_weight, small_own), own_a)
        ]
        mixing_diag, small_diag = swap_core(after(mixing_y, own_a)), swap_core(after(small_y, own_b))
        recv_b = swap_core(other_b)
        contract_y = jnp.where(
            odd == 0, jnp.concatenate([half_y, half_x]), jnp.concatenate([half_x, half_y])
        )
        contract_diag = swap_core(contract_y)
        normed_one, inverse_one, pair, hidden0, slope0, slope1, partial = first_half(
            tokens, own_a, recv_a, own_b, recv_b, mixing_weight, mixing_core, mixing_y, mixing_diag,
            residual_biases, norm_gains, norm_shifts,
            expand_weight, contract_weight, expand_core, contract_core, small_own, small_core,
        )
        pair_there = swap_core(pair)
        expand_y = after(expand_y, partial)
        expand_diag = swap_core(expand_y)
        hidden2, slope2, partial = third_slot(pair, expand_y, contract_y, small_y, partial)
        layer_out, grad_two, send, later_sums = second_half(
            normed_one, pair, partial, norm_gains, norm_shifts,
            expand_diag, contract_diag, contract_core, small_diag, slope1, cotangent,
        )
        arrived = swap_core(send)
        unit_grad0, unit_grad2, grad_one, outgoing, early = unit_back(
            send, contract_weight, contract_y, slope0, slope2,
            expand_weight, expand_core, expand_y, expand_diag,
            grad_two, normed_one, inverse_one, norm_gains, later_sums,
        )
        outgoing_there = swap_core(outgoing)
        early_there = swap_core(early)

        contract_bits = list(range(1, stages)) + [0, -1]
        contract_keep, contract_give = both_halves(
            digit_of(contract_bits[0]), dp_count, after(hidden2, outgoing), (arrived, 3),
            hidden0, (pair_there, 1), (send, 0), (arrived, 0),
        )
        contract_came = exchange(contract_give, contract_bits[0])
        expand_two = pair_grad(
            dp_count, (after(pair, contract_give), 0), (pair_there, 0), unit_grad2, (arrived, 2)
        )
        expand_across = swap_y(expand_two)
        expand_own = pair_grad(
            dp_count, (after(pair, expand_two), 0), (pair_there, 0), unit_grad0, (arrived, 1)
        )

        def backward(saved, weight, mixing_here, attended, ready, before=()):
            return attend_back(
                limits, mixing_here, after(outgoing, ready), outgoing_there, *saved, bucket_row,
                key_code, seg_row, tokens, x_other, weight, *attended, early, early_there, *before,
                pieces=dp_count, last=bool(before),
            )

        pieces_b, inputs_own, inputs_other, tail_b = backward(
            saved_b, weight_y, mixing_y, (own_b, other_b), expand_own
        )
        pieces_y = swap_y(pieces_b)
        contract_came, expand_across = after((contract_came, expand_across), pieces_b)
        contract_keep, contract_give = split(digit_of(contract_bits[1]), contract_keep, contract_came)
        contract_came = exchange(contract_give, contract_bits[1])
        expand_keep, expand_give = split(digit_of(0), expand_own, expand_across)
        expand_came = swap_dp(expand_give, 1)
        pieces_a, inputs_own, inputs_other, tail_a = backward(
            saved_a, weight_own, mixing_weight, (own_a, other_a),
            (pieces_b, contract_give, expand_give), (inputs_own, inputs_other),
        )
        pieces_y = after(pieces_y, pieces_a)
        expand_came = after(expand_came, pieces_a)
        contract_came = after(contract_came, pieces_a)

        def projection_steps():
            keep, give = split(digit_of(0), pieces_a, pieces_y)
            came = yield give, 0
            splits = (3 * width // dp_count, width // dp_count)
            return (yield from sum_over_dp(keep, came, range(1, stages), splits))

        def small_steps():
            value = tail_a + (yield tail_b, -1)
            for bit in list(range(1, stages)) + [0]:
                value = value + (yield value, bit)
            return value

        def input_steps():
            there = yield inputs_other, -2
            return total_of(digit_of(0), inputs_own, there, f32, grad_one)

        results = interleave(
            "tpecsepctcecepcpepsscsps",
            {
                "t": input_steps(),
                "p": projection_steps(),
                "c": sum_over_dp(contract_keep, contract_came, contract_bits[2:]),
                "e": sum_over_dp(expand_keep, expand_came, range(1, stages)),
                "s": small_steps(),
            },
        )
        (contract_total,), (expand_total,) = results["c"], results["e"]
        projection_total, mixing_total = results["p"]
        sums = results["s"]
        tokens_grad = results["t"]

        return (
            layer_out,
            tokens_grad,
            projection_total.reshape(3, width, model_width).transpose(2, 0, 1),
            sums[NH : NH + 2, :width],
            sums[:NH, :bucket_count].T,
            mixing_total,
            sums[5:7],
            sums[7:9],
            sums[9:11],
            expand_total,
            sums[11],
            contract_total,
        )

    return body


def solution(mesh):
    return jax.shard_map(
        make_body(mesh.shape["dp"]),
        mesh=mesh,
        in_specs=(
            P(("dp", "tensor"), None),
            P("dp", None),
            P("dp", None),
            P(),
            P(None, None, "tensor"),
            P(None, "tensor"),
            P(None, "tensor"),
            P("tensor", None),
            P(),
            P(),
            P(),
            P(None, "tensor"),
            P("tensor"),
            P("tensor", None),
            P(("dp", "tensor"), None),
        ),
        out_specs=(
            P(("dp", "tensor"), None),
            P(("dp", "tensor"), None),
            P(None, None, "tensor"),
            P(None, "tensor"),
            P(None, "tensor"),
            P("tensor", None),
            P(),
            P(),
            P(),
            P(None, "tensor"),
            P("tensor"),
            P("tensor", None),
        ),
        check_vma=False,
    )
```
